32 devices in a mesh: prow: 4 (over y, core), pcol: 8 (over z, x).
Axes of the slice: x: 2, y: 2, z: 4, core: 2. Of those that a mesh axis runs over, the one named last changes fastest.
Arguments:
- matrix: bfloat16 [14336, 4096], P('prow', 'pcol'), may hold values from -6 to 6
- u_inverse: float32 [2, 512, 512], replicated, may hold values from -0.02 to 0.2, as said below
- l_inverse: float32 [2, 512, 512], replicated, may hold values from -0.02 to 0.2, as said below
Outputs:
- factored: bfloat16 [14336, 4096], P('prow', 'pcol')
The draws below stay inside these ranges and needn't reach their ends.
Inputs may be any that keep to these rules, and one draw needn't show every extreme that they name: u_inverse[p] is upper triangular with positive diagonal. l_inverse[p] is lower triangular with positive diagonal.
All inputs are finite; a program needn't handle non-finite values.
Results may differ from the reference program's by a relative error of at most 0.008.
Values may be sent and summed in bfloat16 or wider, within the bound.
A program may use at most 64 MiB of HBM per device.

```python
import jax
import jax.numpy as jnp
from jax import lax

NB = 512
PANELS = 2
RB = 7
ORDER = 14336
WCOLS = 4096
N_PROW = 4


def draw_u_inverse(key, part):
    first, second = jax.random.split(jax.random.fold_in(key, 11))
    diagonal = jax.random.uniform(first, (PANELS, NB), jnp.float32, 0.1, 0.2)
    spread = jax.random.uniform(second, (PANELS, NB, NB), jnp.float32, -0.02, 0.02)
    return jnp.triu(spread, 1) + diagonal[:, :, None] * jnp.eye(NB, dtype=jnp.float32)[None]


def draw_l_inverse(key, part):
    first, second = jax.random.split(jax.random.fold_in(key, 23))
    diagonal = jax.random.uniform(first, (PANELS, NB), jnp.float32, 0.1, 0.2)
    spread = jax.random.uniform(second, (PANELS, NB, NB), jnp.float32, -0.02, 0.02)
    return jnp.tril(spread, -1) + diagonal[:, :, None] * jnp.eye(NB, dtype=jnp.float32)[None]


def block_scale(rng, extent, cuts, smallest, largest):
    loudness = 1.0
    for dim, blocks in cuts:
        steps = jax.random.uniform(jax.random.fold_in(jax.random.fold_in(rng, 6), dim), (blocks,), jnp.float32, smallest / len(cuts), largest / len(cuts))
        loudness = loudness * jnp.repeat(jnp.exp(steps), extent[dim] // blocks).reshape((-1,) + (1,) * (len(extent) - 1 - dim))
    return loudness


def scatter_about(stream_key, shape, scale, most, cuts=(), held_as=jnp.bfloat16):
    loudness = block_scale(stream_key, shape, cuts, -0.22, 0.18) if cuts else 1.0
    values = jax.random.normal(stream_key, shape, jnp.float32) * scale * loudness
    return jnp.minimum(jnp.maximum(values, -most), most).astype(held_as)


def setup_inputs(seed: int = 0) -> dict:
    arg_keys = jax.random.split(jax.random.key(seed), 4)
    matrix = scatter_about(arg_keys[0], (ORDER, WCOLS), 1.0, 6.0, ((0, 4), (1, 8)))
    u_inverse = draw_u_inverse(jax.random.fold_in(arg_keys[3], 71), 0)
    l_inverse = draw_l_inverse(jax.random.fold_in(arg_keys[3], 71), 0)
    return dict(matrix=matrix, u_inverse=u_inverse, l_inverse=l_inverse)


def reference(matrix, u_inverse, l_inverse):
    stored = jnp.arange(ORDER) // NB
    row_ids = (stored % RB) * N_PROW + stored // RB
    col_ids = jnp.arange(WCOLS) // NB
    current = matrix
    for panel_id in range(PANELS):
        start = panel_id * NB
        head_start = panel_id * RB * NB
        panel = current[:, start:start + NB].astype(jnp.float32)
        lower = jnp.dot(panel, u_inverse[panel_id], precision=lax.Precision.HIGHEST).astype(jnp.bfloat16)
        lower = jnp.where(row_ids[:, None] > panel_id, lower, jnp.zeros_like(lower))
        head = current[head_start:head_start + NB].astype(jnp.float32)
        upper = jnp.dot(l_inverse[panel_id], head, precision=lax.Precision.HIGHEST).astype(jnp.bfloat16)
        upper = jnp.where(col_ids[None, :] > panel_id, upper, jnp.zeros_like(upper))

        def refresh(pair, upper=upper):
            block, left = pair
            product = jnp.dot(left, upper, preferred_element_type=jnp.float32)
            return (block.astype(jnp.float32) - product).astype(jnp.bfloat16)

        blocks = lax.map(refresh, (current.reshape(ORDER // NB, NB, WCOLS), lower.reshape(ORDER // NB, NB, NB)))
        current = blocks.reshape(ORDER, WCOLS)
        current = current.at[:, start:start + NB].set(
            jnp.where(row_ids[:, None] > panel_id, lower, current[:, start:start + NB]))
        current = current.at[head_start:head_start + NB].set(
            jnp.where(col_ids[None, :] > panel_id, upper, current[head_start:head_start + NB]))
    return current
```

```python
import functools

import jax
import jax.numpy as jnp
from jax import lax
from jax.experimental import pallas as pl
from jax.experimental.pallas import tpu as pltpu
from jax.sharding import PartitionSpec as P

MESH = pl.DeviceIdType.MESH
BF = jnp.bfloat16
F32 = jnp.float32
PIECES = 2
PER = 4


def sizes(rows, width, n_prow):
    tile = width // PER
    moved = 3 * PER // 2 if n_prow > 2 else 0
    return tile, tile // 2, tile // 4, rows // tile, moved


def dot(a, b):
    return jnp.dot(a, b, preferred_element_type=F32)


def times_upper(a, u_ref, panel):
    half = a.shape[1] // 2
    left = sum(dot(a[:, :half], u_ref[panel, i, :half, :half]) for i in reversed(range(PIECES)))
    right = sum(dot(a, u_ref[panel, i, :, half:]) for i in reversed(range(PIECES)))
    return jnp.concatenate([left, right], 1).astype(BF)


def kernel(
    n_prow, n_pcol, width, m_ref, u_hbm, l_hbm, out_ref,
    own, buf, head, uf, lf, us, ls, u0, u1,
    load_sem, recv, fwd, cross, ysem, hrecv, hsend, out_sem,
):
    rows = own.shape[0]
    tile, unit, pkt, tiles, moved = sizes(rows, width, n_prow)
    n_pkt = rows // pkt
    half = width // 2
    prow, pcol = lax.axis_index("prow"), lax.axis_index("pcol")
    x, r = pcol % 2, prow % 2
    pcol_x, prow_x = pcol + 1 - 2 * x, prow + 1 - 2 * r
    is_s0, is_s1, is_g = pcol == 0, pcol == 1, pcol >= 2
    source, last = pcol < 2, pcol + 2 >= n_pcol
    top, bottom = prow < 2, prow + 2 >= n_prow
    far = jnp.logical_not(last)
    lends, borrows = (prow == 2) & (moved > 0), (prow == 0) & (moved > 0)

    a0 = jnp.where(prow == 0, PER, 0)
    n_a = tiles - a0
    n_r = jnp.where(borrows, moved, 0)
    b0 = jnp.where(top, PER, jnp.where(lends, moved, 0))
    n_b = tiles - b0

    def at(ph, p):
        return buf.at[ph, pl.ds(pl.multiple_of(p * pkt, pkt), pkt)]

    def m_at(p):
        return m_ref.at[pl.ds(pl.multiple_of(p * pkt, pkt), pkt)]

    def own_at(p):
        return own.at[pl.ds(pl.multiple_of(p * pkt, pkt), pkt)]

    def remote(src, dst, send_sem, recv_sem, where):
        return pltpu.make_async_remote_copy(
            src_ref=src, dst_ref=dst, send_sem=send_sem, recv_sem=recv_sem,
            device_id=where, device_id_type=MESH,
        )

    def fwd_copy(ph, p, src=None):
        ref = at(ph, p)
        return remote(ref if src is None else src, ref, fwd.at[ph, p], recv.at[ph, p], {"pcol": pcol + 2})

    def cross_copy(ph, p, src=None):
        ref = at(ph, p)
        return remote(ref if src is None else src, ref, cross.at[ph, p], recv.at[ph, p], {"pcol": pcol_x})

    def raw_copy(p):
        return remote(m_at(p), own_at(p), cross.at[0, p], recv.at[1, p], {"pcol": pcol_x})

    def lent(j):
        return 2 * (2 * (j // 2) + x) + j % 2

    def lend_copy(j):
        return remote(at(1, lent(j)), at(1, n_pkt + j), ysem.at[j], recv.at[1, n_pkt + j], {"prow": prow - 2})

    def give_copy(j):
        return remote(at(1, n_pkt + j), at(1, lent(j)), ysem.at[j], recv.at[1, lent(j)], {"prow": prow + 2})

    def arrived(ph, p):
        cross_copy(ph, p).wait_recv()

    def loop(lo, hi, step):
        def one(k, carry):
            step(k)
            return carry

        lax.fori_loop(lo, hi, one, 0)

    def pair(t, lane):
        p = 2 * (2 * t + lane)
        return p, p + 1

    load_lane = pltpu.make_async_copy(m_ref, buf.at[0, pl.ds(0, rows)], load_sem.at[0])
    load_own = pltpu.make_async_copy(m_ref, own, load_sem.at[0])
    load_u = pltpu.make_async_copy(u_hbm, uf, load_sem.at[1])
    load_l = pltpu.make_async_copy(l_hbm, lf, load_sem.at[2])
    has_head = (prow == 0) & (pcol >= 1)
    load_head = pltpu.make_async_copy(m_ref.at[pl.ds(0, width)], head, load_sem.at[3])
    pl.when(has_head)(load_head.start)
    load_u.start()
    load_l.start()
    pl.when(is_s0)(load_lane.start)
    pl.when(jnp.logical_not(is_s0))(load_own.start)

    barrier = pltpu.get_barrier_semaphore()

    def greet(where):
        pl.semaphore_signal(barrier, inc=1, device_id=where, device_id_type=MESH)

    greet({"pcol": pcol_x})
    greet({"prow": prow_x})
    for ok, where in (
        (jnp.logical_not(source), {"pcol": pcol - 2}),
        (far, {"pcol": pcol + 2}),
        (jnp.logical_not(top), {"prow": prow - 2}),
        (jnp.logical_not(bottom), {"prow": prow + 2}),
    ):
        pl.when(ok)(functools.partial(greet, where))
    absent = [jnp.where(ok, 1, 0) for ok in (source, last, top, bottom)]
    pl.semaphore_wait(barrier, 6 - sum(absent))

    def head_copy(i, where, src=head):
        return remote(src, head, hsend.at[i], hrecv.at[0], where)

    def pass_head(src=head):
        head_copy(0, {"prow": prow + 1}, src).start()
        pl.when(jnp.logical_not(bottom))(lambda: head_copy(1, {"prow": prow + 2}, src).start())

    @pl.when(has_head)
    def _():
        first = m_ref.at[pl.ds(0, width)]
        pl.when(is_s1)(lambda: head_copy(2, {"pcol": pcol_x}, first).start())
        pass_head(first)

    @pl.when(is_s0)
    def _():
        def send(t):
            for p, c in zip(pair(t, 0), pair(t, 1)):
                pl.when(far)(lambda: fwd_copy(0, p, m_at(p)).start())
                cross_copy(0, c, m_at(c)).start()

        loop(a0, tiles, send)

    @pl.when(is_s1)
    def _():
        def send(t):
            for p in pair(t, 0):
                raw_copy(p).start()

        loop(a0, tiles, send)

    def split(src, dst, panel):
        rest = src[panel]
        for i in range(PIECES):
            piece = rest.astype(BF)
            dst[panel, i] = piece
            rest = rest - piece.astype(F32)

    load_u.wait()
    load_l.wait()
    split(lf, ls, 0)
    split(uf, us, 0)
    pl.when(source)(lambda: split(uf, us, 1))
    pl.when(is_g & (prow == 1))(lambda: split(lf, ls, 1))
    pl.when(is_s0)(load_lane.wait)
    pl.when(jnp.logical_not(is_s0))(load_own.wait)

    def lower_times(panel, value, out):
        upper = sum(dot(ls[panel, i, :half, :half], value[:half]) for i in reversed(range(PIECES)))
        out[:half] = upper.astype(BF)
        lower = sum(dot(ls[panel, i, half:], value) for i in reversed(range(PIECES)))
        out[half:] = lower.astype(BF)

    def first_upper():
        pl.when(has_head)(load_head.wait)

        @pl.when(jnp.logical_not(has_head))
        def _():
            head_copy(0, {"prow": prow_x}).wait_recv()
            pl.when(r == 0)(pass_head)

        lower_times(0, head[...], u0)

    def out_copy(src, at_row, n, sem):
        return pltpu.make_async_copy(src, out_ref.at[pl.ds(at_row, n)], sem)

    def out_tile(src, t):
        here = pl.ds(pl.multiple_of(t * tile, tile), tile)
        return pltpu.make_async_copy(src.at[here], out_ref.at[here], out_sem.at[t])

    def out_first(src):
        return out_copy(src, 0, width, out_sem.at[tiles])

    def make_lower(t, low, lane):
        here = pl.ds(pl.multiple_of((2 * t + lane) * unit, unit), unit)
        cur = (own[here].astype(F32) - dot(low, u0[...])).astype(BF)
        value = times_upper(cur, us, 1)
        buf[1, here] = jnp.where((prow == 1) & (t < PER), cur, value)

    def lend(t):
        @pl.when(lends & (t >= 0) & (t < moved))
        def _():
            for i in range(2):
                lend_copy(2 * t + i).start()

    def borrow():
        @pl.when(borrows)
        def _():
            def one(j):
                arrived(1, n_pkt + j)
                pl.when(far)(lambda: fwd_copy(1, n_pkt + j).start())

            loop(0, 2 * moved, one)

    def sent_common():
        pl.when(lends)(lambda: loop(0, 2 * moved, lambda j: lend_copy(j).wait_send()))
        pl.when(borrows & far)(lambda: loop(0, 2 * moved, lambda j: fwd_copy(1, n_pkt + j).wait_send()))

    @pl.when(is_s0)
    def _():
        first_upper()
        wait_raw = lambda p: remote(own_at(p), own_at(p), cross.at[1, p], recv.at[1, p], {"pcol": pcol_x}).wait_recv()
        begin = 16

        pl.when(prow == 0)(lambda: out_first(buf.at[0, pl.ds(0, width)]).start())

        def send(t):
            for p in pair(t, 0):
                pl.when(far & (t >= b0))(lambda: fwd_copy(1, p).start())
                cross_copy(1, p).start()

        def step(i):
            t = a0 + i
            here = pl.ds(pl.multiple_of(t * tile, tile), tile)
            low = times_upper(buf[0, here], us, 0)
            buf[0, here] = low
            for p in pair(t, 0):
                wait_raw(p)
            make_lower(t, low[:unit], 0)
            out_tile(buf.at[0], t).start()
            lend(t - 1)
            pl.when(i == begin)(borrow)

            @pl.when(i > begin)
            def _():
                for n in range(2):
                    send(a0 + 2 * (i - begin - 1) + n)

        loop(0, n_a, step)
        loop(a0 + 2 * (n_a - begin - 1), tiles, send)

        def sent(t):
            for p, c in zip(pair(t, 0), pair(t, 1)):
                pl.when(far)(lambda: fwd_copy(0, p).wait_send())
                cross_copy(0, c).wait_send()
                pl.when(far & (t >= b0))(lambda: fwd_copy(1, p).wait_send())
                cross_copy(1, p).wait_send()
            out_tile(buf.at[0], t).wait()

        loop(a0, tiles, sent)
        sent_common()
        pl.when(prow == 0)(lambda: out_first(buf.at[0, pl.ds(0, width)]).wait())

    @pl.when(is_s1)
    def _():
        lag = 8

        def relay(t):
            for p in pair(t, 1):
                arrived(0, p)
                pl.when(far)(lambda: fwd_copy(0, p).start())

        def make(t):
            here = pl.ds(pl.multiple_of((2 * t + 1) * unit, unit), unit)
            make_lower(t, times_upper(buf[0, here], us, 0), 1)
            lend(t - 1)

        def step(s):
            relay(a0 + s)
            pl.when(s == lag)(first_upper)
            pl.when(s >= lag)(lambda: make(a0 + s - lag))

        loop(0, n_a, step)
        pl.when(prow == 0)(lambda: out_first(u0).start())
        borrow()

        def late(i):
            pl.when(i < lag)(lambda: make(tiles - lag + i))
            for p in pair(b0 + i, 1):
                pl.when(far)(lambda: fwd_copy(1, p).start())

        loop(0, n_b, late)

        def finish(t):
            for p in pair(t, 0):
                arrived(1, p)
            out_tile(buf.at[1], t).start()

        loop(a0, tiles, finish)

        def sent(t):
            for p, c in zip(pair(t, 0), pair(t, 1)):
                raw_copy(p).wait_send()
                pl.when(far)(lambda: fwd_copy(0, c).wait_send())
                pl.when(far & (t >= b0))(lambda: fwd_copy(1, c).wait_send())
            out_tile(buf.at[1], t).wait()

        loop(a0, tiles, sent)
        sent_common()

        @pl.when(prow == 0)
        def _():
            out_first(u0).wait()
            head_copy(2, {"pcol": pcol_x}).wait_send()

    @pl.when(is_g)
    def _():
        lag_a = 4
        lag_b = jnp.where(x == 0, 4, 3)
        b_from = n_a + n_r
        total = b_from + n_b
        cross_lent = tiles
        use_lent = tiles + 6
        first_of_1 = lag_a + PER

        def u1_copy(i, where):
            return remote(u1, u1, hsend.at[3 + i], hrecv.at[1], where)

        def pass_u1():
            u1_copy(0, {"prow": prow - 1}).start()
            pl.when(jnp.logical_not(bottom))(lambda: u1_copy(1, {"prow": prow + 2}).start())

        def arrived_u1():
            u1_copy(0, {"prow": prow_x}).wait_recv()

        def apply_a(t):
            for p in pair(t, 1 - x):
                arrived(0, p)
            here = pl.ds(pl.multiple_of(t * tile, tile), tile)
            low = times_upper(buf[0, here], us, 0)
            own[here] = (own[here].astype(F32) - dot(low, u0[...])).astype(BF)

        def apply_b(t):
            for p in pair(t, 1 - x):
                arrived(1, p)
            here = pl.ds(pl.multiple_of(t * tile, tile), tile)
            own[here] = (own[here].astype(F32) - dot(buf[1, here], u1[...])).astype(BF)
            out_tile(own, t).start()

        def step(s):
            in_a = s < n_a
            in_r = jnp.logical_not(in_a) & (s < b_from)
            ph = jnp.where(in_a, 0, 1)
            p0 = jnp.where(in_a, 2 * (2 * (a0 + s) + x), 2 * (2 * (b0 + s - b_from) + x))
            p0 = jnp.where(in_r, n_pkt + 2 * (s - n_a), p0)

            def relay(i):
                @pl.when(s < total)
                def _():
                    p = p0 + i
                    arrived(ph, p)
                    pl.when(far)(lambda: fwd_copy(ph, p).start())
                    pl.when(jnp.logical_not(in_r))(lambda: cross_copy(ph, p).start())
                    pl.when(in_r)(lambda: give_copy(p - n_pkt).start())

            relay(0)
            pl.when(s == lag_a)(first_upper)
            ta = s - lag_a
            pl.when((ta >= 0) & (ta < n_a))(lambda: apply_a(a0 + ta))
            relay(1)

            @pl.when((prow == 1) & (s == first_of_1))
            def _():
                lower_times(1, own[pl.ds(0, width)], u1)

            pl.when((prow == 1) & (s == first_of_1 + 1))(pass_u1)
            pl.when((prow == 0) & (s == first_of_1 + 1))(lambda: out_first(u0).start())
            pl.when((prow == 1) & (s == first_of_1 + 1))(lambda: out_first(u1).start())

            @pl.when((r == 1) & (prow > 1) & (s == tiles - PER - 2))
            def _():
                arrived_u1()
                pass_u1()

            pl.when((r == 0) & (s == tiles - PER - 1))(arrived_u1)

            @pl.when(lends & (s >= cross_lent) & (s < cross_lent + moved))
            def _():
                for p in pair(s - cross_lent, x):
                    arrived(1, p)
                    cross_copy(1, p).start()

            tb = s - b_from - lag_b
            n_plain = jnp.where((tb >= 0) & (tb < n_b), 1, 0)
            n_lent = jnp.where(lends & (s >= use_lent) & (s < use_lent + moved), 1, 0)
            loop(
                1 - n_plain, 1 + n_lent,
                lambda k: apply_b(jnp.where(k == 0, b0 + tb, s - use_lent)),
            )

        loop(0, total + lag_b, step)

        def sent(ph, t):
            for p in pair(t, x):
                pl.when(far)(lambda: fwd_copy(ph, p).wait_send())
                cross_copy(ph, p).wait_send()

        loop(a0, tiles, lambda t: sent(0, t))
        loop(b0, tiles, lambda t: sent(1, t))

        @pl.when(borrows)
        def _():
            def one(j):
                give_copy(j).wait_send()
                pl.when(far)(lambda: fwd_copy(1, n_pkt + j).wait_send())

            loop(0, 2 * moved, one)

        @pl.when(lends)
        def _():
            def one(t):
                for p in pair(t, x):
                    cross_copy(1, p).wait_send()

            loop(0, moved, one)

        @pl.when(r == 1)
        def _():
            u1_copy(0, {"prow": prow_x}).wait_send()
            pl.when(jnp.logical_not(bottom))(lambda: u1_copy(1, {"prow": prow_x}).wait_send())

        loop(jnp.where(top, PER, 0), tiles, lambda t: out_tile(own, t).wait())
        pl.when(top)(lambda: out_first(u0).wait())

    @pl.when(r == 0)
    def _():
        head_copy(0, {"prow": prow_x}).wait_send()
        pl.when(jnp.logical_not(bottom))(lambda: head_copy(1, {"prow": prow_x}).wait_send())


def body(n_prow, n_pcol, matrix, u_inverse, l_inverse):
    rows, width = matrix.shape
    tile, unit, pkt, tiles, moved = sizes(rows, width, n_prow)
    square = (width, width)
    n_pkt = rows // pkt
    dma = pltpu.SemaphoreType.DMA
    operands = [
        pltpu.with_memory_space_constraint(a, pltpu.HBM) for a in (matrix, u_inverse, l_inverse)
    ]
    return pl.pallas_call(
        functools.partial(kernel, n_prow, n_pcol, width),
        out_shape=jax.ShapeDtypeStruct(matrix.shape, matrix.dtype),
        in_specs=[pl.BlockSpec(memory_space=pltpu.HBM)] * 3,
        out_specs=pl.BlockSpec(memory_space=pl.ANY),
        scratch_shapes=[
            pltpu.VMEM((rows, width), BF),
            pltpu.VMEM((2, rows + moved * unit, width), BF),
            pltpu.VMEM(square, BF),
            pltpu.VMEM((2,) + square, F32),
            pltpu.VMEM((2,) + square, F32),
            pltpu.VMEM((2, PIECES) + square, BF),
            pltpu.VMEM((2, PIECES) + square, BF),
            pltpu.VMEM(square, BF),
            pltpu.VMEM(square, BF),
            dma((4,)),
            dma((2, n_pkt + 2 * moved)),
            dma((2, n_pkt + 2 * moved)),
            dma((2, n_pkt)),
            dma((max(2 * moved, 1),)),
            dma((2,)),
            dma((5,)),
            dma((tiles + 1,)),
        ],
        compiler_params=pltpu.CompilerParams(
            collective_id=0, has_side_effects=True, vmem_limit_bytes=46 * 1024 * 1024
        ),
    )(*operands)


def solution(mesh):
    run = functools.partial(body, mesh.shape["prow"], mesh.shape["pcol"])
    in_specs = (P("prow", "pcol"), P(), P())
    out_specs = P("prow", "pcol")
    return jax.shard_map(run, mesh=mesh, in_specs=in_specs, out_specs=out_specs, check_vma=False)
```

```python
import functools

import jax
import jax.numpy as jnp
from jax import lax
from jax.experimental import pallas as pl
from jax.experimental.pallas import tpu as pltpu
from jax.sharding import PartitionSpec as P

MESH = pl.DeviceIdType.MESH
BF = jnp.bfloat16
F32 = jnp.float32
PIECES = 2
PER = 4
EARLY = 8
HEAD_AT = 20


def sizes(rows, width, n_prow):
    tile = width // PER
    moved = 3 * PER // 2 if n_prow > 2 else 0
    return tile, tile // 2, tile // 4, rows // tile, moved


def dot(a, b):
    return jnp.dot(a, b, preferred_element_type=F32)


def times_upper(a, u_ref, panel):
    half = a.shape[1] // 2
    left = sum(dot(a[:, :half], u_ref[panel, i, :half, :half]) for i in reversed(range(PIECES)))
    right = sum(dot(a, u_ref[panel, i, :, half:]) for i in reversed(range(PIECES)))
    return jnp.concatenate([left, right], 1).astype(BF)


def kernel(
    n_prow, n_pcol, width, m_ref, u_hbm, l_hbm, out_ref,
    own, buf, head, uf, lf, us, ls, u0, u1,
    load_sem, lane_sem, unit_sem, send_sem, hrecv, hsend, out_sem,
):
    rows = own.shape[0]
    tile, unit, pkt, tiles, moved = sizes(rows, width, n_prow)
    n_pkt = rows // pkt
    lane_pkts = 2 * tiles
    half = width // 2
    prow, pcol = lax.axis_index("prow"), lax.axis_index("pcol")
    x, r = pcol % 2, prow % 2
    pcol_x, prow_x = pcol + 1 - 2 * x, prow + 1 - 2 * r
    is_s0, is_s1, is_g = pcol == 0, pcol == 1, pcol >= 2
    source, last = pcol < 2, pcol + 2 >= n_pcol
    top, bottom = prow < 2, prow + 2 >= n_prow
    far = jnp.logical_not(last)
    lends, borrows = (prow == 2) & (moved > 0), (prow == 0) & (moved > 0)

    a0 = jnp.where(prow == 0, PER, 0)
    n_a = tiles - a0
    n_r = jnp.where(borrows, moved, 0)
    b0 = jnp.where(top, PER, jnp.where(lends, moved, 0))
    n_b = tiles - b0

    def at(ph, p):
        return buf.at[ph, pl.ds(pl.multiple_of(p * pkt, pkt), pkt)]

    def m_at(p):
        return m_ref.at[pl.ds(pl.multiple_of(p * pkt, pkt), pkt)]

    def unit_of(t, lane):
        return pl.ds(pl.multiple_of((2 * t + lane) * unit, unit), unit)

    def tile_of(t):
        return pl.ds(pl.multiple_of(t * tile, tile), tile)

    def remote(src, dst, sem, recv_sem, where):
        return pltpu.make_async_remote_copy(
            src_ref=src, dst_ref=dst, send_sem=sem, recv_sem=recv_sem,
            device_id=where, device_id_type=MESH,
        )

    FWD, CROSS, SIDE = (send_sem.at[i] for i in range(3))

    def lane_at(ph, t, i):
        return lane_sem.at[ph * lane_pkts + 2 * t + i]

    def spare_at(j):
        return lane_sem.at[jnp.where(j < 2 * PER, j, lane_pkts + j - 2 * PER)]

    def unit_at(ph, t):
        return unit_sem.at[ph * tiles + t]

    def row_of(t, lane, i):
        return 2 * (2 * t + lane) + i

    def fwd_copy(ph, p, sem, src=None):
        ref = at(ph, p)
        return remote(ref if src is None else src, ref, FWD, sem, {"pcol": pcol + 2})

    def arrived(ph, p, sem):
        ref = at(ph, p)
        remote(ref, ref, FWD, sem, {"pcol": pcol_x}).wait_recv()

    def cross_copy(ph, t, p):
        ref = at(ph, p)
        return remote(ref, ref, CROSS, unit_at(ph, t), {"pcol": pcol_x})

    def unit_copy(ph, t, lane, dst, src=None):
        ref = dst.at[unit_of(t, lane)]
        return remote(ref if src is None else src, ref, CROSS, unit_at(ph, t), {"pcol": pcol_x})

    def lend_copy(j):
        return remote(at(1, row_of(j // 2, x, j % 2)), at(1, n_pkt + j), SIDE, spare_at(j), {"prow": prow - 2})

    def give_copy(j):
        return remote(
            at(1, n_pkt + j), at(1, row_of(j // 2, x, j % 2)), SIDE, lane_at(1, j // 2, j % 2), {"prow": prow + 2}
        )

    def sent(sem, units):
        ref = buf.at[0, pl.ds(0, units * unit)]
        remote(ref, ref, sem, lane_sem.at[0], {"pcol": pcol_x}).wait_send()

    def sent_by_prow(sem, units):
        for k, n in enumerate(units):
            here = prow == k if k + 1 < len(units) else prow >= k
            pl.when(here)(functools.partial(sent, sem, n))

    def loop(lo, hi, step):
        def one(k, carry):
            step(k)
            return carry

        lax.fori_loop(lo, hi, one, 0)

    load_lane = pltpu.make_async_copy(m_ref, buf.at[0, pl.ds(0, rows)], load_sem.at[0])
    load_own = pltpu.make_async_copy(m_ref, own, load_sem.at[0])
    load_u = pltpu.make_async_copy(u_hbm, uf, load_sem.at[1])
    load_l = pltpu.make_async_copy(l_hbm, lf, load_sem.at[2])
    has_head = (prow == 0) & (pcol >= 1)
    load_head = pltpu.make_async_copy(m_ref.at[pl.ds(0, width)], head, load_sem.at[3])
    pl.when(has_head)(load_head.start)
    load_u.start()
    load_l.start()
    pl.when(is_s0)(load_lane.start)
    pl.when(jnp.logical_not(is_s0))(load_own.start)

    barrier = pltpu.get_barrier_semaphore()

    def greet(where):
        pl.semaphore_signal(barrier, inc=1, device_id=where, device_id_type=MESH)

    greet({"pcol": pcol_x})
    greet({"prow": prow_x})
    for ok, where in (
        (jnp.logical_not(source), {"pcol": pcol - 2}),
        (far, {"pcol": pcol + 2}),
        (jnp.logical_not(top), {"prow": prow - 2}),
        (jnp.logical_not(bottom), {"prow": prow + 2}),
    ):
        pl.when(ok)(functools.partial(greet, where))
    absent = [jnp.where(ok, 1, 0) for ok in (source, last, top, bottom)]
    pl.semaphore_wait(barrier, 6 - sum(absent))

    def head_copy(i, where, src=head):
        return remote(src, head, hsend.at[i], hrecv.at[0], where)

    def pass_head(src=head):
        head_copy(0, {"prow": prow + 1}, src).start()
        pl.when(jnp.logical_not(bottom))(lambda: head_copy(1, {"prow": prow + 2}, src).start())

    @pl.when(has_head)
    def _():
        first = m_ref.at[pl.ds(0, width)]
        pl.when(is_s1)(lambda: head_copy(2, {"pcol": pcol_x}, first).start())
        pass_head(first)

    @pl.when(is_s0)
    def _():
        def send(t):
            for i in range(2):
                p, c = row_of(t, 0, i), row_of(t, 1, i)
                pl.when(far)(lambda: fwd_copy(0, p, lane_at(0, t, i), m_at(p)).start())
                remote(m_at(c), at(0, c), CROSS, lane_at(0, t, i), {"pcol": pcol_x}).start()

        loop(a0, tiles, send)

    @pl.when(is_s1)
    def _():
        def send(t):
            unit_copy(1, t, 0, own, m_ref.at[unit_of(t, 0)]).start()

        loop(a0, tiles, send)

    def split(src, dst, panel):
        rest = src[panel]
        for i in range(PIECES):
            piece = rest.astype(BF)
            dst[panel, i] = piece
            rest = rest - piece.astype(F32)

    load_u.wait()
    load_l.wait()
    split(lf, ls, 0)
    split(uf, us, 0)
    pl.when(source)(lambda: split(uf, us, 1))
    pl.when(is_g & (prow == 1))(lambda: split(lf, ls, 1))
    pl.when(is_s0)(load_lane.wait)
    pl.when(jnp.logical_not(is_s0))(load_own.wait)

    def lower_times(panel, value, out):
        upper = sum(dot(ls[panel, i, :half, :half], value[:half]) for i in reversed(range(PIECES)))
        out[:half] = upper.astype(BF)
        lower = sum(dot(ls[panel, i, half:], value) for i in reversed(range(PIECES)))
        out[half:] = lower.astype(BF)

    def take_head():
        pl.when(has_head)(load_head.wait)

        @pl.when(jnp.logical_not(has_head))
        def _():
            head_copy(0, {"prow": prow_x}).wait_recv()
            pl.when(r == 0)(pass_head)

    def make_u0():
        lower_times(0, head[...], u0)

    def out_tile(src, t):
        here = tile_of(t)
        return pltpu.make_async_copy(src.at[here], out_ref.at[here], out_sem)

    def out_first(src):
        return pltpu.make_async_copy(src, out_ref.at[pl.ds(0, width)], out_sem)

    def make_lower(t, low, lane):
        here = unit_of(t, lane)
        cur = (own[here].astype(F32) - dot(low, u0[...])).astype(BF)
        value = times_upper(cur, us, 1)
        buf[1, here] = jnp.where((prow == 1) & (t < PER), cur, value)

    def lend(t):
        @pl.when(lends & (t >= 0) & (t < moved))
        def _():
            for i in range(2):
                lend_copy(2 * t + i).start()

    def borrow():
        @pl.when(borrows)
        def _():
            def one(j):
                arrived(1, n_pkt + j, spare_at(j))
                pl.when(far)(lambda: fwd_copy(1, n_pkt + j, spare_at(j)).start())

            loop(0, 2 * moved, one)

    @pl.when(is_s0)
    def _():
        pl.when(prow == 0)(lambda: out_first(buf.at[0, pl.ds(0, width)]).start())

        def low_step(i):
            t = a0 + i
            here = tile_of(t)
            buf[0, here] = times_upper(buf[0, here], us, 0)
            out_tile(buf.at[0], t).start()
            pl.when(i == jnp.where(prow == 0, HEAD_AT, n_a - 1))(take_head)

        loop(0, n_a, low_step)
        make_u0()

        def send(t):
            for i in range(2):
                p = row_of(t, 0, i)
                pl.when(far & (t >= b0))(lambda: fwd_copy(1, p, lane_at(1, t, i)).start())
            unit_copy(1, t, 0, buf.at[1]).start()

        def step(i):
            t = a0 + i
            unit_copy(1, t, 0, own).wait_recv()
            make_lower(t, buf[0, unit_of(t, 0)], 0)
            lend(t - 1)
            pl.when(i == EARLY + 1)(borrow)
            pl.when(i >= 1)(lambda: send(t - 1))

        loop(0, n_a, step)
        send(tiles - 1)

    @pl.when(is_s1)
    def _():
        lag = 8

        def relay(t):
            for i in range(2):
                p, sem = row_of(t, 1, i), lane_at(0, t, i)
                arrived(0, p, sem)
                pl.when(far)(lambda: fwd_copy(0, p, sem).start())

        def make(t):
            make_lower(t, times_upper(buf[0, unit_of(t, 1)], us, 0), 1)
            lend(t - 1)

        def step(s):
            relay(a0 + s)
            pl.when(s == jnp.where(r == 0, PER, lag))(take_head)
            pl.when(s == lag)(make_u0)
            pl.when(s >= lag)(lambda: make(a0 + s - lag))

        loop(0, n_a, step)
        pl.when(prow == 0)(lambda: out_first(u0).start())

        def late(i):
            pl.when(i < lag)(lambda: make(tiles - lag + i))
            pl.when(i == EARLY)(borrow)
            t = b0 + i
            for n in range(2):
                pl.when(far)(lambda: fwd_copy(1, row_of(t, 1, n), lane_at(1, t, n)).start())

        loop(0, n_b, late)

        def finish(t):
            unit_copy(1, t, 0, buf.at[1]).wait_recv()
            out_tile(buf.at[1], t).start()

        loop(a0, tiles, finish)

    @pl.when(is_g)
    def _():
        lag_a = 6
        lag_b = jnp.where(x == 0, 6, 4)
        total = n_a + n_r + n_b
        cross_lent = tiles - PER + EARLY + 3
        use_lent = cross_lent + 6
        first_of_1 = lag_a + PER

        def u1_copy(i, where):
            return remote(u1, u1, hsend.at[3 + i], hrecv.at[1], where)

        def pass_u1():
            u1_copy(0, {"prow": prow - 1}).start()
            pl.when(jnp.logical_not(bottom))(lambda: u1_copy(1, {"prow": prow + 2}).start())

        def arrived_u1():
            u1_copy(0, {"prow": prow_x}).wait_recv()

        def apply_a(t):
            unit_copy(0, t, 1 - x, buf.at[0]).wait_recv()
            here = tile_of(t)
            low = times_upper(buf[0, here], us, 0)
            own[here] = (own[here].astype(F32) - dot(low, u0[...])).astype(BF)

        def apply_b(t):
            unit_copy(1, t, 1 - x, buf.at[1]).wait_recv()
            here = tile_of(t)
            own[here] = (own[here].astype(F32) - dot(buf[1, here], u1[...])).astype(BF)
            out_tile(own, t).start()

        def place(s):
            q = s - n_a
            spare = (q >= EARLY) & (q < EARLY + n_r)
            return spare, b0 + q - jnp.where(q >= EARLY + n_r, n_r, 0)

        def step(s):
            in_a = s < n_a
            spare, tb = place(s)
            in_r = jnp.logical_not(in_a) & spare
            ph = jnp.where(in_a, 0, 1)
            t = jnp.where(in_a, a0 + s, tb)

            def relay(i):
                @pl.when((s < total) & jnp.logical_not(in_r))
                def _():
                    p, sem = row_of(t, x, i), lane_at(ph, t, i)
                    arrived(ph, p, sem)
                    pl.when(far)(lambda: fwd_copy(ph, p, sem).start())
                    cross_copy(ph, t, p).start()

                @pl.when(in_r)
                def _():
                    j = 2 * (s - n_a - EARLY) + i
                    arrived(1, n_pkt + j, spare_at(j))
                    pl.when(far)(lambda: fwd_copy(1, n_pkt + j, spare_at(j)).start())
                    give_copy(j).start()

            relay(0)
            pl.when(s == jnp.where(r == 0, PER, lag_a))(take_head)
            pl.when(s == lag_a)(make_u0)
            ta = s - lag_a
            pl.when((ta >= 0) & (ta < n_a))(lambda: apply_a(a0 + ta))
            relay(1)

            @pl.when((prow == 1) & (s == first_of_1))
            def _():
                lower_times(1, own[pl.ds(0, width)], u1)

            pl.when((prow == 1) & (s == first_of_1 + 1))(pass_u1)
            pl.when((prow == 0) & (s == first_of_1 + 1))(lambda: out_first(u0).start())
            pl.when((prow == 1) & (s == first_of_1 + 1))(lambda: out_first(u1).start())

            @pl.when((r == 1) & (prow > 1) & (s == tiles - PER - 2))
            def _():
                arrived_u1()
                pass_u1()

            pl.when((r == 0) & (s == tiles - PER - 1))(arrived_u1)

            @pl.when(lends & (s >= cross_lent) & (s < cross_lent + moved))
            def _():
                k = s - cross_lent
                for i in range(2):
                    p = row_of(k, x, i)
                    arrived(1, p, lane_at(1, k, i))
                    cross_copy(1, k, p).start()

            u = s - lag_b
            u_spare, u_tile = place(u)
            n_plain = jnp.where((u >= n_a) & (u < total) & jnp.logical_not(u_spare), 1, 0)
            n_lent = jnp.where(lends & (s >= use_lent) & (s < use_lent + moved), 1, 0)
            loop(
                1 - n_plain, 1 + n_lent,
                lambda k: apply_b(jnp.where(k == 0, u_tile, s - use_lent)),
            )

        loop(0, total + lag_b, step)

        @pl.when(r == 1)
        def _():
            u1_copy(0, {"prow": prow_x}).wait_send()
            pl.when(jnp.logical_not(bottom))(lambda: u1_copy(1, {"prow": prow_x}).wait_send())

    @pl.when(r == 0)
    def _():
        head_copy(0, {"prow": prow_x}).wait_send()
        pl.when(jnp.logical_not(bottom))(lambda: head_copy(1, {"prow": prow_x}).wait_send())

    pl.when(is_s1 & (prow == 0))(lambda: head_copy(2, {"pcol": pcol_x}).wait_send())
    side = (borrows & is_g) | (lends & source)
    pl.when(side)(lambda: sent(SIDE, moved)) if moved else None
    full = 2 * tiles
    ahead = (full - 2 * PER + moved, full - PER, full - moved, full)
    pl.when(far)(lambda: sent_by_prow(FWD, ahead))
    pl.when(is_g)(lambda: sent_by_prow(CROSS, (full - 2 * PER, full - PER, full)))
    pl.when(is_s0)(lambda: sent_by_prow(CROSS, (full - 2 * PER, full)))
    pl.when(is_s1)(lambda: sent_by_prow(CROSS, (tiles - PER, tiles)))
    pltpu.make_async_copy(own, out_ref, out_sem).wait()


def body(n_prow, n_pcol, matrix, u_inverse, l_inverse):
    rows, width = matrix.shape
    tile, unit, pkt, tiles, moved = sizes(rows, width, n_prow)
    square = (width, width)
    dma = pltpu.SemaphoreType.DMA
    operands = [
        pltpu.with_memory_space_constraint(a, pltpu.HBM) for a in (matrix, u_inverse, l_inverse)
    ]
    return pl.pallas_call(
        functools.partial(kernel, n_prow, n_pcol, width),
        out_shape=jax.ShapeDtypeStruct(matrix.shape, matrix.dtype),
        in_specs=[pl.BlockSpec(memory_space=pltpu.HBM)] * 3,
        out_specs=pl.BlockSpec(memory_space=pl.ANY),
        scratch_shapes=[
            pltpu.VMEM((rows, width), BF),
            pltpu.VMEM((2, rows + moved * unit, width), BF),
            pltpu.VMEM(square, BF),
            pltpu.VMEM((2,) + square, F32),
            pltpu.VMEM((2,) + square, F32),
            pltpu.VMEM((2, PIECES) + square, BF),
            pltpu.VMEM((2, PIECES) + square, BF),
            pltpu.VMEM(square, BF),
            pltpu.VMEM(square, BF),
            dma((4,)),
            dma((4 * tiles,)),
            dma((2 * tiles,)),
            dma((3,)),
            dma((2,)),
            dma((5,)),
            dma(()),
        ],
        compiler_params=pltpu.CompilerParams(
            collective_id=0, has_side_effects=True, vmem_limit_bytes=46 * 1024 * 1024
        ),
    )(*operands)


def solution(mesh):
    run = functools.partial(body, mesh.shape["prow"], mesh.shape["pcol"])
    in_specs = (P("prow", "pcol"), P(), P())
    out_specs = P("prow", "pcol")
    return jax.shard_map(run, mesh=mesh, in_specs=in_specs, out_specs=out_specs, check_vma=False)
```

```python
import functools

import jax
import jax.numpy as jnp
from jax import lax
from jax.experimental import pallas as pl
from jax.experimental.pallas import tpu as pltpu
from jax.sharding import PartitionSpec as P

MESH = pl.DeviceIdType.MESH
BF = jnp.bfloat16
F32 = jnp.float32
PIECES = 2
PER = 4
EARLY = 8
HEAD_AT = 20


def sizes(rows, width, n_prow):
    tile = width // PER
    moved = 3 * PER // 2 if n_prow > 2 else 0
    return tile, tile // 2, tile // 4, rows // tile, moved


def dot(a, b):
    return jnp.dot(a, b, preferred_element_type=F32)


def times_upper(a, u_ref, panel):
    half = a.shape[1] // 2
    left = sum(dot(a[:, :half], u_ref[panel, i, :half, :half]) for i in reversed(range(PIECES)))
    right = sum(dot(a, u_ref[panel, i, :, half:]) for i in reversed(range(PIECES)))
    return jnp.concatenate([left, right], 1).astype(BF)


def kernel(
    n_prow, n_pcol, width, m_ref, u_hbm, l_hbm, out_ref,
    own, buf, head, uf, lf, us, ls, u0, u1,
    load_sem, lane_sem, unit_sem, send_sem, hrecv, hsend, out_sem,
):
    rows = own.shape[0]
    tile, unit, pkt, tiles, moved = sizes(rows, width, n_prow)
    n_pkt = rows // pkt
    lane_pkts = 2 * tiles
    half = width // 2
    prow, pcol = lax.axis_index("prow"), lax.axis_index("pcol")
    x, r = pcol % 2, prow % 2
    pcol_x, prow_x = pcol + 1 - 2 * x, prow + 1 - 2 * r
    is_s0, is_s1, is_g = pcol == 0, pcol == 1, pcol >= 2
    source, last = pcol < 2, pcol + 2 >= n_pcol
    top, bottom = prow < 2, prow + 2 >= n_prow
    far = jnp.logical_not(last)
    lends, borrows = (prow == 2) & (moved > 0), (prow == 0) & (moved > 0)

    a0 = jnp.where(prow == 0, PER, 0)
    n_a = tiles - a0
    n_r = jnp.where(borrows, moved, 0)
    b0 = jnp.where(top, PER, jnp.where(lends, moved, 0))
    n_b = tiles - b0

    def at(ph, p):
        return buf.at[ph, pl.ds(pl.multiple_of(p * pkt, pkt), pkt)]

    def m_at(p):
        return m_ref.at[pl.ds(pl.multiple_of(p * pkt, pkt), pkt)]

    def unit_of(t, lane):
        return pl.ds(pl.multiple_of((2 * t + lane) * unit, unit), unit)

    def tile_of(t):
        return pl.ds(pl.multiple_of(t * tile, tile), tile)

    def remote(src, dst, sem, recv_sem, where):
        return pltpu.make_async_remote_copy(
            src_ref=src, dst_ref=dst, send_sem=sem, recv_sem=recv_sem,
            device_id=where, device_id_type=MESH,
        )

    FWD, CROSS, SIDE = (send_sem.at[i] for i in range(3))

    def lane_at(ph, t, i):
        return lane_sem.at[ph * lane_pkts + 2 * t + i]

    def spare_at(j):
        return lane_sem.at[jnp.where(j < 2 * PER, j, lane_pkts + j - 2 * PER)]

    def unit_at(ph, t):
        return unit_sem.at[ph * tiles + t]

    def row_of(t, lane, i):
        return 2 * (2 * t + lane) + i

    def fwd_copy(ph, p, sem, src=None):
        ref = at(ph, p)
        return remote(ref if src is None else src, ref, FWD, sem, {"pcol": pcol + 2})

    def arrived(ph, p, sem):
        ref = at(ph, p)
        remote(ref, ref, FWD, sem, {"pcol": pcol_x}).wait_recv()

    def cross_copy(ph, t, p):
        ref = at(ph, p)
        return remote(ref, ref, CROSS, unit_at(ph, t), {"pcol": pcol_x})

    def unit_copy(ph, t, lane, dst, src=None):
        ref = dst.at[unit_of(t, lane)]
        return remote(ref if src is None else src, ref, CROSS, unit_at(ph, t), {"pcol": pcol_x})

    def spare_row(k, i):
        return n_pkt + row_of(k, x, i)

    def spare_unit_at(k):
        return unit_sem.at[jnp.where(k < PER, k, tiles + k - PER)]

    def lend_copy(k, i):
        return remote(at(1, row_of(k, x, i)), at(1, spare_row(k, i)), SIDE, spare_at(2 * k + i), {"prow": prow - 2})

    def give_copy(k, i):
        return remote(at(1, spare_row(k, i)), at(1, row_of(k, x, i)), SIDE, lane_at(1, k, i), {"prow": prow + 2})

    def spare_cross_copy(k, i):
        ref = at(1, spare_row(k, i))
        return remote(ref, ref, CROSS, spare_unit_at(k), {"pcol": pcol_x})

    def give_unit_copy(k):
        src, dst = buf.at[1, unit_of(tiles + k, 1 - x)], buf.at[1, unit_of(k, 1 - x)]
        return remote(src, dst, SIDE, unit_at(1, k), {"prow": prow + 2})

    def spare_unit_arrived(k):
        ref = buf.at[1, unit_of(tiles + k, 1 - x)]
        remote(ref, ref, CROSS, spare_unit_at(k), {"pcol": pcol_x}).wait_recv()

    def sent(sem, units):
        ref = buf.at[0, pl.ds(0, units * unit)]
        remote(ref, ref, sem, lane_sem.at[0], {"pcol": pcol_x}).wait_send()

    def sent_by_prow(sem, units):
        for k, n in enumerate(units):
            here = prow == k if k + 1 < len(units) else prow >= k
            pl.when(here)(functools.partial(sent, sem, n))

    def loop(lo, hi, step):
        def one(k, carry):
            step(k)
            return carry

        lax.fori_loop(lo, hi, one, 0)

    load_lane = pltpu.make_async_copy(m_ref, buf.at[0, pl.ds(0, rows)], load_sem.at[0])
    load_own = pltpu.make_async_copy(m_ref, own, load_sem.at[0])
    load_u = pltpu.make_async_copy(u_hbm, uf, load_sem.at[1])
    load_l = pltpu.make_async_copy(l_hbm, lf, load_sem.at[2])
    has_head = (prow == 0) & (pcol >= 1)
    load_head = pltpu.make_async_copy(m_ref.at[pl.ds(0, width)], head, load_sem.at[3])
    pl.when(has_head)(load_head.start)
    load_u.start()
    load_l.start()
    pl.when(is_s0)(load_lane.start)
    pl.when(jnp.logical_not(is_s0))(load_own.start)

    barrier = pltpu.get_barrier_semaphore()

    def greet(where):
        pl.semaphore_signal(barrier, inc=1, device_id=where, device_id_type=MESH)

    greet({"pcol": pcol_x})
    greet({"prow": prow_x})
    for ok, where in (
        (jnp.logical_not(source), {"pcol": pcol - 2}),
        (far, {"pcol": pcol + 2}),
        (jnp.logical_not(top), {"prow": prow - 2}),
        (jnp.logical_not(bottom), {"prow": prow + 2}),
    ):
        pl.when(ok)(functools.partial(greet, where))
    absent = [jnp.where(ok, 1, 0) for ok in (source, last, top, bottom)]
    pl.semaphore_wait(barrier, 6 - sum(absent))

    def head_copy(i, where, src=head):
        return remote(src, head, hsend.at[i], hrecv.at[0], where)

    def pass_head(src=head):
        head_copy(0, {"prow": prow + 1}, src).start()
        pl.when(jnp.logical_not(bottom))(lambda: head_copy(1, {"prow": prow + 2}, src).start())

    @pl.when(has_head)
    def _():
        first = m_ref.at[pl.ds(0, width)]
        pl.when(is_s1)(lambda: head_copy(2, {"pcol": pcol_x}, first).start())
        pass_head(first)

    @pl.when(is_s0)
    def _():
        def send(t):
            for i in range(2):
                p, c = row_of(t, 0, i), row_of(t, 1, i)
                pl.when(far)(lambda: fwd_copy(0, p, lane_at(0, t, i), m_at(p)).start())
                remote(m_at(c), at(0, c), CROSS, lane_at(0, t, i), {"pcol": pcol_x}).start()

        loop(a0, tiles, send)

    @pl.when(is_s1)
    def _():
        def send(t):
            unit_copy(1, t, 0, own, m_ref.at[unit_of(t, 0)]).start()

        loop(a0, tiles, send)

    def split(src, dst, panel):
        rest = src[panel]
        for i in range(PIECES):
            piece = rest.astype(BF)
            dst[panel, i] = piece
            rest = rest - piece.astype(F32)

    load_u.wait()
    load_l.wait()
    split(lf, ls, 0)
    split(uf, us, 0)
    pl.when(source)(lambda: split(uf, us, 1))
    pl.when(is_g & (prow == 1))(lambda: split(lf, ls, 1))
    pl.when(is_s0)(load_lane.wait)
    pl.when(jnp.logical_not(is_s0))(load_own.wait)

    def lower_times(panel, value, out):
        upper = sum(dot(ls[panel, i, :half, :half], value[:half]) for i in reversed(range(PIECES)))
        out[:half] = upper.astype(BF)
        lower = sum(dot(ls[panel, i, half:], value) for i in reversed(range(PIECES)))
        out[half:] = lower.astype(BF)

    def take_head():
        pl.when(has_head)(load_head.wait)

        @pl.when(jnp.logical_not(has_head))
        def _():
            head_copy(0, {"prow": prow_x}).wait_recv()
            pl.when(r == 0)(pass_head)

    def make_u0():
        lower_times(0, head[...], u0)

    def out_tile(src, t):
        here = tile_of(t)
        return pltpu.make_async_copy(src.at[here], out_ref.at[here], out_sem)

    def out_first(src):
        return pltpu.make_async_copy(src, out_ref.at[pl.ds(0, width)], out_sem)

    def make_lower(t, low, lane):
        here = unit_of(t, lane)
        cur = (own[here].astype(F32) - dot(low, u0[...])).astype(BF)
        value = times_upper(cur, us, 1)
        buf[1, here] = jnp.where((prow == 1) & (t < PER), cur, value)

    def lend(t):
        @pl.when(lends & (t >= 0) & (t < moved))
        def _():
            for i in range(2):
                lend_copy(t, i).start()

    def borrow():
        @pl.when(borrows)
        def _():
            def one(k):
                for i in range(2):
                    p, sem = spare_row(k, i), spare_at(2 * k + i)
                    arrived(1, p, sem)
                    pl.when(far)(lambda: fwd_copy(1, p, sem).start())

            loop(0, moved, one)

    @pl.when(is_s0)
    def _():
        pl.when(prow == 0)(lambda: out_first(buf.at[0, pl.ds(0, width)]).start())

        def low_step(i):
            t = a0 + i
            here = tile_of(t)
            buf[0, here] = times_upper(buf[0, here], us, 0)
            out_tile(buf.at[0], t).start()
            pl.when(i == jnp.where(prow == 0, HEAD_AT, n_a - 1))(take_head)

        loop(0, n_a, low_step)
        make_u0()

        def send(t):
            for i in range(2):
                p = row_of(t, 0, i)
                pl.when(far & (t >= b0))(lambda: fwd_copy(1, p, lane_at(1, t, i)).start())
            unit_copy(1, t, 0, buf.at[1]).start()

        def step(i):
            t = a0 + i
            unit_copy(1, t, 0, own).wait_recv()
            make_lower(t, buf[0, unit_of(t, 0)], 0)
            lend(t - 1)
            pl.when(i == EARLY + 1)(borrow)
            pl.when(i >= 1)(lambda: send(t - 1))

        loop(0, n_a, step)
        send(tiles - 1)

    @pl.when(is_s1)
    def _():
        lag = 8

        def relay(t):
            for i in range(2):
                p, sem = row_of(t, 1, i), lane_at(0, t, i)
                arrived(0, p, sem)
                pl.when(far)(lambda: fwd_copy(0, p, sem).start())

        def make(t):
            make_lower(t, times_upper(buf[0, unit_of(t, 1)], us, 0), 1)
            lend(t - 1)

        def step(s):
            relay(a0 + s)
            pl.when(s == jnp.where(r == 0, PER, lag))(take_head)
            pl.when(s == lag)(make_u0)
            pl.when(s >= lag)(lambda: make(a0 + s - lag))

        loop(0, n_a, step)
        pl.when(prow == 0)(lambda: out_first(u0).start())

        def late(i):
            pl.when(i < lag)(lambda: make(tiles - lag + i))
            pl.when(i == EARLY)(borrow)
            t = b0 + i
            for n in range(2):
                pl.when(far)(lambda: fwd_copy(1, row_of(t, 1, n), lane_at(1, t, n)).start())

        loop(0, n_b, late)

        def finish(t):
            unit_copy(1, t, 0, buf.at[1]).wait_recv()
            out_tile(buf.at[1], t).start()

        loop(a0, tiles, finish)

    @pl.when(is_g)
    def _():
        lag_a = 6
        lag_b = jnp.where(x == 0, 6, 4)
        total = n_a + n_r + n_b
        give_from = n_a + EARLY + jnp.where(x == 0, 5, 3)
        use_lent = tiles - PER + EARLY + 9
        first_of_1 = lag_a + PER

        def u1_copy(i, where):
            return remote(u1, u1, hsend.at[3 + i], hrecv.at[1], where)

        def pass_u1():
            u1_copy(0, {"prow": prow - 1}).start()
            pl.when(jnp.logical_not(bottom))(lambda: u1_copy(1, {"prow": prow + 2}).start())

        def arrived_u1():
            u1_copy(0, {"prow": prow_x}).wait_recv()

        def apply_a(t):
            unit_copy(0, t, 1 - x, buf.at[0]).wait_recv()
            here = tile_of(t)
            low = times_upper(buf[0, here], us, 0)
            own[here] = (own[here].astype(F32) - dot(low, u0[...])).astype(BF)

        def apply_b(t, was_lent):
            @pl.when(was_lent)
            def _():
                for i in range(2):
                    arrived(1, row_of(t, x, i), lane_at(1, t, i))

            unit_copy(1, t, 1 - x, buf.at[1]).wait_recv()
            here = tile_of(t)
            own[here] = (own[here].astype(F32) - dot(buf[1, here], u1[...])).astype(BF)
            out_tile(own, t).start()

        def place(s):
            q = s - n_a
            spare = (q >= EARLY) & (q < EARLY + n_r)
            return spare, b0 + q - jnp.where(q >= EARLY + n_r, n_r, 0)

        def step(s):
            in_a = s < n_a
            spare, tb = place(s)
            in_r = jnp.logical_not(in_a) & spare
            ph = jnp.where(in_a, 0, 1)
            t = jnp.where(in_a, a0 + s, tb)

            def relay(i):
                @pl.when((s < total) & jnp.logical_not(in_r))
                def _():
                    p, sem = row_of(t, x, i), lane_at(ph, t, i)
                    arrived(ph, p, sem)
                    pl.when(far)(lambda: fwd_copy(ph, p, sem).start())
                    cross_copy(ph, t, p).start()

                @pl.when(in_r)
                def _():
                    k = s - n_a - EARLY
                    p, sem = spare_row(k, i), spare_at(2 * k + i)
                    arrived(1, p, sem)
                    pl.when(far)(lambda: fwd_copy(1, p, sem).start())
                    spare_cross_copy(k, i).start()
                    give_copy(k, i).start()

            relay(0)
            pl.when(s == jnp.where(r == 0, PER, lag_a))(take_head)
            pl.when(s == lag_a)(make_u0)
            ta = s - lag_a
            pl.when((ta >= 0) & (ta < n_a))(lambda: apply_a(a0 + ta))
            relay(1)

            @pl.when((prow == 1) & (s == first_of_1))
            def _():
                lower_times(1, own[pl.ds(0, width)], u1)

            pl.when((prow == 1) & (s == first_of_1 + 1))(pass_u1)
            pl.when((prow == 0) & (s == first_of_1 + 1))(lambda: out_first(u0).start())
            pl.when((prow == 1) & (s == first_of_1 + 1))(lambda: out_first(u1).start())

            @pl.when((r == 1) & (prow > 1) & (s == tiles - PER - 2))
            def _():
                arrived_u1()
                pass_u1()

            pl.when((r == 0) & (s == tiles - PER - 1))(arrived_u1)

            @pl.when(borrows & (s >= give_from) & (s < give_from + moved))
            def _():
                spare_unit_arrived(s - give_from)
                give_unit_copy(s - give_from).start()

            u = s - lag_b
            u_spare, u_tile = place(u)
            n_plain = jnp.where((u >= n_a) & (u < total) & jnp.logical_not(u_spare), 1, 0)
            n_lent = jnp.where(lends & (s >= use_lent) & (s < use_lent + moved), 1, 0)
            loop(
                1 - n_plain, 1 + n_lent,
                lambda k: apply_b(jnp.where(k == 0, u_tile, s - use_lent), k == 1),
            )

        loop(0, total + lag_b, step)

        @pl.when(r == 1)
        def _():
            u1_copy(0, {"prow": prow_x}).wait_send()
            pl.when(jnp.logical_not(bottom))(lambda: u1_copy(1, {"prow": prow_x}).wait_send())

    @pl.when(r == 0)
    def _():
        head_copy(0, {"prow": prow_x}).wait_send()
        pl.when(jnp.logical_not(bottom))(lambda: head_copy(1, {"prow": prow_x}).wait_send())

    pl.when(is_s1 & (prow == 0))(lambda: head_copy(2, {"pcol": pcol_x}).wait_send())
    if moved:
        pl.when(borrows & is_g)(lambda: sent(SIDE, 2 * moved))
        pl.when(lends & source)(lambda: sent(SIDE, moved))
    full = 2 * tiles
    ahead = (full - 2 * PER + moved, full - PER, full - moved, full)
    pl.when(far)(lambda: sent_by_prow(FWD, ahead))
    pl.when(is_g)(lambda: sent_by_prow(CROSS, ahead))
    pl.when(is_s0)(lambda: sent_by_prow(CROSS, (full - 2 * PER, full)))
    pl.when(is_s1)(lambda: sent_by_prow(CROSS, (tiles - PER, tiles)))
    pltpu.make_async_copy(own, out_ref, out_sem).wait()


def body(n_prow, n_pcol, matrix, u_inverse, l_inverse):
    rows, width = matrix.shape
    tile, unit, pkt, tiles, moved = sizes(rows, width, n_prow)
    square = (width, width)
    dma = pltpu.SemaphoreType.DMA
    operands = [
        pltpu.with_memory_space_constraint(a, pltpu.HBM) for a in (matrix, u_inverse, l_inverse)
    ]
    return pl.pallas_call(
        functools.partial(kernel, n_prow, n_pcol, width),
        out_shape=jax.ShapeDtypeStruct(matrix.shape, matrix.dtype),
        in_specs=[pl.BlockSpec(memory_space=pltpu.HBM)] * 3,
        out_specs=pl.BlockSpec(memory_space=pl.ANY),
        scratch_shapes=[
            pltpu.VMEM((rows, width), BF),
            pltpu.VMEM((2, rows + moved * tile, width), BF),
            pltpu.VMEM(square, BF),
            pltpu.VMEM((2,) + square, F32),
            pltpu.VMEM((2,) + square, F32),
            pltpu.VMEM((2, PIECES) + square, BF),
            pltpu.VMEM((2, PIECES) + square, BF),
            pltpu.VMEM(square, BF),
            pltpu.VMEM(square, BF),
            dma((4,)),
            dma((4 * tiles,)),
            dma((2 * tiles,)),
            dma((3,)),
            dma((2,)),
            dma((5,)),
            dma(()),
        ],
        compiler_params=pltpu.CompilerParams(
            collective_id=0, has_side_effects=True, vmem_limit_bytes=46 * 1024 * 1024
        ),
    )(*operands)


def solution(mesh):
    run = functools.partial(body, mesh.shape["prow"], mesh.shape["pcol"])
    in_specs = (P("prow", "pcol"), P(), P())
    out_specs = P("prow", "pcol")
    return jax.shard_map(run, mesh=mesh, in_specs=in_specs, out_specs=out_specs, check_vma=False)
```

```python
import functools

import jax
import jax.numpy as jnp
from jax import lax
from jax.experimental import pallas as pl
from jax.experimental.pallas import tpu as pltpu
from jax.sharding import PartitionSpec as P

MESH = pl.DeviceIdType.MESH
BF = jnp.bfloat16
F32 = jnp.float32
PIECES = 2
PER = 4
SPLIT = 4
EARLY = 8
MID = 16
HEAD_AT = 20


def sizes(rows, width, n_prow):
    tile = width // PER
    moved = 3 * PER // 2 if n_prow > 2 else 0
    return tile, tile // 2, tile // 2 // SPLIT, rows // tile, moved


def dot(a, b):
    return jnp.dot(a, b, preferred_element_type=F32)


def times_upper(a, u_ref, panel):
    half = a.shape[1] // 2
    left = sum(dot(a[:, :half], u_ref[panel, i, :half, :half]) for i in reversed(range(PIECES)))
    right = sum(dot(a, u_ref[panel, i, :, half:]) for i in reversed(range(PIECES)))
    return jnp.concatenate([left, right], 1).astype(BF)


def kernel(
    n_prow, n_pcol, width, m_ref, u_hbm, l_hbm, out_ref,
    own, buf, head, uf, lf, us, ls, u0, u1,
    load_sem, lane_sem, unit_sem, send_sem, hrecv, hsend, out_sem, credit,
):
    rows = own.shape[0]
    tile, unit, pkt, tiles, moved = sizes(rows, width, n_prow)
    n_pkt = rows // pkt
    end = tiles - 1
    half = width // 2
    prow, pcol = lax.axis_index("prow"), lax.axis_index("pcol")
    x, r = pcol % 2, prow % 2
    pcol_x, prow_x = pcol + 1 - 2 * x, prow + 1 - 2 * r
    is_s0, is_s1, is_g = pcol == 0, pcol == 1, pcol >= 2
    source, last = pcol < 2, pcol + 2 >= n_pcol
    top, bottom = prow < 2, prow + 2 >= n_prow
    far = jnp.logical_not(last)
    lends, borrows = (prow == 2) & (moved > 0), (prow == 0) & (moved > 0)

    a0 = jnp.where(prow == 0, PER, 0)
    n_a = tiles - a0
    n_r = jnp.where(borrows, moved, 0)
    b0 = jnp.where(top, PER, jnp.where(lends, moved, 0))
    n_b = tiles - b0

    def at(ph, p):
        return buf.at[ph, pl.ds(pl.multiple_of(p * pkt, pkt), pkt)]

    def m_at(p):
        return m_ref.at[pl.ds(pl.multiple_of(p * pkt, pkt), pkt)]

    def unit_of(t, lane):
        return pl.ds(pl.multiple_of((2 * t + lane) * unit, unit), unit)

    def tile_of(t):
        return pl.ds(pl.multiple_of(t * tile, tile), tile)

    def remote(src, dst, sem, recv_sem, where):
        return pltpu.make_async_remote_copy(
            src_ref=src, dst_ref=dst, send_sem=sem, recv_sem=recv_sem,
            device_id=where, device_id_type=MESH,
        )

    FWD, CROSS, SIDE = (send_sem.at[i] for i in range(3))

    def lane_at(slot, i):
        return lane_sem.at[SPLIT * slot + i]

    def unit_at(slot):
        return unit_sem.at[slot]

    def row_of(t, lane, i):
        return SPLIT * (2 * t + lane) + i

    def fwd_copy(ph, p, sem, src=None):
        ref = at(ph, p)
        return remote(ref if src is None else src, ref, FWD, sem, {"pcol": pcol + 2})

    def arrived(ph, p, sem):
        ref = at(ph, p)
        remote(ref, ref, FWD, sem, {"pcol": pcol_x}).wait_recv()

    def cross_copy(ph, p, sem):
        ref = at(ph, p)
        return remote(ref, ref, CROSS, sem, {"pcol": pcol_x})

    def unit_copy(t, lane, slot, dst, src=None):
        ref = dst.at[unit_of(t, lane)]
        return remote(ref if src is None else src, ref, CROSS, unit_at(slot), {"pcol": pcol_x})

    def spare_row(k, i):
        return n_pkt + row_of(k, x, i)

    def spare_at(j):
        return lane_sem.at[jnp.where(j < SPLIT * PER, j, SPLIT * (tiles + 1 - PER) + j)]

    def spare_unit_at(k):
        return unit_sem.at[jnp.where(k < PER, k, tiles + 1 - PER + k)]

    def lend_copy(k, i):
        return remote(at(1, row_of(k, x, i)), at(1, spare_row(k, i)), SIDE, spare_at(SPLIT * k + i), {"prow": prow - 2})

    def give_copy(k, i):
        return remote(at(1, spare_row(k, i)), at(1, row_of(k, x, i)), SIDE, lane_at(k, i), {"prow": prow + 2})

    def give_unit_copy(k):
        src, dst = buf.at[1, unit_of(tiles + k, 1 - x)], buf.at[1, unit_of(k, 1 - x)]
        return remote(src, dst, SIDE, unit_at(k), {"prow": prow + 2})

    def spare_unit_arrived(k):
        ref = buf.at[1, unit_of(tiles + k, 1 - x)]
        remote(ref, ref, CROSS, spare_unit_at(k), {"pcol": pcol_x}).wait_recv()

    Z, X, Y = (credit.at[i] for i in range(3))

    def allow(sem, where):
        pl.semaphore_signal(sem, inc=1, device_id=where, device_id_type=MESH)

    def allowed(sem):
        pl.semaphore_wait(sem, 1)

    def sent(sem, units):
        ref = buf.at[0, pl.ds(0, units * unit)]
        remote(ref, ref, sem, lane_at(0, 0), {"pcol": pcol_x}).wait_send()

    def sent_by_prow(sem, units):
        for k, n in enumerate(units):
            here = prow == k if k + 1 < len(units) else prow >= k
            pl.when(here)(functools.partial(sent, sem, n))

    def loop(lo, hi, step):
        def one(k, carry):
            step(k)
            return carry

        lax.fori_loop(lo, hi, one, 0)

    load_lane = pltpu.make_async_copy(m_ref, buf.at[0, pl.ds(0, rows)], load_sem.at[0])
    load_own = pltpu.make_async_copy(m_ref, own, load_sem.at[0])
    load_u = pltpu.make_async_copy(u_hbm, uf, load_sem.at[1])
    load_l = pltpu.make_async_copy(l_hbm, lf, load_sem.at[2])
    has_head = (prow == 0) & (pcol >= 1)
    load_head = pltpu.make_async_copy(m_ref.at[pl.ds(0, width)], head, load_sem.at[3])
    pl.when(has_head)(load_head.start)
    load_u.start()
    load_l.start()
    pl.when(is_s0)(load_lane.start)
    pl.when(jnp.logical_not(is_s0))(load_own.start)

    barrier = pltpu.get_barrier_semaphore()

    def greet(where):
        pl.semaphore_signal(barrier, inc=1, device_id=where, device_id_type=MESH)

    greet({"pcol": pcol_x})
    greet({"prow": prow_x})
    for ok, where in (
        (jnp.logical_not(source), {"pcol": pcol - 2}),
        (far, {"pcol": pcol + 2}),
        (jnp.logical_not(top), {"prow": prow - 2}),
        (jnp.logical_not(bottom), {"prow": prow + 2}),
    ):
        pl.when(ok)(functools.partial(greet, where))
    absent = [jnp.where(ok, 1, 0) for ok in (source, last, top, bottom)]
    pl.semaphore_wait(barrier, 6 - sum(absent))

    def head_copy(i, where, src=head):
        return remote(src, head, hsend.at[i], hrecv.at[0], where)

    def pass_head(src=head):
        head_copy(0, {"prow": prow + 1}, src).start()
        pl.when(jnp.logical_not(bottom))(lambda: head_copy(1, {"prow": prow + 2}, src).start())

    @pl.when(has_head)
    def _():
        first = m_ref.at[pl.ds(0, width)]
        pl.when(is_s1)(lambda: head_copy(2, {"pcol": pcol_x}, first).start())
        pass_head(first)

    @pl.when(is_s0)
    def _():
        def ahead(t, lane, slot):
            for i in range(SPLIT):
                p = row_of(t, lane, i)
                pl.when(far)(lambda: fwd_copy(0, p, lane_at(slot, i), m_at(p)).start())

        def across(t, lane, slot):
            for i in range(SPLIT):
                p = row_of(t, lane, i)
                remote(m_at(p), at(0, p), CROSS, lane_at(slot, i), {"pcol": pcol_x}).start()

        def send(t):
            ahead(t, 0, t)
            across(t, 1, t)

        loop(a0, tiles, send)
        ahead(end, 1, tiles)
        across(end, 0, tiles)

    @pl.when(is_s1)
    def _():
        def send(t, lane, slot):
            unit_copy(t, lane, slot, own, m_ref.at[unit_of(t, lane)]).start()

        loop(a0, tiles, lambda t: send(t, 0, t))
        send(end, 1, tiles)

    def split(src, dst, panel):
        rest = src[panel]
        for i in range(PIECES):
            piece = rest.astype(BF)
            dst[panel, i] = piece
            rest = rest - piece.astype(F32)

    load_u.wait()
    load_l.wait()
    split(lf, ls, 0)
    split(uf, us, 0)
    pl.when(source)(lambda: split(uf, us, 1))
    pl.when(is_g & (prow == 1))(lambda: split(lf, ls, 1))
    pl.when(is_s0)(load_lane.wait)
    pl.when(jnp.logical_not(is_s0))(load_own.wait)

    def lower_times(panel, value, out):
        upper = sum(dot(ls[panel, i, :half, :half], value[:half]) for i in reversed(range(PIECES)))
        out[:half] = upper.astype(BF)
        lower = sum(dot(ls[panel, i, half:], value) for i in reversed(range(PIECES)))
        out[half:] = lower.astype(BF)

    def take_head():
        pl.when(has_head)(load_head.wait)

        @pl.when(jnp.logical_not(has_head))
        def _():
            head_copy(0, {"prow": prow_x}).wait_recv()
            pl.when(r == 0)(pass_head)

    def make_u0():
        lower_times(0, head[...], u0)

    def out_tile(src, t):
        here = tile_of(t)
        return pltpu.make_async_copy(src.at[here], out_ref.at[here], out_sem)

    def out_first(src):
        return pltpu.make_async_copy(src, out_ref.at[pl.ds(0, width)], out_sem)

    def make_lower(t, low, lane):
        here = unit_of(t, lane)
        cur = (own[here].astype(F32) - dot(low, u0[...])).astype(BF)
        value = times_upper(cur, us, 1)
        buf[1, here] = jnp.where((prow == 1) & (t < PER), cur, value)

    def lend(t):
        @pl.when(lends & (t >= 0) & (t < moved))
        def _():
            for i in range(SPLIT):
                lend_copy(t, i).start()

    def borrow():
        @pl.when(borrows)
        def _():
            def one(k):
                for i in range(SPLIT):
                    p, sem = spare_row(k, i), spare_at(SPLIT * k + i)
                    arrived(1, p, sem)
                    pl.when(far)(lambda: fwd_copy(1, p, sem).start())

            loop(0, moved, one)

    def send_lower(t, lane, slot):
        pl.when(far & ((t == b0) | (t == MID)))(lambda: allowed(Z))
        for i in range(SPLIT):
            p = row_of(t, lane, i)
            pl.when(far & (t >= b0))(lambda: fwd_copy(1, p, lane_at(slot, i)).start())

    @pl.when(is_s0)
    def _():
        pl.when(prow == 0)(lambda: out_first(buf.at[0, pl.ds(0, width)]).start())

        def low_step(i):
            t = a0 + i
            here = tile_of(t)
            buf[0, here] = times_upper(buf[0, here], us, 0)
            out_tile(buf.at[0], t).start()
            pl.when(i == jnp.where(prow == 0, HEAD_AT, n_a - 1))(take_head)

        loop(0, n_a, low_step)
        make_u0()

        def make(t, lane, slot):
            unit_copy(t, lane, slot, own).wait_recv()
            make_lower(t, buf[0, unit_of(t, lane)], lane)

        def send(t):
            send_lower(t, 0, t)
            unit_copy(t, 0, t, buf.at[1]).start()

        def step(i):
            t = a0 + i
            make(t, 0, t)
            lend(t - 1)
            pl.when(i == EARLY + 1)(borrow)
            pl.when(i >= 1)(lambda: send(t - 1))

        loop(0, n_a, step)
        make(end, 1, tiles)
        send_lower(end, 0, end)
        send_lower(end, 1, tiles)

    @pl.when(is_s1)
    def _():
        lag = 8

        def relay(t):
            for i in range(SPLIT):
                p, sem = row_of(t, 1, i), lane_at(t, i)
                arrived(0, p, sem)
                pl.when(far)(lambda: fwd_copy(0, p, sem).start())

        def make(t, lane=1):
            make_lower(t, times_upper(buf[0, unit_of(t, lane)], us, 0), lane)
            lend(t - 1)

        def step(s):
            relay(a0 + s)
            pl.when(s == jnp.where(r == 0, PER, lag))(take_head)
            pl.when(s == lag)(make_u0)
            pl.when(s >= lag)(lambda: make(a0 + s - lag))

        loop(0, n_a - 1, step)
        pl.when(prow == 0)(lambda: out_first(u0).start())

        def late(i):
            pl.when(i == EARLY)(borrow)
            send_lower(b0 + i, 1, b0 + i)

            @pl.when(i <= lag + 1)
            def _():
                lane = jnp.where(i <= lag, 1, 0)

                @pl.when(i >= lag)
                def _():
                    for n in range(SPLIT):
                        arrived(0, row_of(end, lane, n), lane_at(tiles - lane, n))

                make(jnp.minimum(end - lag + i, end), lane)

        loop(0, n_b, late)
        send_lower(end, 0, tiles)
        out_tile(buf.at[1], end).start()

        def finish(t):
            unit_copy(t, 0, t, buf.at[1]).wait_recv()
            out_tile(buf.at[1], t).start()

        loop(a0, end, finish)

    @pl.when(is_g)
    def _():
        lag_a, lag_b = 6, 4
        n_ax = n_a + 1 - 2 * x
        total = n_ax + n_r + n_b + 1
        give_from = n_ax + EARLY + 3
        use_lent = tiles - PER + EARLY + 9
        first_of_1 = lag_a + PER

        def u1_copy(i, where):
            return remote(u1, u1, hsend.at[3 + i], hrecv.at[1], where)

        def pass_u1():
            u1_copy(0, {"prow": prow - 1}).start()
            pl.when(jnp.logical_not(bottom))(lambda: u1_copy(1, {"prow": prow + 2}).start())

        def arrived_u1():
            u1_copy(0, {"prow": prow_x}).wait_recv()

        def apply_a(t):
            pl.when((t < end) | (x == 1))(lambda: unit_copy(t, 1 - x, t, buf.at[0]).wait_recv())
            pl.when((t == end) & (x == 1))(lambda: unit_copy(t, x, tiles, buf.at[0]).wait_recv())
            here = tile_of(t)
            low = times_upper(buf[0, here], us, 0)
            own[here] = (own[here].astype(F32) - dot(low, u0[...])).astype(BF)

        def apply_b(t, was_lent):
            if was_lent:
                for i in range(SPLIT):
                    arrived(1, row_of(t, x, i), lane_at(t, i))

            pl.when(t < end)(lambda: unit_copy(t, 1 - x, t, buf.at[1]).wait_recv())
            here = tile_of(t)
            own[here] = (own[here].astype(F32) - dot(buf[1, here], u1[...])).astype(BF)
            out_tile(own, t).start()

        def place(s):
            q = s - n_ax
            return (q >= EARLY) & (q < EARLY + n_r), q - jnp.where(q >= EARLY + n_r, n_r, 0)

        def apply_plain(u):
            u_spare, n = place(u)
            plain = (u >= n_ax) & jnp.logical_not(u_spare) & (n != n_b - 1)
            pl.when(plain)(lambda: apply_b(jnp.where(n == n_b, end, b0 + n), False))

        def apply_lent(k):
            pl.when(lends & (k >= 0) & (k < moved))(lambda: apply_b(k, True))

        def step(s):
            in_a = s < n_ax
            spare, k = place(s)
            in_r = jnp.logical_not(in_a) & spare
            in_b = (s >= n_ax) & (s < total) & jnp.logical_not(spare)
            ph = jnp.where(in_a, 0, 1)
            other = jnp.where(in_a, s == n_a, k == n_b)
            t = jnp.where(other, end, jnp.where(in_a, a0 + s, b0 + k))
            slot = jnp.where(other, tiles, t)
            lane = jnp.where(other, 1 - x, x)

            pl.when(s == jnp.where(r == 0, PER, lag_a))(take_head)
            pl.when(s == lag_a)(make_u0)

            @pl.when(in_b & ((k == 0) | (t == MID)))
            def _():
                allowed(X)
                pl.when(far)(lambda: allowed(Z))

            pl.when(borrows & (s == n_ax + EARLY))(lambda: allowed(Y))
            ta = s - lag_a

            def micro(i):
                @pl.when((s < total) & jnp.logical_not(in_r))
                def _():
                    p, sem = row_of(t, lane, i), lane_at(slot, i)
                    arrived(ph, p, sem)
                    pl.when(far)(lambda: fwd_copy(ph, p, sem).start())
                    pl.when(in_a | (t < end))(lambda: cross_copy(ph, p, unit_at(slot)).start())

                @pl.when(in_r)
                def _():
                    n = s - n_ax - EARLY
                    p, sem = spare_row(n, i), spare_at(SPLIT * n + i)
                    arrived(1, p, sem)
                    pl.when(far)(lambda: fwd_copy(1, p, sem).start())
                    cross_copy(1, p, spare_unit_at(n)).start()
                    give_copy(n, i).start()

                pl.when((i == 1) & (ta >= 0) & (ta < n_a))(lambda: apply_a(a0 + ta))
                pl.when(i == SPLIT - 1)(lambda: apply_plain(s - lag_b))
                pl.when(i == 1)(lambda: apply_lent(s - use_lent))

            loop(0, SPLIT, micro)

            pl.when((s == MID - 1 - a0) | (s == n_ax - 1))(lambda: allow(Z, {"pcol": pcol - 2}))
            pl.when((ta == MID - 1 - a0) | (ta == n_a - 1))(lambda: allow(X, {"pcol": pcol_x}))
            pl.when(lends & (ta == MID - 1 - a0))(lambda: allow(Y, {"prow": prow - 2}))

            @pl.when((prow == 1) & (s == first_of_1))
            def _():
                lower_times(1, own[pl.ds(0, width)], u1)

            pl.when((prow == 1) & (s == first_of_1 + 1))(pass_u1)
            pl.when((prow == 0) & (s == first_of_1 + 1))(lambda: out_first(u0).start())
            pl.when((prow == 1) & (s == first_of_1 + 1))(lambda: out_first(u1).start())

            @pl.when((r == 1) & (prow > 1) & (s == tiles - PER - 2))
            def _():
                arrived_u1()
                pass_u1()

            pl.when((r == 0) & (s == tiles - PER - 1))(arrived_u1)

            @pl.when(borrows & (s >= give_from) & (s < give_from + moved))
            def _():
                spare_unit_arrived(s - give_from)
                give_unit_copy(s - give_from).start()

        loop(0, total, step)
        loop(total - lag_b, total, apply_plain)

        @pl.when(r == 1)
        def _():
            u1_copy(0, {"prow": prow_x}).wait_send()
            pl.when(jnp.logical_not(bottom))(lambda: u1_copy(1, {"prow": prow_x}).wait_send())

    @pl.when(r == 0)
    def _():
        head_copy(0, {"prow": prow_x}).wait_send()
        pl.when(jnp.logical_not(bottom))(lambda: head_copy(1, {"prow": prow_x}).wait_send())

    pl.when(is_s1 & (prow == 0))(lambda: head_copy(2, {"pcol": pcol_x}).wait_send())
    if moved:
        pl.when(borrows & is_g)(lambda: sent(SIDE, 2 * moved))
        pl.when(lends & source)(lambda: sent(SIDE, moved))
    full = 2 * tiles
    base = (full - 2 * PER + moved, full - PER, full - moved, full)
    more, less = [n + 2 for n in base], [n - 2 for n in base]
    pl.when(far & (x == 0))(lambda: sent_by_prow(FWD, more))
    pl.when(far & (x == 1))(lambda: sent_by_prow(FWD, base))
    pl.when(is_g & (x == 0))(lambda: sent_by_prow(CROSS, base))
    pl.when(is_g & (x == 1))(lambda: sent_by_prow(CROSS, less))
    pl.when(is_s0)(lambda: sent_by_prow(CROSS, (full - 2 * PER, full)))
    pl.when(is_s1)(lambda: sent_by_prow(CROSS, (tiles - PER + 1, tiles + 1)))
    pltpu.make_async_copy(own, out_ref, out_sem).wait()


def body(n_prow, n_pcol, matrix, u_inverse, l_inverse):
    rows, width = matrix.shape
    tile, unit, pkt, tiles, moved = sizes(rows, width, n_prow)
    square = (width, width)
    dma = pltpu.SemaphoreType.DMA
    operands = [
        pltpu.with_memory_space_constraint(a, pltpu.HBM) for a in (matrix, u_inverse, l_inverse)
    ]
    return pl.pallas_call(
        functools.partial(kernel, n_prow, n_pcol, width),
        out_shape=jax.ShapeDtypeStruct(matrix.shape, matrix.dtype),
        in_specs=[pl.BlockSpec(memory_space=pltpu.HBM)] * 3,
        out_specs=pl.BlockSpec(memory_space=pl.ANY),
        scratch_shapes=[
            pltpu.VMEM((rows, width), BF),
            pltpu.VMEM((2, rows + max(moved, 1) * tile, width), BF),
            pltpu.VMEM(square, BF),
            pltpu.VMEM((2,) + square, F32),
            pltpu.VMEM((2,) + square, F32),
            pltpu.VMEM((2, PIECES) + square, BF),
            pltpu.VMEM((2, PIECES) + square, BF),
            pltpu.VMEM(square, BF),
            pltpu.VMEM(square, BF),
            dma((4,)),
            dma((SPLIT * (tiles + 1 + max(moved - PER, 0)),)),
            dma((tiles + 1 + max(moved - PER, 0),)),
            dma((3,)),
            dma((2,)),
            dma((5,)),
            dma(()),
            pltpu.SemaphoreType.REGULAR((3,)),
        ],
        compiler_params=pltpu.CompilerParams(
            collective_id=0, has_side_effects=True, vmem_limit_bytes=46 * 1024 * 1024
        ),
    )(*operands)


def solution(mesh):
    run = functools.partial(body, mesh.shape["prow"], mesh.shape["pcol"])
    in_specs = (P("prow", "pcol"), P(), P())
    out_specs = P("prow", "pcol")
    return jax.shard_map(run, mesh=mesh, in_specs=in_specs, out_specs=out_specs, check_vma=False)
```

```python
import functools

import jax
import jax.numpy as jnp
from jax import lax
from jax.experimental import pallas as pl
from jax.experimental.pallas import tpu as pltpu
from jax.sharding import PartitionSpec as P

MESH = pl.DeviceIdType.MESH
BF = jnp.bfloat16
F32 = jnp.float32
PIECES = 2
PER = 4
SPLIT = 4
EARLY = 8
MID = 16
HEAD_AT = 20
TAIL = 4


def sizes(rows, width, n_prow):
    tile = width // PER
    moved = (PER, PER // 2) if n_prow > 2 else (0, 0)
    return tile, tile // 2, tile // 2 // SPLIT, rows // tile, moved


def dot(a, b):
    return jnp.dot(a, b, preferred_element_type=F32)


def times_upper(a, u_ref, panel):
    half = a.shape[1] // 2
    left = sum(dot(a[:, :half], u_ref[panel, i, :half, :half]) for i in reversed(range(PIECES)))
    right = sum(dot(a, u_ref[panel, i, :, half:]) for i in reversed(range(PIECES)))
    return jnp.concatenate([left, right], 1).astype(BF)


def kernel(
    n_prow, n_pcol, width, m_ref, u_hbm, l_hbm, out_ref, cur_ref, low_ref, up_ref,
    own, buf, head, uf, lf, us, ls, u0, u1,
    load_sem, lane_sem, unit_sem, lend_sem, send_sem, hrecv, hsend, out_sem, tail_sem, credit,
):
    rows = own.shape[0]
    tile, unit, pkt, tiles, moved = sizes(rows, width, n_prow)
    n_pkt = rows // pkt
    end = tiles - 1
    half = width // 2
    prow, pcol = lax.axis_index("prow"), lax.axis_index("pcol")
    x, r = pcol % 2, prow % 2
    pcol_x, prow_x = pcol + 1 - 2 * x, prow + 1 - 2 * r
    is_s0, is_s1, is_g = pcol == 0, pcol == 1, pcol >= 2
    source, last = pcol < 2, pcol + 2 >= n_pcol
    top, bottom = prow < 2, prow + 2 >= n_prow
    far = jnp.logical_not(last)
    mine = jnp.where(r == 0, moved[0], moved[1])
    lends, borrows = (prow >= 2) & (prow < 4) & (mine > 0), top & (mine > 0)

    a0 = jnp.where(prow == 0, PER, 0)
    n_a = tiles - a0
    n_r = jnp.where(borrows, mine, 0)
    b0 = jnp.where(top, PER, jnp.where(lends, mine, 0))
    n_b = tiles - b0

    def at(ph, p):
        return buf.at[ph, pl.ds(pl.multiple_of(p * pkt, pkt), pkt)]

    def m_at(p):
        return m_ref.at[pl.ds(pl.multiple_of(p * pkt, pkt), pkt)]

    def unit_of(t, lane):
        return pl.ds(pl.multiple_of((2 * t + lane) * unit, unit), unit)

    def tile_of(t):
        return pl.ds(pl.multiple_of(t * tile, tile), tile)

    def remote(src, dst, sem, recv_sem, where):
        return pltpu.make_async_remote_copy(
            src_ref=src, dst_ref=dst, send_sem=sem, recv_sem=recv_sem,
            device_id=where, device_id_type=MESH,
        )

    FWD, CROSS, SIDE = (send_sem.at[i] for i in range(3))

    def lane_at(slot, i):
        return lane_sem.at[SPLIT * slot + i]

    def unit_at(slot):
        return unit_sem.at[slot]

    def row_of(t, lane, i):
        return SPLIT * (2 * t + lane) + i

    def fwd_copy(ph, p, sem, src=None):
        ref = at(ph, p)
        return remote(ref if src is None else src, ref, FWD, sem, {"pcol": pcol + 2})

    def arrived(ph, p, sem):
        ref = at(ph, p)
        remote(ref, ref, FWD, sem, {"pcol": pcol_x}).wait_recv()

    def cross_copy(ph, p, sem):
        ref = at(ph, p)
        return remote(ref, ref, CROSS, sem, {"pcol": pcol_x})

    def unit_copy(t, lane, slot, dst, src=None):
        ref = dst.at[unit_of(t, lane)]
        return remote(ref if src is None else src, ref, CROSS, unit_at(slot), {"pcol": pcol_x})

    def spare_row(k, i):
        return n_pkt + row_of(k, x, i)

    def lend_copy(k):
        src, dst = buf.at[1, unit_of(k, x)], buf.at[1, unit_of(tiles + k, x)]
        return remote(src, dst, SIDE, lend_sem.at[k], {"prow": prow - 2})

    def give_copy(k, i):
        return remote(at(1, spare_row(k, i)), at(1, row_of(k, x, i)), SIDE, lane_at(k, i), {"prow": prow + 2})

    def give_unit_copy(k):
        src, dst = buf.at[1, unit_of(tiles + k, 1 - x)], buf.at[1, unit_of(k, 1 - x)]
        return remote(src, dst, SIDE, unit_at(k), {"prow": prow + 2})

    def spare_unit_arrived(k):
        ref = buf.at[1, unit_of(tiles + k, 1 - x)]
        remote(ref, ref, CROSS, unit_at(k), {"pcol": pcol_x}).wait_recv()

    Z, X, Y = (credit.at[i] for i in range(3))

    def allow(sem, where):
        pl.semaphore_signal(sem, inc=1, device_id=where, device_id_type=MESH)

    def allowed(sem):
        pl.semaphore_wait(sem, 1)

    def sent(sem, units):
        ref = buf.at[0, pl.ds(0, units * unit)]
        remote(ref, ref, sem, lane_at(0, 0), {"pcol": pcol_x}).wait_send()

    def sent_by_prow(sem, units):
        for k, n in enumerate(units):
            here = prow == k if k + 1 < len(units) else prow >= k
            pl.when(here)(functools.partial(sent, sem, n))

    def loop(lo, hi, step):
        def one(k, carry):
            step(k)
            return carry

        lax.fori_loop(lo, hi, one, 0)

    load_lane = pltpu.make_async_copy(m_ref, buf.at[0, pl.ds(0, rows)], load_sem.at[0])
    load_own = pltpu.make_async_copy(m_ref, own, load_sem.at[0])
    load_u = pltpu.make_async_copy(u_hbm, uf, load_sem.at[1])
    load_l = pltpu.make_async_copy(l_hbm, lf, load_sem.at[2])
    has_head = (prow == 0) & (pcol >= 1)
    load_head = pltpu.make_async_copy(m_ref.at[pl.ds(0, width)], head, load_sem.at[3])
    pl.when(has_head)(load_head.start)
    load_u.start()
    load_l.start()
    pl.when(is_s0)(load_lane.start)
    pl.when(jnp.logical_not(is_s0))(load_own.start)

    barrier = pltpu.get_barrier_semaphore()

    def greet(where):
        pl.semaphore_signal(barrier, inc=1, device_id=where, device_id_type=MESH)

    greet({"pcol": pcol_x})
    greet({"prow": prow_x})
    for ok, where in (
        (jnp.logical_not(source), {"pcol": pcol - 2}),
        (far, {"pcol": pcol + 2}),
        (jnp.logical_not(top), {"prow": prow - 2}),
        (jnp.logical_not(bottom), {"prow": prow + 2}),
    ):
        pl.when(ok)(functools.partial(greet, where))
    absent = [jnp.where(ok, 1, 0) for ok in (source, last, top, bottom)]
    pl.semaphore_wait(barrier, 6 - sum(absent))

    def head_copy(i, where, src=head):
        return remote(src, head, hsend.at[i], hrecv.at[0], where)

    def pass_head(src=head):
        head_copy(0, {"prow": prow + 1}, src).start()
        pl.when(jnp.logical_not(bottom))(lambda: head_copy(1, {"prow": prow + 2}, src).start())

    @pl.when(has_head)
    def _():
        first = m_ref.at[pl.ds(0, width)]
        pl.when(is_s1)(lambda: head_copy(2, {"pcol": pcol_x}, first).start())
        pass_head(first)

    @pl.when(is_s0)
    def _():
        def ahead(t, lane, slot):
            for i in range(SPLIT):
                p = row_of(t, lane, i)
                pl.when(far)(lambda: fwd_copy(0, p, lane_at(slot, i), m_at(p)).start())

        def across(t, lane, slot):
            for i in range(SPLIT):
                p = row_of(t, lane, i)
                remote(m_at(p), at(0, p), CROSS, lane_at(slot, i), {"pcol": pcol_x}).start()

        def send(t):
            ahead(t, 0, t)
            across(t, 1, t)

        loop(a0, tiles, send)
        ahead(end, 1, tiles)
        across(end, 0, tiles)

    @pl.when(is_s1)
    def _():
        def send(t, lane, slot):
            unit_copy(t, lane, slot, own, m_ref.at[unit_of(t, lane)]).start()

        loop(a0, tiles, lambda t: send(t, 0, t))
        send(end, 1, tiles)

    def split(src, dst, panel):
        rest = src[panel]
        for i in range(PIECES):
            piece = rest.astype(BF)
            dst[panel, i] = piece
            rest = rest - piece.astype(F32)

    load_u.wait()
    load_l.wait()
    split(lf, ls, 0)
    split(uf, us, 0)
    pl.when(source)(lambda: split(uf, us, 1))
    pl.when(is_g & (prow == 1))(lambda: split(lf, ls, 1))
    pl.when(is_s0)(load_lane.wait)
    pl.when(jnp.logical_not(is_s0))(load_own.wait)

    def lower_times(panel, value, out):
        upper = sum(dot(ls[panel, i, :half, :half], value[:half]) for i in reversed(range(PIECES)))
        out[:half] = upper.astype(BF)
        lower = sum(dot(ls[panel, i, half:], value) for i in reversed(range(PIECES)))
        out[half:] = lower.astype(BF)

    def take_head():
        pl.when(has_head)(load_head.wait)

        @pl.when(jnp.logical_not(has_head))
        def _():
            head_copy(0, {"prow": prow_x}).wait_recv()
            pl.when(r == 0)(pass_head)

    def make_u0():
        lower_times(0, head[...], u0)

    def out_tile(src, t):
        here = tile_of(t)
        return pltpu.make_async_copy(src.at[here], out_ref.at[here], out_sem)

    def out_first(src):
        return pltpu.make_async_copy(src, out_ref.at[pl.ds(0, width)], out_sem)

    def make_lower(t, low, lane):
        here = unit_of(t, lane)
        cur = (own[here].astype(F32) - dot(low, u0[...])).astype(BF)
        value = times_upper(cur, us, 1)
        buf[1, here] = jnp.where((prow == 1) & (t < PER), cur, value)

    def lend(t):
        pl.when(lends & (t >= 0) & (t < mine))(lambda: lend_copy(t).start())

    def borrow():
        @pl.when(borrows)
        def _():
            def one(k):
                lend_copy(k).wait_recv()
                for i in range(SPLIT):
                    pl.when(far)(lambda: fwd_copy(1, spare_row(k, i), lane_at(k, i)).start())

            loop(0, mine, one)

    def send_lower(t, lane, slot):
        pl.when(far & ((t == b0) | (t == MID)))(lambda: allowed(Z))
        for i in range(SPLIT):
            p = row_of(t, lane, i)
            pl.when(far & (t >= b0))(lambda: fwd_copy(1, p, lane_at(slot, i)).start())

    @pl.when(is_s0)
    def _():
        pl.when(prow == 0)(lambda: out_first(buf.at[0, pl.ds(0, width)]).start())

        def low_step(i):
            t = a0 + i
            here = tile_of(t)
            buf[0, here] = times_upper(buf[0, here], us, 0)
            out_tile(buf.at[0], t).start()
            pl.when(i == jnp.where(prow == 0, HEAD_AT, n_a - 1))(take_head)

        loop(0, n_a, low_step)
        make_u0()

        def make(t, lane, slot):
            unit_copy(t, lane, slot, own).wait_recv()
            make_lower(t, buf[0, unit_of(t, lane)], lane)

        def send(t):
            send_lower(t, 0, t)
            unit_copy(t, 0, t, buf.at[1]).start()

        def step(i):
            t = a0 + i
            make(t, 0, t)
            lend(t - 1)
            pl.when(i == EARLY + 1 + b0 - a0)(borrow)
            pl.when(i >= 1)(lambda: send(t - 1))

        loop(0, n_a, step)
        make(end, 1, tiles)
        send_lower(end, 0, end)
        send_lower(end, 1, tiles)

    @pl.when(is_s1)
    def _():
        lag = 8

        def relay(t):
            for i in range(SPLIT):
                p, sem = row_of(t, 1, i), lane_at(t, i)
                arrived(0, p, sem)
                pl.when(far)(lambda: fwd_copy(0, p, sem).start())

        def make(t, lane=1):
            make_lower(t, times_upper(buf[0, unit_of(t, lane)], us, 0), lane)
            lend(t - 1)

        def step(s):
            relay(a0 + s)
            pl.when(s == jnp.where(r == 0, PER, lag))(take_head)
            pl.when(s == lag)(make_u0)
            pl.when(s >= lag)(lambda: make(a0 + s - lag))

        loop(0, n_a - 1, step)
        pl.when(prow == 0)(lambda: out_first(u0).start())

        def late(i):
            pl.when(i == EARLY)(borrow)
            send_lower(b0 + i, 1, b0 + i)

            @pl.when(i <= lag + 1)
            def _():
                lane = jnp.where(i <= lag, 1, 0)

                @pl.when(i >= lag)
                def _():
                    for n in range(SPLIT):
                        arrived(0, row_of(end, lane, n), lane_at(tiles - lane, n))

                make(jnp.minimum(end - lag + i, end), lane)

        loop(0, n_b, late)
        send_lower(end, 0, tiles)
        out_tile(buf.at[1], end).start()

        def finish(t):
            unit_copy(t, 0, t, buf.at[1]).wait_recv()
            out_tile(buf.at[1], t).start()

        loop(a0, end, finish)

    @pl.when(is_g)
    def _():
        lag_a, lag_b = 6, 4
        n_ax = n_a + 1 - 2 * x
        total = n_ax + n_r + n_b + 1
        give_from = n_ax + EARLY + 3
        use_lent = tiles - PER + EARLY + jnp.where(r == 0, 9, 14)
        first_of_1 = lag_a + PER

        def u1_copy(i, where):
            return remote(u1, u1, hsend.at[3 + i], hrecv.at[1], where)

        def pass_u1():
            u1_copy(0, {"prow": prow - 1}).start()
            pl.when(jnp.logical_not(bottom))(lambda: u1_copy(1, {"prow": prow + 2}).start())

        def arrived_u1():
            u1_copy(0, {"prow": prow_x}).wait_recv()

        tail = tiles - TAIL

        def to_tail(src, dst, t, i):
            return pltpu.make_async_copy(src, dst.at[tile_of(t - tail)], tail_sem.at[i])

        def save_u1():
            pltpu.make_async_copy(u1, up_ref, tail_sem.at[2]).start()

        def apply_a(t):
            pl.when((t < end) | (x == 1))(lambda: unit_copy(t, 1 - x, t, buf.at[0]).wait_recv())
            pl.when((t == end) & (x == 1))(lambda: unit_copy(t, x, tiles, buf.at[0]).wait_recv())
            here = tile_of(t)
            low = times_upper(buf[0, here], us, 0)
            own[here] = (own[here].astype(F32) - dot(low, u0[...])).astype(BF)
            pl.when(t >= tail)(lambda: to_tail(own.at[here], cur_ref, t, 0).start())

        def apply_b(t, was_lent):
            if was_lent:
                for i in range(SPLIT):
                    arrived(1, row_of(t, x, i), lane_at(t, i))

            pl.when(t < end)(lambda: unit_copy(t, 1 - x, t, buf.at[1]).wait_recv())
            here = tile_of(t)

            @pl.when(t < tail)
            def _():
                own[here] = (own[here].astype(F32) - dot(buf[1, here], u1[...])).astype(BF)
                out_tile(own, t).start()

            pl.when(t >= tail)(lambda: to_tail(buf.at[1, here], low_ref, t, 1).start())

        def place(s):
            q = s - n_ax
            return (q >= EARLY) & (q < EARLY + n_r), q - jnp.where(q >= EARLY + n_r, n_r, 0)

        def apply_plain(u):
            u_spare, n = place(u)
            plain = (u >= n_ax) & jnp.logical_not(u_spare) & (n != n_b - 1)
            pl.when(plain)(lambda: apply_b(jnp.where(n == n_b, end, b0 + n), False))

        def apply_lent(k):
            pl.when(lends & (k >= 0) & (k < mine))(lambda: apply_b(k, True))

        def step(s):
            in_a = s < n_ax
            spare, k = place(s)
            in_r = jnp.logical_not(in_a) & spare
            in_b = (s >= n_ax) & (s < total) & jnp.logical_not(spare)
            ph = jnp.where(in_a, 0, 1)
            other = jnp.where(in_a, s == n_a, k == n_b)
            t = jnp.where(other, end, jnp.where(in_a, a0 + s, b0 + k))
            slot = jnp.where(other, tiles, t)
            lane = jnp.where(other, 1 - x, x)

            pl.when(s == jnp.where(r == 0, PER, lag_a))(take_head)
            pl.when(s == lag_a)(make_u0)

            @pl.when(in_b & ((k == 0) | (t == MID)))
            def _():
                allowed(X)
                pl.when(far)(lambda: allowed(Z))

            pl.when(borrows & (s == n_ax + EARLY))(lambda: allowed(Y))
            ta = s - lag_a

            def micro(i):
                @pl.when((s < total) & jnp.logical_not(in_r))
                def _():
                    p, sem = row_of(t, lane, i), lane_at(slot, i)
                    arrived(ph, p, sem)
                    pl.when(far)(lambda: fwd_copy(ph, p, sem).start())
                    pl.when(in_a | (t < end))(lambda: cross_copy(ph, p, unit_at(slot)).start())

                @pl.when(in_r)
                def _():
                    n = s - n_ax - EARLY
                    p, sem = spare_row(n, i), lane_at(n, i)
                    arrived(1, p, sem)
                    pl.when(far)(lambda: fwd_copy(1, p, sem).start())
                    cross_copy(1, p, unit_at(n)).start()
                    give_copy(n, i).start()

                pl.when((i == 1) & (ta >= 0) & (ta < n_a))(lambda: apply_a(a0 + ta))
                pl.when(i == SPLIT - 1)(lambda: apply_plain(s - lag_b))
                pl.when(i == 1)(lambda: apply_lent(s - use_lent))

            loop(0, SPLIT, micro)

            pl.when((s == MID - 1 - a0) | (s == n_ax - 1))(lambda: allow(Z, {"pcol": pcol - 2}))
            pl.when((ta == MID - 1 - a0) | (ta == n_a - 1))(lambda: allow(X, {"pcol": pcol_x}))
            pl.when(lends & (ta == MID - 1 - a0))(lambda: allow(Y, {"prow": prow - 2}))

            @pl.when((prow == 1) & (s == first_of_1))
            def _():
                lower_times(1, own[pl.ds(0, width)], u1)

            pl.when((prow == 1) & (s == first_of_1 + 1))(pass_u1)
            pl.when(s == tiles - PER)(save_u1)
            pl.when((prow == 0) & (s == first_of_1 + 1))(lambda: out_first(u0).start())
            pl.when((prow == 1) & (s == first_of_1 + 1))(lambda: out_first(u1).start())

            @pl.when((r == 1) & (prow > 1) & (s == tiles - PER - 2))
            def _():
                arrived_u1()
                pass_u1()

            pl.when((r == 0) & (s == tiles - PER - 1))(arrived_u1)

            @pl.when(borrows & (s >= give_from) & (s < give_from + mine))
            def _():
                spare_unit_arrived(s - give_from)
                give_unit_copy(s - give_from).start()

        loop(0, total, step)
        loop(total - lag_b, total, apply_plain)

        for i, (src, dst) in enumerate(((own, cur_ref), (own, low_ref), (u1, up_ref))):
            pltpu.make_async_copy(src.at[pl.ds(0, dst.shape[0])], dst, tail_sem.at[i]).wait()
        done = pl.ds(0, tail * tile)
        pltpu.make_async_copy(own.at[done], out_ref.at[done], out_sem).wait()

        @pl.when(r == 1)
        def _():
            u1_copy(0, {"prow": prow_x}).wait_send()
            pl.when(jnp.logical_not(bottom))(lambda: u1_copy(1, {"prow": prow_x}).wait_send())

    @pl.when(r == 0)
    def _():
        head_copy(0, {"prow": prow_x}).wait_send()
        pl.when(jnp.logical_not(bottom))(lambda: head_copy(1, {"prow": prow_x}).wait_send())

    pl.when(is_s1 & (prow == 0))(lambda: head_copy(2, {"pcol": pcol_x}).wait_send())
    for k, n in enumerate(moved):
        if n:
            pl.when(is_g & (prow == k))(functools.partial(sent, SIDE, 2 * n))
            pl.when(source & (prow == k + 2))(functools.partial(sent, SIDE, n))
    full = 2 * tiles
    base = [full - 2 * PER + moved[0], full - PER + moved[1], full - moved[0], full - moved[1], full]
    more, less = [n + 2 for n in base], [n - 2 for n in base]
    pl.when(far & (x == 0))(lambda: sent_by_prow(FWD, more))
    pl.when(far & (x == 1))(lambda: sent_by_prow(FWD, base))
    pl.when(is_g & (x == 0))(lambda: sent_by_prow(CROSS, base))
    pl.when(is_g & (x == 1))(lambda: sent_by_prow(CROSS, less))
    pl.when(is_s0)(lambda: sent_by_prow(CROSS, (full - 2 * PER, full)))
    pl.when(is_s1)(lambda: sent_by_prow(CROSS, (tiles - PER + 1, tiles + 1)))
    pl.when(source)(lambda: pltpu.make_async_copy(own, out_ref, out_sem).wait())


def finish(main_ref, cur_ref, low_ref, up_ref, out_ref, res, sem):
    pcol = lax.axis_index("pcol")
    rows, late = main_ref.shape[0], cur_ref.shape[0]
    done = pl.ds(0, rows - late)
    rest = pl.ds(rows - late, late)
    bulk = pltpu.make_async_copy(main_ref.at[done], out_ref.at[done], sem.at[0])
    bulk.start()
    through = pltpu.make_async_copy(main_ref.at[rest], out_ref.at[rest], sem.at[1])
    made = pltpu.make_async_copy(res, out_ref.at[rest], sem.at[1])
    pl.when(pcol < 2)(through.start)

    @pl.when(pcol >= 2)
    def _():
        res[...] = (cur_ref[...].astype(F32) - dot(low_ref[...], up_ref[...])).astype(BF)
        made.start()

    bulk.wait()
    made.wait()


def body(n_prow, n_pcol, matrix, u_inverse, l_inverse):
    rows, width = matrix.shape
    tile, unit, pkt, tiles, moved = sizes(rows, width, n_prow)
    square = (width, width)
    dma = pltpu.SemaphoreType.DMA
    operands = [
        pltpu.with_memory_space_constraint(a, pltpu.HBM) for a in (matrix, u_inverse, l_inverse)
    ]
    tail = (TAIL * tile, width)
    pieces = pl.pallas_call(
        functools.partial(kernel, n_prow, n_pcol, width),
        out_shape=[jax.ShapeDtypeStruct(shape, BF) for shape in (matrix.shape, tail, tail, square)],
        in_specs=[pl.BlockSpec(memory_space=pltpu.HBM)] * 3,
        out_specs=[pl.BlockSpec(memory_space=pl.ANY)] * 4,
        scratch_shapes=[
            pltpu.VMEM((rows, width), BF),
            pltpu.VMEM((2, rows + PER * tile, width), BF),
            pltpu.VMEM(square, BF),
            pltpu.VMEM((2,) + square, F32),
            pltpu.VMEM((2,) + square, F32),
            pltpu.VMEM((2, PIECES) + square, BF),
            pltpu.VMEM((2, PIECES) + square, BF),
            pltpu.VMEM(square, BF),
            pltpu.VMEM(square, BF),
            dma((4,)),
            dma((SPLIT * (tiles + 1),)),
            dma((tiles + 1,)),
            dma((PER,)),
            dma((3,)),
            dma((2,)),
            dma((5,)),
            dma(()),
            dma((3,)),
            pltpu.SemaphoreType.REGULAR((3,)),
        ],
        compiler_params=pltpu.CompilerParams(
            collective_id=0, has_side_effects=True, vmem_limit_bytes=46 * 1024 * 1024
        ),
    )(*operands)
    return pl.pallas_call(
        finish,
        out_shape=jax.ShapeDtypeStruct(matrix.shape, BF),
        in_specs=[pl.BlockSpec(memory_space=pl.ANY)] + [pl.BlockSpec(memory_space=pltpu.VMEM)] * 3,
        out_specs=pl.BlockSpec(memory_space=pl.ANY),
        scratch_shapes=[pltpu.VMEM(tail, BF), dma((2,))],
        compiler_params=pltpu.CompilerParams(vmem_limit_bytes=8 * 1024 * 1024),
    )(*pieces)


def solution(mesh):
    run = functools.partial(body, mesh.shape["prow"], mesh.shape["pcol"])
    in_specs = (P("prow", "pcol"), P(), P())
    out_specs = P("prow", "pcol")
    return jax.shard_map(run, mesh=mesh, in_specs=in_specs, out_specs=out_specs, check_vma=False)
```

```python
import functools

import jax
import jax.numpy as jnp
from jax import lax
from jax.experimental import pallas as pl
from jax.experimental.pallas import tpu as pltpu
from jax.sharding import PartitionSpec as P

MESH = pl.DeviceIdType.MESH
BF = jnp.bfloat16
F32 = jnp.float32
PIECES = 2
PER = 4
SPLIT = 4
EARLY = 8
MID = 16
HEAD_AT = 20
TAIL = 4


def sizes(rows, width, n_prow):
    tile = width // PER
    moved = (PER, PER // 2) if n_prow > 2 else (0, 0)
    return tile, tile // 2, tile // 2 // SPLIT, rows // tile, moved


def dot(a, b):
    return jnp.dot(a, b, preferred_element_type=F32)


def times_upper(a, u_ref, panel):
    half = a.shape[1] // 2
    left = sum(dot(a[:, :half], u_ref[panel, i, :half, :half]) for i in reversed(range(PIECES)))
    right = sum(dot(a, u_ref[panel, i, :, half:]) for i in reversed(range(PIECES)))
    return jnp.concatenate([left, right], 1).astype(BF)


def kernel(
    n_prow, n_pcol, width, m_ref, u_hbm, l_hbm, own, buf, u1,
    head, uf, lf, us, ls, u0,
    load_sem, lane_sem, unit_sem, lend_sem, send_sem, hrecv, hsend, credit,
):
    rows = own.shape[0]
    tile, unit, pkt, tiles, moved = sizes(rows, width, n_prow)
    n_pkt = rows // pkt
    end = tiles - 1
    half = width // 2
    prow, pcol = lax.axis_index("prow"), lax.axis_index("pcol")
    x, r = pcol % 2, prow % 2
    pcol_x, prow_x = pcol + 1 - 2 * x, prow + 1 - 2 * r
    is_s0, is_s1, is_g = pcol == 0, pcol == 1, pcol >= 2
    source, last = pcol < 2, pcol + 2 >= n_pcol
    top, bottom = prow < 2, prow + 2 >= n_prow
    far = jnp.logical_not(last)
    mine = jnp.where(r == 0, moved[0], moved[1])
    lends, borrows = (prow >= 2) & (prow < 4) & (mine > 0), top & (mine > 0)

    a0 = jnp.where(prow == 0, PER, 0)
    n_a = tiles - a0
    n_r = jnp.where(borrows, mine, 0)
    b0 = jnp.where(top, PER, jnp.where(lends, mine, 0))
    n_b = tiles - b0

    def at(ph, p):
        return buf.at[ph, pl.ds(pl.multiple_of(p * pkt, pkt), pkt)]

    def m_at(p):
        return m_ref.at[pl.ds(pl.multiple_of(p * pkt, pkt), pkt)]

    def unit_of(t, lane):
        return pl.ds(pl.multiple_of((2 * t + lane) * unit, unit), unit)

    def tile_of(t):
        return pl.ds(pl.multiple_of(t * tile, tile), tile)

    def remote(src, dst, sem, recv_sem, where):
        return pltpu.make_async_remote_copy(
            src_ref=src, dst_ref=dst, send_sem=sem, recv_sem=recv_sem,
            device_id=where, device_id_type=MESH,
        )

    FWD, CROSS, SIDE = (send_sem.at[i] for i in range(3))

    def lane_at(slot, i):
        return lane_sem.at[SPLIT * slot + i]

    def unit_at(slot):
        return unit_sem.at[slot]

    def row_of(t, lane, i):
        return SPLIT * (2 * t + lane) + i

    def fwd_copy(ph, p, sem, src=None):
        ref = at(ph, p)
        return remote(ref if src is None else src, ref, FWD, sem, {"pcol": pcol + 2})

    def arrived(ph, p, sem):
        ref = at(ph, p)
        remote(ref, ref, FWD, sem, {"pcol": pcol_x}).wait_recv()

    def cross_copy(ph, p, sem):
        ref = at(ph, p)
        return remote(ref, ref, CROSS, sem, {"pcol": pcol_x})

    def unit_copy(t, lane, slot, dst, src=None):
        ref = dst.at[unit_of(t, lane)]
        return remote(ref if src is None else src, ref, CROSS, unit_at(slot), {"pcol": pcol_x})

    def spare_row(k, i):
        return n_pkt + row_of(k, x, i)

    def lend_copy(k):
        src, dst = buf.at[1, unit_of(k, x)], buf.at[1, unit_of(tiles + k, x)]
        return remote(src, dst, SIDE, lend_sem.at[k], {"prow": prow - 2})

    def give_copy(k, i):
        return remote(at(1, spare_row(k, i)), at(1, row_of(k, x, i)), SIDE, lane_at(k, i), {"prow": prow + 2})

    def give_unit_copy(k):
        src, dst = buf.at[1, unit_of(tiles + k, 1 - x)], buf.at[1, unit_of(k, 1 - x)]
        return remote(src, dst, SIDE, unit_at(k), {"prow": prow + 2})

    def spare_unit_arrived(k):
        ref = buf.at[1, unit_of(tiles + k, 1 - x)]
        remote(ref, ref, CROSS, unit_at(k), {"pcol": pcol_x}).wait_recv()

    Z, X, Y = (credit.at[i] for i in range(3))

    def allow(sem, where):
        pl.semaphore_signal(sem, inc=1, device_id=where, device_id_type=MESH)

    def allowed(sem):
        pl.semaphore_wait(sem, 1)

    def sent(sem, units):
        ref = buf.at[0, pl.ds(0, units * unit)]
        remote(ref, ref, sem, lane_at(0, 0), {"pcol": pcol_x}).wait_send()

    def sent_by_prow(sem, units):
        for k, n in enumerate(units):
            here = prow == k if k + 1 < len(units) else prow >= k
            pl.when(here)(functools.partial(sent, sem, n))

    def loop(lo, hi, step):
        def one(k, carry):
            step(k)
            return carry

        lax.fori_loop(lo, hi, one, 0)

    load_lane = pltpu.make_async_copy(m_ref, buf.at[0, pl.ds(0, rows)], load_sem.at[0])
    load_own = pltpu.make_async_copy(m_ref, own, load_sem.at[0])
    load_u = pltpu.make_async_copy(u_hbm, uf, load_sem.at[1])
    load_l = pltpu.make_async_copy(l_hbm, lf, load_sem.at[2])
    has_head = (prow == 0) & (pcol >= 1)
    load_head = pltpu.make_async_copy(m_ref.at[pl.ds(0, width)], head, load_sem.at[3])
    pl.when(has_head)(load_head.start)
    load_u.start()
    load_l.start()
    pl.when(is_s0)(load_lane.start)
    pl.when(jnp.logical_not(is_s0))(load_own.start)

    barrier = pltpu.get_barrier_semaphore()

    def greet(where):
        pl.semaphore_signal(barrier, inc=1, device_id=where, device_id_type=MESH)

    greet({"pcol": pcol_x})
    greet({"prow": prow_x})
    for ok, where in (
        (jnp.logical_not(source), {"pcol": pcol - 2}),
        (far, {"pcol": pcol + 2}),
        (jnp.logical_not(top), {"prow": prow - 2}),
        (jnp.logical_not(bottom), {"prow": prow + 2}),
    ):
        pl.when(ok)(functools.partial(greet, where))
    absent = [jnp.where(ok, 1, 0) for ok in (source, last, top, bottom)]
    pl.semaphore_wait(barrier, 6 - sum(absent))

    def head_copy(i, where, src=head):
        return remote(src, head, hsend.at[i], hrecv.at[0], where)

    def pass_head(src=head):
        head_copy(0, {"prow": prow + 1}, src).start()
        pl.when(jnp.logical_not(bottom))(lambda: head_copy(1, {"prow": prow + 2}, src).start())

    @pl.when(has_head)
    def _():
        first = m_ref.at[pl.ds(0, width)]
        pl.when(is_s1)(lambda: head_copy(2, {"pcol": pcol_x}, first).start())
        pass_head(first)

    @pl.when(is_s0)
    def _():
        def ahead(t, lane, slot):
            for i in range(SPLIT):
                p = row_of(t, lane, i)
                pl.when(far)(lambda: fwd_copy(0, p, lane_at(slot, i), m_at(p)).start())

        def across(t, lane, slot):
            for i in range(SPLIT):
                p = row_of(t, lane, i)
                remote(m_at(p), at(0, p), CROSS, lane_at(slot, i), {"pcol": pcol_x}).start()

        def send(t):
            ahead(t, 0, t)
            across(t, 1, t)

        loop(a0, tiles, send)
        ahead(end, 1, tiles)
        across(end, 0, tiles)

    @pl.when(is_s1)
    def _():
        def send(t, lane, slot):
            unit_copy(t, lane, slot, own, m_ref.at[unit_of(t, lane)]).start()

        loop(a0, tiles, lambda t: send(t, 0, t))
        send(end, 1, tiles)

    def split(src, dst, panel):
        rest = src[panel]
        for i in range(PIECES):
            piece = rest.astype(BF)
            dst[panel, i] = piece
            rest = rest - piece.astype(F32)

    load_u.wait()
    load_l.wait()
    split(lf, ls, 0)
    split(uf, us, 0)
    pl.when(source)(lambda: split(uf, us, 1))
    pl.when(is_g & (prow == 1))(lambda: split(lf, ls, 1))
    pl.when(is_s0)(load_lane.wait)
    pl.when(jnp.logical_not(is_s0))(load_own.wait)

    def lower_times(panel, value, out):
        upper = sum(dot(ls[panel, i, :half, :half], value[:half]) for i in reversed(range(PIECES)))
        out[:half] = upper.astype(BF)
        lower = sum(dot(ls[panel, i, half:], value) for i in reversed(range(PIECES)))
        out[half:] = lower.astype(BF)

    def take_head():
        pl.when(has_head)(load_head.wait)

        @pl.when(jnp.logical_not(has_head))
        def _():
            head_copy(0, {"prow": prow_x}).wait_recv()
            pl.when(r == 0)(pass_head)

    def make_u0():
        lower_times(0, head[...], u0)

    def make_lower(t, low, lane):
        here = unit_of(t, lane)
        cur = (own[here].astype(F32) - dot(low, u0[...])).astype(BF)
        value = times_upper(cur, us, 1)
        buf[1, here] = jnp.where((prow == 1) & (t < PER), cur, value)

    def lend(t):
        pl.when(lends & (t >= 0) & (t < mine))(lambda: lend_copy(t).start())

    def borrow():
        @pl.when(borrows)
        def _():
            def one(k):
                lend_copy(k).wait_recv()
                for i in range(SPLIT):
                    pl.when(far)(lambda: fwd_copy(1, spare_row(k, i), lane_at(k, i)).start())

            loop(0, mine, one)

    def send_lower(t, lane, slot):
        pl.when(far & ((t == b0) | (t == MID)))(lambda: allowed(Z))
        for i in range(SPLIT):
            p = row_of(t, lane, i)
            pl.when(far & (t >= b0))(lambda: fwd_copy(1, p, lane_at(slot, i)).start())

    @pl.when(is_s0)
    def _():
        def low_step(i):
            t = a0 + i
            here = tile_of(t)
            buf[0, here] = times_upper(buf[0, here], us, 0)
            pl.when(i == jnp.where(prow == 0, HEAD_AT, n_a - 1))(take_head)

        loop(0, n_a, low_step)
        make_u0()

        def make(t, lane, slot):
            unit_copy(t, lane, slot, own).wait_recv()
            make_lower(t, buf[0, unit_of(t, lane)], lane)

        def send(t):
            send_lower(t, 0, t)
            unit_copy(t, 0, t, buf.at[1]).start()

        def step(i):
            t = a0 + i
            make(t, 0, t)
            lend(t - 1)
            pl.when(i == EARLY + 1 + b0 - a0)(borrow)
            pl.when(i >= 1)(lambda: send(t - 1))

        loop(0, n_a, step)
        make(end, 1, tiles)
        send_lower(end, 0, end)
        send_lower(end, 1, tiles)

    @pl.when(is_s1)
    def _():
        lag = 8

        def relay(t):
            for i in range(SPLIT):
                p, sem = row_of(t, 1, i), lane_at(t, i)
                arrived(0, p, sem)
                pl.when(far)(lambda: fwd_copy(0, p, sem).start())

        def make(t, lane=1):
            make_lower(t, times_upper(buf[0, unit_of(t, lane)], us, 0), lane)
            lend(t - 1)

        def step(s):
            relay(a0 + s)
            pl.when(s == jnp.where(r == 0, PER, lag))(take_head)
            pl.when(s == lag)(make_u0)
            pl.when(s >= lag)(lambda: make(a0 + s - lag))

        loop(0, n_a - 1, step)

        @pl.when(prow == 0)
        def _():
            buf[1, :width] = u0[...]

        def late(i):
            pl.when(i == EARLY)(borrow)
            send_lower(b0 + i, 1, b0 + i)

            @pl.when(i <= lag + 1)
            def _():
                lane = jnp.where(i <= lag, 1, 0)

                @pl.when(i >= lag)
                def _():
                    for n in range(SPLIT):
                        arrived(0, row_of(end, lane, n), lane_at(tiles - lane, n))

                make(jnp.minimum(end - lag + i, end), lane)

        loop(0, n_b, late)
        send_lower(end, 0, tiles)

        def finish(t):
            unit_copy(t, 0, t, buf.at[1]).wait_recv()

        loop(a0, end, finish)

    @pl.when(is_g)
    def _():
        lag_a, lag_b = 6, 4
        n_ax = n_a + 1 - 2 * x
        total = n_ax + n_r + n_b + 1
        give_from = n_ax + EARLY + 3
        use_lent = tiles - PER + EARLY + jnp.where(r == 0, 9, 14)
        first_of_1 = lag_a + PER

        def u1_copy(i, where):
            return remote(u1, u1, hsend.at[3 + i], hrecv.at[1], where)

        def pass_u1():
            u1_copy(0, {"prow": prow - 1}).start()
            pl.when(jnp.logical_not(bottom))(lambda: u1_copy(1, {"prow": prow + 2}).start())

        def arrived_u1():
            u1_copy(0, {"prow": prow_x}).wait_recv()

        tail = tiles - TAIL

        def apply_a(t):
            pl.when((t < end) | (x == 1))(lambda: unit_copy(t, 1 - x, t, buf.at[0]).wait_recv())
            pl.when((t == end) & (x == 1))(lambda: unit_copy(t, x, tiles, buf.at[0]).wait_recv())
            here = tile_of(t)
            low = times_upper(buf[0, here], us, 0)
            own[here] = (own[here].astype(F32) - dot(low, u0[...])).astype(BF)

        def apply_b(t, was_lent):
            if was_lent:
                for i in range(SPLIT):
                    arrived(1, row_of(t, x, i), lane_at(t, i))

            pl.when(t < end)(lambda: unit_copy(t, 1 - x, t, buf.at[1]).wait_recv())
            here = tile_of(t)

            @pl.when(t < tail)
            def _():
                own[here] = (own[here].astype(F32) - dot(buf[1, here], u1[...])).astype(BF)

        def place(s):
            q = s - n_ax
            return (q >= EARLY) & (q < EARLY + n_r), q - jnp.where(q >= EARLY + n_r, n_r, 0)

        def apply_plain(u):
            u_spare, n = place(u)
            plain = (u >= n_ax) & jnp.logical_not(u_spare) & (n != n_b - 1)
            pl.when(plain)(lambda: apply_b(jnp.where(n == n_b, end, b0 + n), False))

        def apply_lent(k):
            pl.when(lends & (k >= 0) & (k < mine))(lambda: apply_b(k, True))

        def step(s):
            in_a = s < n_ax
            spare, k = place(s)
            in_r = jnp.logical_not(in_a) & spare
            in_b = (s >= n_ax) & (s < total) & jnp.logical_not(spare)
            ph = jnp.where(in_a, 0, 1)
            other = jnp.where(in_a, s == n_a, k == n_b)
            t = jnp.where(other, end, jnp.where(in_a, a0 + s, b0 + k))
            slot = jnp.where(other, tiles, t)
            lane = jnp.where(other, 1 - x, x)

            pl.when(s == jnp.where(r == 0, PER, lag_a))(take_head)
            pl.when(s == lag_a)(make_u0)

            @pl.when(in_b & ((k == 0) | (t == MID)))
            def _():
                allowed(X)
                pl.when(far)(lambda: allowed(Z))

            pl.when(borrows & (s == n_ax + EARLY))(lambda: allowed(Y))
            ta = s - lag_a

            def micro(i):
                @pl.when((s < total) & jnp.logical_not(in_r))
                def _():
                    p, sem = row_of(t, lane, i), lane_at(slot, i)
                    arrived(ph, p, sem)
                    pl.when(far)(lambda: fwd_copy(ph, p, sem).start())
                    pl.when(in_a | (t < end))(lambda: cross_copy(ph, p, unit_at(slot)).start())

                @pl.when(in_r)
                def _():
                    n = s - n_ax - EARLY
                    p, sem = spare_row(n, i), lane_at(n, i)
                    arrived(1, p, sem)
                    pl.when(far)(lambda: fwd_copy(1, p, sem).start())
                    cross_copy(1, p, unit_at(n)).start()
                    give_copy(n, i).start()

                pl.when((i == 1) & (ta >= 0) & (ta < n_a))(lambda: apply_a(a0 + ta))
                pl.when(i == SPLIT - 1)(lambda: apply_plain(s - lag_b))
                pl.when(i == 1)(lambda: apply_lent(s - use_lent))

            loop(0, SPLIT, micro)

            pl.when((s == MID - 1 - a0) | (s == n_ax - 1))(lambda: allow(Z, {"pcol": pcol - 2}))
            pl.when((ta == MID - 1 - a0) | (ta == n_a - 1))(lambda: allow(X, {"pcol": pcol_x}))
            pl.when(lends & (ta == MID - 1 - a0))(lambda: allow(Y, {"prow": prow - 2}))

            @pl.when((prow == 1) & (s == first_of_1))
            def _():
                lower_times(1, own[pl.ds(0, width)], u1)

            pl.when((prow == 1) & (s == first_of_1 + 1))(pass_u1)
            @pl.when((prow == 0) & (s == first_of_1))
            def _():
                own[:width] = u0[...]

            @pl.when((prow == 1) & (s == first_of_1 + 1))
            def _():
                own[:width] = u1[...]

            @pl.when((r == 1) & (prow > 1) & (s == tiles - PER - 2))
            def _():
                arrived_u1()
                pass_u1()

            pl.when((r == 0) & (s == tiles - PER - 1))(arrived_u1)

            @pl.when(borrows & (s >= give_from) & (s < give_from + mine))
            def _():
                spare_unit_arrived(s - give_from)
                give_unit_copy(s - give_from).start()

        loop(0, total, step)
        loop(total - lag_b, total, apply_plain)

        @pl.when(r == 1)
        def _():
            u1_copy(0, {"prow": prow_x}).wait_send()
            pl.when(jnp.logical_not(bottom))(lambda: u1_copy(1, {"prow": prow_x}).wait_send())

    @pl.when(r == 0)
    def _():
        head_copy(0, {"prow": prow_x}).wait_send()
        pl.when(jnp.logical_not(bottom))(lambda: head_copy(1, {"prow": prow_x}).wait_send())

    pl.when(is_s1 & (prow == 0))(lambda: head_copy(2, {"pcol": pcol_x}).wait_send())
    for k, n in enumerate(moved):
        if n:
            pl.when(is_g & (prow == k))(functools.partial(sent, SIDE, 2 * n))
            pl.when(source & (prow == k + 2))(functools.partial(sent, SIDE, n))
    full = 2 * tiles
    base = [full - 2 * PER + moved[0], full - PER + moved[1], full - moved[0], full - moved[1], full]
    more, less = [n + 2 for n in base], [n - 2 for n in base]
    pl.when(far & (x == 0))(lambda: sent_by_prow(FWD, more))
    pl.when(far & (x == 1))(lambda: sent_by_prow(FWD, base))
    pl.when(is_g & (x == 0))(lambda: sent_by_prow(CROSS, base))
    pl.when(is_g & (x == 1))(lambda: sent_by_prow(CROSS, less))
    pl.when(is_s0)(lambda: sent_by_prow(CROSS, (full - 2 * PER, full)))
    pl.when(is_s1)(lambda: sent_by_prow(CROSS, (tiles - PER + 1, tiles + 1)))


def finish(own, buf, u1, out_ref, res, sem):
    pcol = lax.axis_index("pcol")
    rows, late = own.shape[0], res.shape[0]
    whole, done, rest = pl.ds(0, rows), pl.ds(0, rows - late), pl.ds(rows - late, late)
    for i in range(2):
        copy = pltpu.make_async_copy(buf.at[i, whole], out_ref, sem.at[0])
        pl.when(pcol == i)(copy.start)
        pl.when(pcol == i)(copy.wait)

    @pl.when(pcol >= 2)
    def _():
        bulk = pltpu.make_async_copy(own.at[done], out_ref.at[done], sem.at[0])
        made = pltpu.make_async_copy(res, out_ref.at[rest], sem.at[1])
        bulk.start()
        res[...] = (own[rest].astype(F32) - dot(buf[1, rest], u1[...])).astype(BF)
        made.start()
        bulk.wait()
        made.wait()


def body(n_prow, n_pcol, matrix, u_inverse, l_inverse):
    rows, width = matrix.shape
    tile, unit, pkt, tiles, moved = sizes(rows, width, n_prow)
    square = (width, width)
    dma = pltpu.SemaphoreType.DMA
    operands = [
        pltpu.with_memory_space_constraint(a, pltpu.HBM) for a in (matrix, u_inverse, l_inverse)
    ]
    lanes = (2, rows + PER * tile, width)
    pieces = pl.pallas_call(
        functools.partial(kernel, n_prow, n_pcol, width),
        out_shape=[jax.ShapeDtypeStruct(shape, BF) for shape in (matrix.shape, lanes, square)],
        in_specs=[pl.BlockSpec(memory_space=pltpu.HBM)] * 3,
        out_specs=[pl.BlockSpec(memory_space=pltpu.VMEM)] * 3,
        scratch_shapes=[
            pltpu.VMEM(square, BF),
            pltpu.VMEM((2,) + square, F32),
            pltpu.VMEM((2,) + square, F32),
            pltpu.VMEM((2, PIECES) + square, BF),
            pltpu.VMEM((2, PIECES) + square, BF),
            pltpu.VMEM(square, BF),
            dma((4,)),
            dma((SPLIT * (tiles + 1),)),
            dma((tiles + 1,)),
            dma((PER,)),
            dma((3,)),
            dma((2,)),
            dma((5,)),
            pltpu.SemaphoreType.REGULAR((3,)),
        ],
        compiler_params=pltpu.CompilerParams(
            collective_id=0, has_side_effects=True, vmem_limit_bytes=40 * 1024 * 1024
        ),
    )(*operands)
    return pl.pallas_call(
        finish,
        out_shape=jax.ShapeDtypeStruct(matrix.shape, BF),
        in_specs=[pl.BlockSpec(memory_space=pltpu.VMEM)] * 3,
        out_specs=pl.BlockSpec(memory_space=pl.ANY),
        scratch_shapes=[pltpu.VMEM((TAIL * tile, width), BF), dma((2,))],
        compiler_params=pltpu.CompilerParams(vmem_limit_bytes=8 * 1024 * 1024),
    )(*pieces)


def solution(mesh):
    run = functools.partial(body, mesh.shape["prow"], mesh.shape["pcol"])
    in_specs = (P("prow", "pcol"), P(), P())
    out_specs = P("prow", "pcol")
    return jax.shard_map(run, mesh=mesh, in_specs=in_specs, out_specs=out_specs, check_vma=False)
```

```python
import functools

import jax
import jax.numpy as jnp
from jax import lax
from jax.experimental import pallas as pl
from jax.experimental.pallas import tpu as pltpu
from jax.sharding import PartitionSpec as P

MESH = pl.DeviceIdType.MESH
BF = jnp.bfloat16
F32 = jnp.float32
PIECES = 2
PER = 4
SPLIT = 4
EARLY = 8
MID = 16
HEAD_AT = 20
TAIL = 4


def sizes(rows, width, n_prow):
    tile = width // PER
    moved = (PER, PER // 2) if n_prow > 2 else (0, 0)
    return tile, tile // 2, tile // 2 // SPLIT, rows // tile, moved


def dot(a, b):
    return jnp.dot(a, b, preferred_element_type=F32)


def times_upper(a, u_ref, panel):
    half = a.shape[1] // 2
    left = sum(dot(a[:, :half], u_ref[panel, i, :half, :half]) for i in reversed(range(PIECES)))
    right = sum(dot(a, u_ref[panel, i, :, half:]) for i in reversed(range(PIECES)))
    return jnp.concatenate([left, right], 1).astype(BF)


def kernel(
    n_prow, n_pcol, width, m_ref, u_hbm, l_hbm, own, buf, u1,
    low_now, head, uf, lf, us, ls, u0,
    load_sem, lane_sem, unit_sem, lend_sem, send_sem, hrecv, hsend, credit,
):
    rows = own.shape[0]
    tile, unit, pkt, tiles, moved = sizes(rows, width, n_prow)
    n_pkt = rows // pkt
    end = tiles - 1
    half = width // 2
    prow, pcol = lax.axis_index("prow"), lax.axis_index("pcol")
    x, r = pcol % 2, prow % 2
    pcol_x, prow_x = pcol + 1 - 2 * x, prow + 1 - 2 * r
    is_s0, is_s1, is_g = pcol == 0, pcol == 1, pcol >= 2
    source, last = pcol < 2, pcol + 2 >= n_pcol
    top, bottom = prow < 2, prow + 2 >= n_prow
    far = jnp.logical_not(last)
    mine = jnp.where(r == 0, moved[0], moved[1])
    lends, borrows = (prow >= 2) & (prow < 4) & (mine > 0), top & (mine > 0)

    a0 = jnp.where(prow == 0, PER, 0)
    n_a = tiles - a0
    n_r = jnp.where(borrows, mine, 0)
    b0 = jnp.where(top, PER, jnp.where(lends, mine, 0))
    n_b = tiles - b0

    def at(ph, p):
        return buf.at[ph, pl.ds(pl.multiple_of(p * pkt, pkt), pkt)]

    def m_at(p):
        return m_ref.at[pl.ds(pl.multiple_of(p * pkt, pkt), pkt)]

    def unit_of(t, lane):
        return pl.ds(pl.multiple_of((2 * t + lane) * unit, unit), unit)

    def tile_of(t):
        return pl.ds(pl.multiple_of(t * tile, tile), tile)

    def remote(src, dst, sem, recv_sem, where):
        return pltpu.make_async_remote_copy(
            src_ref=src, dst_ref=dst, send_sem=sem, recv_sem=recv_sem,
            device_id=where, device_id_type=MESH,
        )

    FWD, CROSS, SIDE = (send_sem.at[i] for i in range(3))

    def lane_at(slot, i):
        return lane_sem.at[SPLIT * slot + i]

    def unit_at(slot):
        return unit_sem.at[slot]

    def row_of(t, lane, i):
        return SPLIT * (2 * t + lane) + i

    def fwd_copy(ph, p, sem, src=None):
        ref = at(ph, p)
        return remote(ref if src is None else src, ref, FWD, sem, {"pcol": pcol + 2})

    def arrived(ph, p, sem):
        ref = at(ph, p)
        remote(ref, ref, FWD, sem, {"pcol": pcol_x}).wait_recv()

    def cross_copy(ph, p, sem):
        ref = at(ph, p)
        return remote(ref, ref, CROSS, sem, {"pcol": pcol_x})

    def unit_copy(t, lane, slot, dst, src=None):
        ref = dst.at[unit_of(t, lane)]
        return remote(ref if src is None else src, ref, CROSS, unit_at(slot), {"pcol": pcol_x})

    def spare_row(k, i):
        return n_pkt + row_of(k, x, i)

    def lend_copy(k):
        src, dst = buf.at[1, unit_of(k, x)], buf.at[1, unit_of(tiles + k, x)]
        return remote(src, dst, SIDE, lend_sem.at[k], {"prow": prow - 2})

    def give_copy(k, i):
        return remote(at(1, spare_row(k, i)), at(1, row_of(k, x, i)), SIDE, lane_at(k, i), {"prow": prow + 2})

    def give_unit_copy(k):
        src, dst = buf.at[1, unit_of(tiles + k, 1 - x)], buf.at[1, unit_of(k, 1 - x)]
        return remote(src, dst, SIDE, unit_at(k), {"prow": prow + 2})

    def spare_unit_arrived(k):
        ref = buf.at[1, unit_of(tiles + k, 1 - x)]
        remote(ref, ref, CROSS, unit_at(k), {"pcol": pcol_x}).wait_recv()

    Z, X, Y = (credit.at[i] for i in range(3))

    def allow(sem, where):
        pl.semaphore_signal(sem, inc=1, device_id=where, device_id_type=MESH)

    def allowed(sem):
        pl.semaphore_wait(sem, 1)

    def sent(sem, units):
        ref = buf.at[0, pl.ds(0, units * unit)]
        remote(ref, ref, sem, lane_at(0, 0), {"pcol": pcol_x}).wait_send()

    def sent_by_prow(sem, units):
        for k, n in enumerate(units):
            here = prow == k if k + 1 < len(units) else prow >= k
            pl.when(here)(functools.partial(sent, sem, n))

    def loop(lo, hi, step):
        def one(k, carry):
            step(k)
            return carry

        lax.fori_loop(lo, hi, one, 0)

    load_lane = pltpu.make_async_copy(m_ref, buf.at[0, pl.ds(0, rows)], load_sem.at[0])
    load_own = pltpu.make_async_copy(m_ref, own, load_sem.at[0])
    load_u = pltpu.make_async_copy(u_hbm, uf, load_sem.at[1])
    load_l = pltpu.make_async_copy(l_hbm, lf, load_sem.at[2])
    has_head = (prow == 0) & (pcol >= 1)
    load_head = pltpu.make_async_copy(m_ref.at[pl.ds(0, width)], head, load_sem.at[3])

    barrier = pltpu.get_barrier_semaphore()

    def greet(where):
        pl.semaphore_signal(barrier, inc=1, device_id=where, device_id_type=MESH)

    greet({"pcol": pcol_x})
    greet({"prow": prow_x})
    for ok, where in (
        (jnp.logical_not(source), {"pcol": pcol - 2}),
        (far, {"pcol": pcol + 2}),
        (jnp.logical_not(top), {"prow": prow - 2}),
        (jnp.logical_not(bottom), {"prow": prow + 2}),
    ):
        pl.when(ok)(functools.partial(greet, where))
    pl.when(has_head)(load_head.start)
    load_u.start()
    load_l.start()
    pl.when(is_s0)(load_lane.start)
    pl.when(jnp.logical_not(is_s0))(load_own.start)
    absent = [jnp.where(ok, 1, 0) for ok in (source, last, top, bottom)]
    pl.semaphore_wait(barrier, 6 - sum(absent))

    def head_copy(i, where, src=head):
        return remote(src, head, hsend.at[i], hrecv.at[0], where)

    def pass_head(src=head):
        head_copy(0, {"prow": prow + 1}, src).start()
        pl.when(jnp.logical_not(bottom))(lambda: head_copy(1, {"prow": prow + 2}, src).start())

    @pl.when(has_head)
    def _():
        first = m_ref.at[pl.ds(0, width)]
        pl.when(is_s1)(lambda: head_copy(2, {"pcol": pcol_x}, first).start())
        pass_head(first)

    @pl.when(is_s0)
    def _():
        def ahead(t, lane, slot):
            for i in range(SPLIT):
                p = row_of(t, lane, i)
                pl.when(far)(lambda: fwd_copy(0, p, lane_at(slot, i), m_at(p)).start())

        def across(t, lane, slot):
            for i in range(SPLIT):
                p = row_of(t, lane, i)
                remote(m_at(p), at(0, p), CROSS, lane_at(slot, i), {"pcol": pcol_x}).start()

        def send(t):
            ahead(t, 0, t)
            across(t, 1, t)

        loop(a0, tiles, send)
        ahead(end, 1, tiles)
        across(end, 0, tiles)

    @pl.when(is_s1)
    def _():
        def send(t, lane, slot):
            unit_copy(t, lane, slot, own, m_ref.at[unit_of(t, lane)]).start()

        loop(a0, tiles, lambda t: send(t, 0, t))
        send(end, 1, tiles)

    def split(src, dst, panel):
        rest = src[panel]
        for i in range(PIECES):
            piece = rest.astype(BF)
            dst[panel, i] = piece
            rest = rest - piece.astype(F32)

    load_u.wait()
    load_l.wait()
    split(lf, ls, 0)
    split(uf, us, 0)
    pl.when(source)(lambda: split(uf, us, 1))
    pl.when(is_g & (prow == 1))(lambda: split(lf, ls, 1))
    pl.when(is_s0)(load_lane.wait)
    pl.when(jnp.logical_not(is_s0))(load_own.wait)

    def lower_times(panel, value, out):
        upper = sum(dot(ls[panel, i, :half, :half], value[:half]) for i in reversed(range(PIECES)))
        out[:half] = upper.astype(BF)
        lower = sum(dot(ls[panel, i, half:], value) for i in reversed(range(PIECES)))
        out[half:] = lower.astype(BF)

    def take_head():
        pl.when(has_head)(load_head.wait)

        @pl.when(jnp.logical_not(has_head))
        def _():
            head_copy(0, {"prow": prow_x}).wait_recv()
            pl.when(r == 0)(pass_head)

    def make_u0():
        lower_times(0, head[...], u0)

    def make_lower(t, low, lane):
        here = unit_of(t, lane)
        cur = (own[here].astype(F32) - dot(low, u0[...])).astype(BF)
        value = times_upper(cur, us, 1)
        buf[1, here] = jnp.where((prow == 1) & (t < PER), cur, value)

    def lend(t):
        pl.when(lends & (t >= 0) & (t < mine))(lambda: lend_copy(t).start())

    def borrow():
        @pl.when(borrows)
        def _():
            def one(k):
                lend_copy(k).wait_recv()
                for i in range(SPLIT):
                    pl.when(far)(lambda: fwd_copy(1, spare_row(k, i), lane_at(k, i)).start())

            loop(0, mine, one)

    def send_lower(t, lane, slot):
        pl.when(far & ((t == b0) | (t == MID)))(lambda: allowed(Z))
        for i in range(SPLIT):
            p = row_of(t, lane, i)
            pl.when(far & (t >= b0))(lambda: fwd_copy(1, p, lane_at(slot, i)).start())

    @pl.when(is_s0)
    def _():
        def low_step(i):
            t = a0 + i
            here = tile_of(t)
            buf[0, here] = times_upper(buf[0, here], us, 0)
            pl.when(i == jnp.where(prow == 0, HEAD_AT, n_a - 1))(take_head)

        loop(0, n_a, low_step)
        make_u0()

        def make(t, lane, slot):
            unit_copy(t, lane, slot, own).wait_recv()
            make_lower(t, buf[0, unit_of(t, lane)], lane)

        def send(t):
            send_lower(t, 0, t)
            unit_copy(t, 0, t, buf.at[1]).start()

        def step(i):
            t = a0 + i
            make(t, 0, t)
            lend(t - 1)
            pl.when(i == EARLY + 1 + b0 - a0)(borrow)
            pl.when(i >= 1)(lambda: send(t - 1))

        loop(0, n_a, step)
        make(end, 1, tiles)
        send_lower(end, 0, end)
        send_lower(end, 1, tiles)

    @pl.when(is_s1)
    def _():
        lag = 8

        def relay(t, i):
            p, sem = row_of(t, 1, i), lane_at(t, i)
            arrived(0, p, sem)
            pl.when(far)(lambda: fwd_copy(0, p, sem).start())

        def make_part(t, i):
            here, low, cur = unit_of(t, 1), slice(0, unit), slice(unit, tile)
            if i == 0:
                low_now[low] = times_upper(buf[0, here], us, 0)
            elif i == 1:
                low_now[cur] = (own[here].astype(F32) - dot(low_now[low], u0[...])).astype(BF)
            elif i == 2:
                value = times_upper(low_now[cur], us, 1)
                buf[1, here] = jnp.where((prow == 1) & (t < PER), low_now[cur], value)
            else:
                lend(t - 1)

        def make(t, lane=1):
            make_lower(t, times_upper(buf[0, unit_of(t, lane)], us, 0), lane)
            lend(t - 1)

        def step(s):
            pl.when(s == jnp.where(r == 0, PER, lag))(take_head)
            pl.when(s == lag)(make_u0)
            for i in range(SPLIT):
                relay(a0 + s, i)
                pl.when(s >= lag)(functools.partial(make_part, a0 + s - lag, i))

        loop(0, n_a - 1, step)

        @pl.when(prow == 0)
        def _():
            buf[1, :width] = u0[...]

        def late(i):
            pl.when(i == EARLY)(borrow)
            send_lower(b0 + i, 1, b0 + i)

            @pl.when(i <= lag + 1)
            def _():
                lane = jnp.where(i <= lag, 1, 0)

                @pl.when(i >= lag)
                def _():
                    for n in range(SPLIT):
                        arrived(0, row_of(end, lane, n), lane_at(tiles - lane, n))

                make(jnp.minimum(end - lag + i, end), lane)

        loop(0, n_b, late)
        send_lower(end, 0, tiles)

        def finish(t):
            unit_copy(t, 0, t, buf.at[1]).wait_recv()

        loop(a0, end, finish)

    @pl.when(is_g)
    def _():
        lag_a, lag_b = 6, 4
        n_ax = n_a + 1 - 2 * x
        total = n_ax + n_r + n_b + 1
        give_from = n_ax + EARLY + 3
        use_lent = tiles - PER + EARLY + jnp.where(r == 0, 9, 14)
        first_of_1 = lag_a + PER

        def u1_copy(i, where):
            return remote(u1, u1, hsend.at[3 + i], hrecv.at[1], where)

        def pass_u1():
            u1_copy(0, {"prow": prow - 1}).start()
            pl.when(jnp.logical_not(bottom))(lambda: u1_copy(1, {"prow": prow + 2}).start())

        def arrived_u1():
            u1_copy(0, {"prow": prow_x}).wait_recv()

        tail = tiles - TAIL

        def lower_a(t):
            pl.when((t < end) | (x == 1))(lambda: unit_copy(t, 1 - x, t, buf.at[0]).wait_recv())
            pl.when((t == end) & (x == 1))(lambda: unit_copy(t, x, tiles, buf.at[0]).wait_recv())
            low_now[...] = times_upper(buf[0, tile_of(t)], us, 0)

        def apply_a(t):
            here = tile_of(t)
            own[here] = (own[here].astype(F32) - dot(low_now[...], u0[...])).astype(BF)

        def apply_b(t, was_lent):
            if was_lent:
                for i in range(SPLIT):
                    arrived(1, row_of(t, x, i), lane_at(t, i))

            pl.when(t < end)(lambda: unit_copy(t, 1 - x, t, buf.at[1]).wait_recv())
            here = tile_of(t)

            @pl.when(t < tail)
            def _():
                own[here] = (own[here].astype(F32) - dot(buf[1, here], u1[...])).astype(BF)

        def place(s):
            q = s - n_ax
            return (q >= EARLY) & (q < EARLY + n_r), q - jnp.where(q >= EARLY + n_r, n_r, 0)

        def apply_plain(u):
            u_spare, n = place(u)
            plain = (u >= n_ax) & jnp.logical_not(u_spare) & (n != n_b - 1)
            pl.when(plain)(lambda: apply_b(jnp.where(n == n_b, end, b0 + n), False))

        def apply_lent(k):
            pl.when(lends & (k >= 0) & (k < mine))(lambda: apply_b(k, True))

        def step(s):
            in_a = s < n_ax
            spare, k = place(s)
            in_r = jnp.logical_not(in_a) & spare
            in_b = (s >= n_ax) & (s < total) & jnp.logical_not(spare)
            ph = jnp.where(in_a, 0, 1)
            other = jnp.where(in_a, s == n_a, k == n_b)
            t = jnp.where(other, end, jnp.where(in_a, a0 + s, b0 + k))
            slot = jnp.where(other, tiles, t)
            lane = jnp.where(other, 1 - x, x)

            pl.when(s == jnp.where(r == 0, PER, lag_a))(take_head)
            pl.when(s == lag_a)(make_u0)

            @pl.when(in_b & ((k == 0) | (t == MID)))
            def _():
                allowed(X)
                pl.when(far)(lambda: allowed(Z))

            pl.when(borrows & (s == n_ax + EARLY))(lambda: allowed(Y))
            ta = s - lag_a

            def micro(i):
                @pl.when((s < total) & jnp.logical_not(in_r))
                def _():
                    p, sem = row_of(t, lane, i), lane_at(slot, i)
                    arrived(ph, p, sem)
                    pl.when(far)(lambda: fwd_copy(ph, p, sem).start())
                    pl.when(in_a | (t < end))(lambda: cross_copy(ph, p, unit_at(slot)).start())

                @pl.when(in_r)
                def _():
                    n = s - n_ax - EARLY
                    p, sem = spare_row(n, i), lane_at(n, i)
                    arrived(1, p, sem)
                    pl.when(far)(lambda: fwd_copy(1, p, sem).start())
                    cross_copy(1, p, unit_at(n)).start()
                    give_copy(n, i).start()

                pl.when((i == 0) & (ta >= 0) & (ta < n_a))(lambda: lower_a(a0 + ta))
                pl.when((i == 1) & (ta >= 0) & (ta < n_a))(lambda: apply_a(a0 + ta))
                pl.when(i == SPLIT - 1)(lambda: apply_plain(s - lag_b))
                pl.when(i == 1)(lambda: apply_lent(s - use_lent))

            loop(0, SPLIT, micro)

            pl.when((s == MID - 1 - a0) | (s == n_ax - 1))(lambda: allow(Z, {"pcol": pcol - 2}))
            pl.when((ta == MID - 1 - a0) | (ta == n_a - 1))(lambda: allow(X, {"pcol": pcol_x}))
            pl.when(lends & (ta == MID - 1 - a0))(lambda: allow(Y, {"prow": prow - 2}))

            @pl.when((prow == 1) & (s == first_of_1))
            def _():
                lower_times(1, own[pl.ds(0, width)], u1)

            pl.when((prow == 1) & (s == first_of_1 + 1))(pass_u1)
            @pl.when((prow == 0) & (s == first_of_1))
            def _():
                own[:width] = u0[...]

            @pl.when((prow == 1) & (s == first_of_1 + 1))
            def _():
                own[:width] = u1[...]

            @pl.when((r == 1) & (prow > 1) & (s == tiles - PER - 2))
            def _():
                arrived_u1()
                pass_u1()

            pl.when((r == 0) & (s == tiles - PER - 1))(arrived_u1)

            @pl.when(borrows & (s >= give_from) & (s < give_from + mine))
            def _():
                spare_unit_arrived(s - give_from)
                give_unit_copy(s - give_from).start()

        loop(0, total, step)
        loop(total - lag_b, total, apply_plain)

        @pl.when(r == 1)
        def _():
            u1_copy(0, {"prow": prow_x}).wait_send()
            pl.when(jnp.logical_not(bottom))(lambda: u1_copy(1, {"prow": prow_x}).wait_send())

    @pl.when(r == 0)
    def _():
        head_copy(0, {"prow": prow_x}).wait_send()
        pl.when(jnp.logical_not(bottom))(lambda: head_copy(1, {"prow": prow_x}).wait_send())

    pl.when(is_s1 & (prow == 0))(lambda: head_copy(2, {"pcol": pcol_x}).wait_send())
    for k, n in enumerate(moved):
        if n:
            pl.when(is_g & (prow == k))(functools.partial(sent, SIDE, 2 * n))
            pl.when(source & (prow == k + 2))(functools.partial(sent, SIDE, n))
    full = 2 * tiles
    base = [full - 2 * PER + moved[0], full - PER + moved[1], full - moved[0], full - moved[1], full]
    more, less = [n + 2 for n in base], [n - 2 for n in base]
    pl.when(far & (x == 0))(lambda: sent_by_prow(FWD, more))
    pl.when(far & (x == 1))(lambda: sent_by_prow(FWD, base))
    pl.when(is_g & (x == 0))(lambda: sent_by_prow(CROSS, base))
    pl.when(is_g & (x == 1))(lambda: sent_by_prow(CROSS, less))
    pl.when(is_s0)(lambda: sent_by_prow(CROSS, (full - 2 * PER, full)))
    pl.when(is_s1)(lambda: sent_by_prow(CROSS, (tiles - PER + 1, tiles + 1)))


def finish(own, buf, u1, out_ref, res, sem):
    pcol = lax.axis_index("pcol")
    rows, late = own.shape[0], res.shape[0]
    whole, done, rest = pl.ds(0, rows), pl.ds(0, rows - late), pl.ds(rows - late, late)
    for i in range(2):
        copy = pltpu.make_async_copy(buf.at[i, whole], out_ref, sem.at[0])
        pl.when(pcol == i)(copy.start)
        pl.when(pcol == i)(copy.wait)

    @pl.when(pcol >= 2)
    def _():
        bulk = pltpu.make_async_copy(own.at[done], out_ref.at[done], sem.at[0])
        made = pltpu.make_async_copy(res, out_ref.at[rest], sem.at[1])
        bulk.start()
        res[...] = (own[rest].astype(F32) - dot(buf[1, rest], u1[...])).astype(BF)
        made.start()
        bulk.wait()
        made.wait()


def body(n_prow, n_pcol, matrix, u_inverse, l_inverse):
    rows, width = matrix.shape
    tile, unit, pkt, tiles, moved = sizes(rows, width, n_prow)
    square = (width, width)
    dma = pltpu.SemaphoreType.DMA
    operands = [
        pltpu.with_memory_space_constraint(a, pltpu.HBM) for a in (matrix, u_inverse, l_inverse)
    ]
    lanes = (2, rows + PER * tile, width)
    pieces = pl.pallas_call(
        functools.partial(kernel, n_prow, n_pcol, width),
        out_shape=[jax.ShapeDtypeStruct(shape, BF) for shape in (matrix.shape, lanes, square)],
        in_specs=[pl.BlockSpec(memory_space=pltpu.HBM)] * 3,
        out_specs=[pl.BlockSpec(memory_space=pltpu.VMEM)] * 3,
        scratch_shapes=[
            pltpu.VMEM((tile, width), BF),
            pltpu.VMEM(square, BF),
            pltpu.VMEM((2,) + square, F32),
            pltpu.VMEM((2,) + square, F32),
            pltpu.VMEM((2, PIECES) + square, BF),
            pltpu.VMEM((2, PIECES) + square, BF),
            pltpu.VMEM(square, BF),
            dma((4,)),
            dma((SPLIT * (tiles + 1),)),
            dma((tiles + 1,)),
            dma((PER,)),
            dma((3,)),
            dma((2,)),
            dma((5,)),
            pltpu.SemaphoreType.REGULAR((3,)),
        ],
        compiler_params=pltpu.CompilerParams(
            collective_id=0, has_side_effects=True, vmem_limit_bytes=40 * 1024 * 1024
        ),
    )(*operands)
    return pl.pallas_call(
        finish,
        out_shape=jax.ShapeDtypeStruct(matrix.shape, BF),
        in_specs=[pl.BlockSpec(memory_space=pltpu.VMEM)] * 3,
        out_specs=pl.BlockSpec(memory_space=pl.ANY),
        scratch_shapes=[pltpu.VMEM((TAIL * tile, width), BF), dma((2,))],
        compiler_params=pltpu.CompilerParams(vmem_limit_bytes=8 * 1024 * 1024),
    )(*pieces)


def solution(mesh):
    run = functools.partial(body, mesh.shape["prow"], mesh.shape["pcol"])
    in_specs = (P("prow", "pcol"), P(), P())
    out_specs = P("prow", "pcol")
    return jax.shard_map(run, mesh=mesh, in_specs=in_specs, out_specs=out_specs, check_vma=False)
```

```python
import functools

import jax
import jax.numpy as jnp
from jax import lax
from jax.experimental import pallas as pl
from jax.experimental.pallas import tpu as pltpu
from jax.sharding import PartitionSpec as P

MESH = pl.DeviceIdType.MESH
BF = jnp.bfloat16
F32 = jnp.float32
PIECES = 2
PER = 4
SPLIT = 4
EARLY = 8
MID = 16
RING, BLOCK = 14, 7
HEAD_AT = 20
TAIL = 4


def sizes(rows, width, n_prow):
    tile = width // PER
    moved = (PER, PER // 2) if n_prow > 2 else (0, 0)
    return tile, tile // 2, tile // 2 // SPLIT, rows // tile, moved


def dot(a, b):
    return jnp.dot(a, b, preferred_element_type=F32)


def times_upper(a, u_ref, panel):
    half = a.shape[1] // 2
    left = sum(dot(a[:, :half], u_ref[panel, i, :half, :half]) for i in reversed(range(PIECES)))
    right = sum(dot(a, u_ref[panel, i, :, half:]) for i in reversed(range(PIECES)))
    return jnp.concatenate([left, right], 1).astype(BF)


def kernel(
    n_prow, n_pcol, width, m_ref, u_hbm, l_hbm, own, buf, u1,
    low_now, head, uf, lf, us, ls, u0,
    load_sem, lane_sem, unit_sem, lend_sem, send_sem, hrecv, hsend, credit,
):
    rows = own.shape[0]
    tile, unit, pkt, tiles, moved = sizes(rows, width, n_prow)
    n_pkt = rows // pkt
    end = tiles - 1
    half = width // 2
    prow, pcol = lax.axis_index("prow"), lax.axis_index("pcol")
    x, r = pcol % 2, prow % 2
    pcol_x, prow_x = pcol + 1 - 2 * x, prow + 1 - 2 * r
    is_s0, is_s1, is_g = pcol == 0, pcol == 1, pcol >= 2
    source, last = pcol < 2, pcol + 2 >= n_pcol
    top, bottom = prow < 2, prow + 2 >= n_prow
    far = jnp.logical_not(last)
    mine = jnp.where(r == 0, moved[0], moved[1])
    lends, borrows = (prow >= 2) & (prow < 4) & (mine > 0), top & (mine > 0)

    a0 = jnp.where(prow == 0, PER, 0)
    n_a = tiles - a0
    n_r = jnp.where(borrows, mine, 0)
    b0 = jnp.where(top, PER, jnp.where(lends, mine, 0))
    n_b = tiles - b0
    n_ax = n_a + 1 - 2 * x
    total = n_ax + n_r + n_b + 1

    def at(ph, p):
        return buf.at[ph, pl.ds(pl.multiple_of(p * pkt, pkt), pkt)]

    def m_at(p):
        return m_ref.at[pl.ds(pl.multiple_of(p * pkt, pkt), pkt)]

    def unit_of(t, lane):
        return pl.ds(pl.multiple_of((2 * t + lane) * unit, unit), unit)

    def tile_of(t):
        return pl.ds(pl.multiple_of(t * tile, tile), tile)

    def remote(src, dst, sem, recv_sem, where):
        return pltpu.make_async_remote_copy(
            src_ref=src, dst_ref=dst, send_sem=sem, recv_sem=recv_sem,
            device_id=where, device_id_type=MESH,
        )

    FWD, CROSS, SIDE = (send_sem.at[i] for i in range(3))

    def lane_at(s, i):
        return lane_sem.at[SPLIT * (s % RING) + i]

    def unit_at(slot):
        return unit_sem.at[slot]

    def row_of(t, lane, i):
        return SPLIT * (2 * t + lane) + i

    def fwd_copy(ph, p, sem, src=None):
        ref = at(ph, p)
        return remote(ref if src is None else src, ref, FWD, sem, {"pcol": pcol + 2})

    def arrived(ph, p, sem):
        ref = at(ph, p)
        remote(ref, ref, FWD, sem, {"pcol": pcol_x}).wait_recv()

    def cross_copy(ph, p, sem):
        ref = at(ph, p)
        return remote(ref, ref, CROSS, sem, {"pcol": pcol_x})

    def unit_copy(t, lane, slot, dst, src=None):
        ref = dst.at[unit_of(t, lane)]
        return remote(ref if src is None else src, ref, CROSS, unit_at(slot), {"pcol": pcol_x})

    def spare_row(k, i):
        return n_pkt + row_of(k, x, i)

    def lend_copy(k):
        src, dst = buf.at[1, unit_of(k, x)], buf.at[1, unit_of(tiles + k, x)]
        return remote(src, dst, SIDE, lend_sem.at[k], {"prow": prow - 2})

    def give_copy(k):
        src, dst = buf.at[1, unit_of(tiles + k, x)], buf.at[1, unit_of(k, x)]
        return remote(src, dst, SIDE, lend_sem.at[k], {"prow": prow + 2})

    def give_unit_copy(k):
        src, dst = buf.at[1, unit_of(tiles + k, 1 - x)], buf.at[1, unit_of(k, 1 - x)]
        return remote(src, dst, SIDE, unit_at(k), {"prow": prow + 2})

    def spare_unit_arrived(k):
        ref = buf.at[1, unit_of(tiles + k, 1 - x)]
        remote(ref, ref, CROSS, unit_at(k), {"pcol": pcol_x}).wait_recv()

    Z, X, Y = (credit.at[i] for i in range(3))

    def allow(sem, where):
        pl.semaphore_signal(sem, inc=1, device_id=where, device_id_type=MESH)

    def allowed(sem):
        pl.semaphore_wait(sem, 1)

    def gate(s, sem=Z):
        pl.when((s >= RING) & (s % BLOCK == 0))(lambda: allowed(sem))

    def open_gate(s, steps, sem, where):
        pl.when((s % BLOCK == BLOCK - 1) & (s + BLOCK + 1 < steps))(lambda: allow(sem, where))

    def step_of(k):
        return n_ax + k + jnp.where(k >= EARLY, n_r, 0)

    def sent(sem, units):
        ref = buf.at[0, pl.ds(0, units * unit)]
        remote(ref, ref, sem, lane_at(0, 0), {"pcol": pcol_x}).wait_send()

    def sent_by_prow(sem, units):
        for k, n in enumerate(units):
            here = prow == k if k + 1 < len(units) else prow >= k
            pl.when(here)(functools.partial(sent, sem, n))

    def loop(lo, hi, step):
        def one(k, carry):
            step(k)
            return carry

        lax.fori_loop(lo, hi, one, 0)

    load_lane = pltpu.make_async_copy(m_ref, buf.at[0, pl.ds(0, rows)], load_sem.at[0])
    load_own = pltpu.make_async_copy(m_ref, own, load_sem.at[0])
    load_u = pltpu.make_async_copy(u_hbm, uf, load_sem.at[1])
    load_l = pltpu.make_async_copy(l_hbm, lf, load_sem.at[2])
    has_head = (prow == 0) & (pcol >= 1)
    load_head = pltpu.make_async_copy(m_ref.at[pl.ds(0, width)], head, load_sem.at[3])

    barrier = pltpu.get_barrier_semaphore()

    def greet(where):
        pl.semaphore_signal(barrier, inc=1, device_id=where, device_id_type=MESH)

    greet({"pcol": pcol_x})
    greet({"prow": prow_x})
    for ok, where in (
        (jnp.logical_not(source), {"pcol": pcol - 2}),
        (far, {"pcol": pcol + 2}),
        (jnp.logical_not(top), {"prow": prow - 2}),
        (jnp.logical_not(bottom), {"prow": prow + 2}),
    ):
        pl.when(ok)(functools.partial(greet, where))
    pl.when(has_head)(load_head.start)
    load_u.start()
    load_l.start()
    pl.when(is_s0)(load_lane.start)
    pl.when(jnp.logical_not(is_s0))(load_own.start)
    absent = [jnp.where(ok, 1, 0) for ok in (source, last, top, bottom)]
    pl.semaphore_wait(barrier, 6 - sum(absent))

    def head_copy(i, where, src=head):
        return remote(src, head, hsend.at[i], hrecv.at[0], where)

    def pass_head(src=head):
        head_copy(0, {"prow": prow + 1}, src).start()
        pl.when(jnp.logical_not(bottom))(lambda: head_copy(1, {"prow": prow + 2}, src).start())

    @pl.when(has_head)
    def _():
        first = m_ref.at[pl.ds(0, width)]
        pl.when(is_s1)(lambda: head_copy(2, {"pcol": pcol_x}, first).start())
        pass_head(first)

    def push(s):
        pl.when(far)(lambda: gate(s))
        gate(s, X)
        t, lane = jnp.where(s < n_a, a0 + s, end), jnp.where(s < n_a, 0, 1)
        for i in range(SPLIT):
            p, c = row_of(t, lane, i), row_of(t, 1 - lane, i)
            pl.when(far)(lambda: fwd_copy(0, p, lane_at(s, i), m_at(p)).start())
            remote(m_at(c), at(0, c), CROSS, lane_at(s, i), {"pcol": pcol_x}).start()

    @pl.when(is_s0)
    def _():
        loop(0, RING, push)

    @pl.when(is_s1)
    def _():
        def send(t, lane, slot):
            unit_copy(t, lane, slot, own, m_ref.at[unit_of(t, lane)]).start()

        loop(a0, tiles, lambda t: send(t, 0, t))
        send(end, 1, tiles)

    def split(src, dst, panel):
        rest = src[panel]
        for i in range(PIECES):
            piece = rest.astype(BF)
            dst[panel, i] = piece
            rest = rest - piece.astype(F32)

    load_u.wait()
    load_l.wait()
    split(lf, ls, 0)
    split(uf, us, 0)
    pl.when(source)(lambda: split(uf, us, 1))
    pl.when(is_g & (prow == 1))(lambda: split(lf, ls, 1))
    pl.when(is_s0)(load_lane.wait)
    pl.when(jnp.logical_not(is_s0))(load_own.wait)

    def lower_times(panel, value, out):
        upper = sum(dot(ls[panel, i, :half, :half], value[:half]) for i in reversed(range(PIECES)))
        out[:half] = upper.astype(BF)
        lower = sum(dot(ls[panel, i, half:], value) for i in reversed(range(PIECES)))
        out[half:] = lower.astype(BF)

    def take_head():
        pl.when(has_head)(load_head.wait)

        @pl.when(jnp.logical_not(has_head))
        def _():
            head_copy(0, {"prow": prow_x}).wait_recv()
            pl.when(r == 0)(pass_head)

    def make_u0():
        lower_times(0, head[...], u0)

    def make_lower(t, low, lane):
        here = unit_of(t, lane)
        cur = (own[here].astype(F32) - dot(low, u0[...])).astype(BF)
        value = times_upper(cur, us, 1)
        buf[1, here] = jnp.where((prow == 1) & (t < PER), cur, value)

    def lend(t):
        pl.when(lends & (t >= 0) & (t < mine))(lambda: lend_copy(t).start())

    def borrow():
        @pl.when(borrows)
        def _():
            def one(k):
                s = n_ax + EARLY + k
                pl.when(far)(lambda: gate(s))
                lend_copy(k).wait_recv()
                for i in range(SPLIT):
                    pl.when(far)(lambda: fwd_copy(1, spare_row(k, i), lane_at(s, i)).start())

            loop(0, mine, one)

    def send_lower(t, lane, s):
        @pl.when(far)
        def _():
            gate(s)
            for i in range(SPLIT):
                fwd_copy(1, row_of(t, lane, i), lane_at(s, i)).start()

    @pl.when(is_s0)
    def _():
        def low_step(i):
            t = a0 + i
            here = tile_of(t)
            buf[0, here] = times_upper(buf[0, here], us, 0)
            pl.when(i == n_a - 2)(lambda: loop(RING, RING + BLOCK, push))
            pl.when(i == jnp.where(prow == 0, HEAD_AT, n_a - 1))(take_head)

        loop(0, n_a, low_step)
        make_u0()

        def make(t, lane, slot):
            unit_copy(t, lane, slot, own).wait_recv()
            make_lower(t, buf[0, unit_of(t, lane)], lane)

        first = PER + 1

        def show(t):
            unit_copy(t, 0, t, buf.at[1]).start()

        def send(k):
            pl.when(k == EARLY)(borrow)
            send_lower(b0 + k, 0, step_of(k))

        def step(i):
            t = a0 + i
            make(t, 0, t)
            lend(t - 1)
            pl.when(i >= PER)(lambda: show(t - PER))

            @pl.when(i < PER)
            def _():
                for n in range(2):
                    k = RING + BLOCK + 2 * i + n
                    pl.when(k <= n_a)(lambda: push(k))

            pl.when(i >= first)(lambda: send(i - first))

        loop(0, n_a, step)
        make(end, 1, tiles)
        loop(n_a - first, n_b, send)
        loop(tiles - PER, end, show)
        send_lower(end, 1, total - 1)

    @pl.when(is_s1)
    def _():
        lag = 8

        def relay(s, i):
            p, sem = row_of(a0 + s, 1, i), lane_at(s, i)
            arrived(0, p, sem)
            pl.when(far)(lambda: fwd_copy(0, p, sem).start())

        def make_part(t, i):
            here, low, cur = unit_of(t, 1), slice(0, unit), slice(unit, tile)
            if i == 0:
                low_now[low] = times_upper(buf[0, here], us, 0)
            elif i == 1:
                low_now[cur] = (own[here].astype(F32) - dot(low_now[low], u0[...])).astype(BF)
            elif i == 2:
                value = times_upper(low_now[cur], us, 1)
                buf[1, here] = jnp.where((prow == 1) & (t < PER), low_now[cur], value)
            else:
                lend(t - 1)

        def make(t, lane=1):
            make_lower(t, times_upper(buf[0, unit_of(t, lane)], us, 0), lane)
            lend(t - 1)

        def step(s):
            pl.when(s == jnp.where(r == 0, PER, lag))(take_head)
            pl.when(s == lag)(make_u0)
            pl.when(far)(lambda: gate(s))
            for i in range(SPLIT):
                relay(s, i)
                pl.when(s >= lag)(functools.partial(make_part, a0 + s - lag, i))
            open_gate(s, n_a + 1, X, {"pcol": pcol_x})

        loop(0, n_a - 1, step)

        @pl.when(prow == 0)
        def _():
            buf[1, :width] = u0[...]

        def late(i):
            pl.when(i == EARLY)(borrow)
            send_lower(b0 + i, 1, step_of(i))

            @pl.when(i <= lag + 1)
            def _():
                lane = jnp.where(i <= lag, 1, 0)

                @pl.when(i >= lag)
                def _():
                    for n in range(SPLIT):
                        arrived(0, row_of(end, lane, n), lane_at(n_a - lane, n))

                make(jnp.minimum(end - lag + i, end), lane)

        loop(0, n_b, late)
        send_lower(end, 0, total - 1)

        def finish(t):
            unit_copy(t, 0, t, buf.at[1]).wait_recv()

        loop(a0, end, finish)

    @pl.when(is_g)
    def _():
        lag_a, lag_b = 6, 4
        give_from = n_ax + EARLY + 3
        use_lent = tiles - PER + EARLY + jnp.where(r == 0, 9, 14)
        first_of_1 = lag_a + PER

        def u1_copy(i, where):
            return remote(u1, u1, hsend.at[3 + i], hrecv.at[1], where)

        def pass_u1():
            u1_copy(0, {"prow": prow - 1}).start()
            pl.when(jnp.logical_not(bottom))(lambda: u1_copy(1, {"prow": prow + 2}).start())

        def arrived_u1():
            u1_copy(0, {"prow": prow_x}).wait_recv()

        tail = tiles - TAIL

        def lower_a(t):
            pl.when((t < end) | (x == 1))(lambda: unit_copy(t, 1 - x, t, buf.at[0]).wait_recv())
            pl.when((t == end) & (x == 1))(lambda: unit_copy(t, x, tiles, buf.at[0]).wait_recv())
            low_now[...] = times_upper(buf[0, tile_of(t)], us, 0)

        def apply_a(t):
            here = tile_of(t)
            own[here] = (own[here].astype(F32) - dot(low_now[...], u0[...])).astype(BF)

        def apply_b(t, was_lent):
            if was_lent:
                give_copy(t).wait_recv()

            pl.when(t < end)(lambda: unit_copy(t, 1 - x, t, buf.at[1]).wait_recv())
            here = tile_of(t)

            @pl.when(t < tail)
            def _():
                own[here] = (own[here].astype(F32) - dot(buf[1, here], u1[...])).astype(BF)

        def place(s):
            q = s - n_ax
            return (q >= EARLY) & (q < EARLY + n_r), q - jnp.where(q >= EARLY + n_r, n_r, 0)

        def apply_plain(u):
            u_spare, n = place(u)
            plain = (u >= n_ax) & jnp.logical_not(u_spare) & (n != n_b - 1)
            pl.when(plain)(lambda: apply_b(jnp.where(n == n_b, end, b0 + n), False))

        def apply_lent(k):
            pl.when(lends & (k >= 0) & (k < mine))(lambda: apply_b(k, True))

        def step(s):
            in_a = s < n_ax
            spare, k = place(s)
            in_r = jnp.logical_not(in_a) & spare
            in_b = (s >= n_ax) & (s < total) & jnp.logical_not(spare)
            ph = jnp.where(in_a, 0, 1)
            other = jnp.where(in_a, s == n_a, k == n_b)
            t = jnp.where(other, end, jnp.where(in_a, a0 + s, b0 + k))
            slot = jnp.where(other, tiles, t)
            lane = jnp.where(other, 1 - x, x)

            pl.when(s == jnp.where(r == 0, PER, lag_a))(take_head)
            pl.when(s == lag_a)(make_u0)

            @pl.when(in_b & ((k == 0) | (t == MID)))
            def _():
                allowed(X)

            pl.when(far & (s < total))(lambda: gate(s))
            pl.when(borrows & (s == n_ax + EARLY))(lambda: allowed(Y))
            ta = s - lag_a

            def micro(i):
                @pl.when((s < total) & jnp.logical_not(in_r))
                def _():
                    p, sem = row_of(t, lane, i), lane_at(s, i)
                    arrived(ph, p, sem)
                    pl.when(far)(lambda: fwd_copy(ph, p, sem).start())
                    pl.when(in_a | (t < end))(lambda: cross_copy(ph, p, unit_at(slot)).start())

                @pl.when(in_r)
                def _():
                    n = s - n_ax - EARLY
                    p, sem = spare_row(n, i), lane_at(s, i)
                    arrived(1, p, sem)
                    pl.when(far)(lambda: fwd_copy(1, p, sem).start())
                    cross_copy(1, p, unit_at(n)).start()
                    pl.when(i == SPLIT - 1)(lambda: give_copy(n).start())

                pl.when((i == 0) & (ta >= 0) & (ta < n_a))(lambda: lower_a(a0 + ta))
                pl.when((i == 1) & (ta >= 0) & (ta < n_a))(lambda: apply_a(a0 + ta))
                pl.when(i == SPLIT - 1)(lambda: apply_plain(s - lag_b))
                pl.when(i == 1)(lambda: apply_lent(s - use_lent))

            loop(0, SPLIT, micro)

            open_gate(s, total, Z, {"pcol": pcol - 2})
            pl.when((ta == MID - 1 - a0) | (ta == n_a - 1))(lambda: allow(X, {"pcol": pcol_x}))
            pl.when(lends & (ta == MID - 1 - a0))(lambda: allow(Y, {"prow": prow - 2}))

            @pl.when((prow == 1) & (s == first_of_1))
            def _():
                lower_times(1, own[pl.ds(0, width)], u1)

            pl.when((prow == 1) & (s == first_of_1 + 1))(pass_u1)
            @pl.when((prow == 0) & (s == first_of_1))
            def _():
                own[:width] = u0[...]

            @pl.when((prow == 1) & (s == first_of_1 + 1))
            def _():
                own[:width] = u1[...]

            @pl.when((r == 1) & (prow > 1) & (s == tiles - PER - 2))
            def _():
                arrived_u1()
                pass_u1()

            pl.when((r == 0) & (s == tiles - PER - 1))(arrived_u1)

            @pl.when(borrows & (s >= give_from) & (s < give_from + mine))
            def _():
                spare_unit_arrived(s - give_from)
                give_unit_copy(s - give_from).start()

        loop(0, total, step)
        loop(total - lag_b, total, apply_plain)

        @pl.when(r == 1)
        def _():
            u1_copy(0, {"prow": prow_x}).wait_send()
            pl.when(jnp.logical_not(bottom))(lambda: u1_copy(1, {"prow": prow_x}).wait_send())

    @pl.when(r == 0)
    def _():
        head_copy(0, {"prow": prow_x}).wait_send()
        pl.when(jnp.logical_not(bottom))(lambda: head_copy(1, {"prow": prow_x}).wait_send())

    pl.when(is_s1 & (prow == 0))(lambda: head_copy(2, {"pcol": pcol_x}).wait_send())
    for k, n in enumerate(moved):
        if n:
            pl.when(is_g & (prow == k))(functools.partial(sent, SIDE, 2 * n))
            pl.when(source & (prow == k + 2))(functools.partial(sent, SIDE, n))
    full = 2 * tiles
    base = [full - 2 * PER + moved[0], full - PER + moved[1], full - moved[0], full - moved[1], full]
    more, less = [n + 2 for n in base], [n - 2 for n in base]
    pl.when(far & (x == 0))(lambda: sent_by_prow(FWD, more))
    pl.when(far & (x == 1))(lambda: sent_by_prow(FWD, base))
    pl.when(is_g & (x == 0))(lambda: sent_by_prow(CROSS, base))
    pl.when(is_g & (x == 1))(lambda: sent_by_prow(CROSS, less))
    pl.when(is_s0)(lambda: sent_by_prow(CROSS, (full - 2 * PER, full)))
    pl.when(is_s1)(lambda: sent_by_prow(CROSS, (tiles - PER + 1, tiles + 1)))


def finish(own, buf, u1, out_ref, res, sem):
    pcol = lax.axis_index("pcol")
    rows, late = own.shape[0], res.shape[0]
    whole, done, rest = pl.ds(0, rows), pl.ds(0, rows - late), pl.ds(rows - late, late)
    for i in range(2):
        copy = pltpu.make_async_copy(buf.at[i, whole], out_ref, sem.at[0])
        pl.when(pcol == i)(copy.start)
        pl.when(pcol == i)(copy.wait)

    @pl.when(pcol >= 2)
    def _():
        bulk = pltpu.make_async_copy(own.at[done], out_ref.at[done], sem.at[0])
        made = pltpu.make_async_copy(res, out_ref.at[rest], sem.at[1])
        bulk.start()
        res[...] = (own[rest].astype(F32) - dot(buf[1, rest], u1[...])).astype(BF)
        made.start()
        bulk.wait()
        made.wait()


def body(n_prow, n_pcol, matrix, u_inverse, l_inverse):
    rows, width = matrix.shape
    tile, unit, pkt, tiles, moved = sizes(rows, width, n_prow)
    square = (width, width)
    dma = pltpu.SemaphoreType.DMA
    operands = [
        pltpu.with_memory_space_constraint(a, pltpu.HBM) for a in (matrix, u_inverse, l_inverse)
    ]
    lanes = (2, rows + PER * tile, width)
    pieces = pl.pallas_call(
        functools.partial(kernel, n_prow, n_pcol, width),
        out_shape=[jax.ShapeDtypeStruct(shape, BF) for shape in (matrix.shape, lanes, square)],
        in_specs=[pl.BlockSpec(memory_space=pltpu.HBM)] * 3,
        out_specs=[pl.BlockSpec(memory_space=pltpu.VMEM)] * 3,
        scratch_shapes=[
            pltpu.VMEM((tile, width), BF),
            pltpu.VMEM(square, BF),
            pltpu.VMEM((2,) + square, F32),
            pltpu.VMEM((2,) + square, F32),
            pltpu.VMEM((2, PIECES) + square, BF),
            pltpu.VMEM((2, PIECES) + square, BF),
            pltpu.VMEM(square, BF),
            dma((4,)),
            dma((SPLIT * RING,)),
            dma((tiles + 1,)),
            dma((PER,)),
            dma((3,)),
            dma((2,)),
            dma((5,)),
            pltpu.SemaphoreType.REGULAR((3,)),
        ],
        compiler_params=pltpu.CompilerParams(
            collective_id=0, has_side_effects=True, vmem_limit_bytes=40 * 1024 * 1024
        ),
    )(*operands)
    return pl.pallas_call(
        finish,
        out_shape=jax.ShapeDtypeStruct(matrix.shape, BF),
        in_specs=[pl.BlockSpec(memory_space=pltpu.VMEM)] * 3,
        out_specs=pl.BlockSpec(memory_space=pl.ANY),
        scratch_shapes=[pltpu.VMEM((TAIL * tile, width), BF), dma((2,))],
        compiler_params=pltpu.CompilerParams(vmem_limit_bytes=8 * 1024 * 1024),
    )(*pieces)


def solution(mesh):
    run = functools.partial(body, mesh.shape["prow"], mesh.shape["pcol"])
    in_specs = (P("prow", "pcol"), P(), P())
    out_specs = P("prow", "pcol")
    return jax.shard_map(run, mesh=mesh, in_specs=in_specs, out_specs=out_specs, check_vma=False)
```

```python
import functools

import jax
import jax.numpy as jnp
from jax import lax
from jax.experimental import pallas as pl
from jax.experimental.pallas import tpu as pltpu
from jax.sharding import PartitionSpec as P

MESH = pl.DeviceIdType.MESH
BF = jnp.bfloat16
F32 = jnp.float32
PIECES = 2
PER = 4
SPLIT = 4
EARLY = 8
MID = 16
RING, BLOCK = 14, 7
HEAD_AT = 20
TAIL = 4


def sizes(rows, width, n_prow):
    tile = width // PER
    moved = (PER, PER // 2) if n_prow > 2 else (0, 0)
    return tile, tile // 2, tile // 2 // SPLIT, rows // tile, moved


def dot(a, b):
    return jnp.dot(a, b, preferred_element_type=F32)


def times_upper(a, u_ref, panel):
    half = a.shape[1] // 2
    left = sum(dot(a[:, :half], u_ref[panel, i, :half, :half]) for i in reversed(range(PIECES)))
    right = sum(dot(a, u_ref[panel, i, :, half:]) for i in reversed(range(PIECES)))
    return jnp.concatenate([left, right], 1).astype(BF)


def kernel(
    n_prow, n_pcol, width, m_ref, u_hbm, l_hbm, own, buf, u1,
    low_now, head, uf, lf, us, ls, u0,
    load_sem, lane_sem, unit_sem, lend_sem, send_sem, hrecv, hsend, credit,
):
    rows = own.shape[0]
    tile, unit, pkt, tiles, moved = sizes(rows, width, n_prow)
    n_pkt = rows // pkt
    end = tiles - 1
    half = width // 2
    prow, pcol = lax.axis_index("prow"), lax.axis_index("pcol")
    x, r = pcol % 2, prow % 2
    pcol_x, prow_x = pcol + 1 - 2 * x, prow + 1 - 2 * r
    is_s0, is_s1, is_g = pcol == 0, pcol == 1, pcol >= 2
    source, last = pcol < 2, pcol + 2 >= n_pcol
    top, bottom = prow < 2, prow + 2 >= n_prow
    far = jnp.logical_not(last)
    mine = jnp.where(r == 0, moved[0], moved[1])
    lends, borrows = (prow >= 2) & (prow < 4) & (mine > 0), top & (mine > 0)

    a0 = jnp.where(prow == 0, PER, 0)
    n_a = tiles - a0
    n_r = jnp.where(borrows, mine, 0)
    b0 = jnp.where(top, PER, jnp.where(lends, mine, 0))
    n_b = tiles - b0
    n_ax = n_a + 1 - 2 * x
    total = n_ax + n_r + n_b + 1

    def at(ph, p):
        return buf.at[ph, pl.ds(pl.multiple_of(p * pkt, pkt), pkt)]

    def m_at(p):
        return m_ref.at[pl.ds(pl.multiple_of(p * pkt, pkt), pkt)]

    def unit_of(t, lane):
        return pl.ds(pl.multiple_of((2 * t + lane) * unit, unit), unit)

    def tile_of(t):
        return pl.ds(pl.multiple_of(t * tile, tile), tile)

    def remote(src, dst, sem, recv_sem, where):
        return pltpu.make_async_remote_copy(
            src_ref=src, dst_ref=dst, send_sem=sem, recv_sem=recv_sem,
            device_id=where, device_id_type=MESH,
        )

    FWD, CROSS, SIDE = (send_sem.at[i] for i in range(3))

    def lane_at(s, i):
        return lane_sem.at[SPLIT * (s % RING) + i]

    def unit_at(slot):
        return unit_sem.at[slot]

    def row_of(t, lane, i):
        return SPLIT * (2 * t + lane) + i

    def fwd_copy(ph, p, sem, src=None):
        ref = at(ph, p)
        return remote(ref if src is None else src, ref, FWD, sem, {"pcol": pcol + 2})

    def arrived(ph, p, sem):
        ref = at(ph, p)
        remote(ref, ref, FWD, sem, {"pcol": pcol_x}).wait_recv()

    def cross_copy(ph, p, sem):
        ref = at(ph, p)
        return remote(ref, ref, CROSS, sem, {"pcol": pcol_x})

    def unit_copy(t, lane, slot, dst, src=None):
        ref = dst.at[unit_of(t, lane)]
        return remote(ref if src is None else src, ref, CROSS, unit_at(slot), {"pcol": pcol_x})

    def spare_row(k, i):
        return n_pkt + row_of(k, x, i)

    def lend_copy(k):
        src, dst = buf.at[1, unit_of(k, x)], buf.at[1, unit_of(tiles + k, x)]
        return remote(src, dst, SIDE, lend_sem.at[k], {"prow": prow - 2})

    def give_copy(k):
        src, dst = buf.at[1, unit_of(tiles + k, x)], buf.at[1, unit_of(k, x)]
        return remote(src, dst, SIDE, lend_sem.at[k], {"prow": prow + 2})

    def give_unit_copy(k):
        src, dst = buf.at[1, unit_of(tiles + k, 1 - x)], buf.at[1, unit_of(k, 1 - x)]
        return remote(src, dst, SIDE, unit_at(k), {"prow": prow + 2})

    def spare_unit_arrived(k):
        ref = buf.at[1, unit_of(tiles + k, 1 - x)]
        remote(ref, ref, CROSS, unit_at(k), {"pcol": pcol_x}).wait_recv()

    Z, X, Y = (credit.at[i] for i in range(3))

    def allow(sem, where):
        pl.semaphore_signal(sem, inc=1, device_id=where, device_id_type=MESH)

    def allowed(sem):
        pl.semaphore_wait(sem, 1)

    def gate(s, sem=Z):
        pl.when((s >= RING) & (s % BLOCK == 0))(lambda: allowed(sem))

    def open_gate(s, steps, sem, where):
        pl.when((s % BLOCK == BLOCK - 1) & (s + BLOCK + 1 < steps))(lambda: allow(sem, where))

    def step_of(k):
        return n_ax + k + jnp.where(k >= EARLY, n_r, 0)

    def sent(sem, units):
        ref = buf.at[0, pl.ds(0, units * unit)]
        remote(ref, ref, sem, lane_at(0, 0), {"pcol": pcol_x}).wait_send()

    def sent_by_prow(sem, units):
        for k, n in enumerate(units):
            here = prow == k if k + 1 < len(units) else prow >= k
            pl.when(here)(functools.partial(sent, sem, n))

    def loop(lo, hi, step):
        def one(k, carry):
            step(k)
            return carry

        lax.fori_loop(lo, hi, one, 0)

    load_lane = pltpu.make_async_copy(m_ref, buf.at[0, pl.ds(0, rows)], load_sem.at[0])
    load_own = pltpu.make_async_copy(m_ref, own, load_sem.at[0])
    load_u = pltpu.make_async_copy(u_hbm, uf, load_sem.at[1])
    load_l = pltpu.make_async_copy(l_hbm, lf, load_sem.at[2])
    has_head = (prow == 0) & (pcol >= 1)
    load_head = pltpu.make_async_copy(m_ref.at[pl.ds(0, width)], head, load_sem.at[3])

    barrier = pltpu.get_barrier_semaphore()

    def greet(where):
        pl.semaphore_signal(barrier, inc=1, device_id=where, device_id_type=MESH)

    greet({"pcol": pcol_x})
    greet({"prow": prow_x})
    for ok, where in (
        (jnp.logical_not(source), {"pcol": pcol - 2}),
        (far, {"pcol": pcol + 2}),
        (jnp.logical_not(top), {"prow": prow - 2}),
        (jnp.logical_not(bottom), {"prow": prow + 2}),
    ):
        pl.when(ok)(functools.partial(greet, where))
    pl.when(has_head)(load_head.start)
    load_u.start()
    load_l.start()
    pl.when(is_s0)(load_lane.start)
    pl.when(jnp.logical_not(is_s0))(load_own.start)
    absent = [jnp.where(ok, 1, 0) for ok in (source, last, top, bottom)]
    pl.semaphore_wait(barrier, 6 - sum(absent))

    def head_copy(i, where, src=head):
        return remote(src, head, hsend.at[i], hrecv.at[0], where)

    def pass_head(src=head):
        head_copy(0, {"prow": prow + 1}, src).start()
        pl.when(jnp.logical_not(bottom))(lambda: head_copy(1, {"prow": prow + 2}, src).start())

    @pl.when(has_head)
    def _():
        first = m_ref.at[pl.ds(0, width)]
        pl.when(is_s1)(lambda: head_copy(2, {"pcol": pcol_x}, first).start())
        pass_head(first)

    def push(s):
        pl.when(far)(lambda: gate(s))
        gate(s, X)
        t, lane = jnp.where(s < n_a, a0 + s, end), jnp.where(s < n_a, 0, 1)
        for i in range(SPLIT):
            p, c = row_of(t, lane, i), row_of(t, 1 - lane, i)
            remote(m_at(c), at(0, c), CROSS, lane_at(s, i), {"pcol": pcol_x}).start()
            pl.when(far)(lambda: fwd_copy(0, p, lane_at(s, i), m_at(p)).start())

    @pl.when(is_s0)
    def _():
        loop(0, RING, push)

    @pl.when(is_s1)
    def _():
        def send(t, lane, slot):
            unit_copy(t, lane, slot, own, m_ref.at[unit_of(t, lane)]).start()

        loop(a0, tiles, lambda t: send(t, 0, t))
        send(end, 1, tiles)

    def split(src, dst, panel):
        rest = src[panel]
        for i in range(PIECES):
            piece = rest.astype(BF)
            dst[panel, i] = piece
            rest = rest - piece.astype(F32)

    load_u.wait()
    load_l.wait()
    split(lf, ls, 0)
    split(uf, us, 0)
    pl.when(source)(lambda: split(uf, us, 1))
    pl.when(is_g & (prow == 1))(lambda: split(lf, ls, 1))
    pl.when(is_s0)(load_lane.wait)
    pl.when(jnp.logical_not(is_s0))(load_own.wait)

    def lower_times(panel, value, out):
        upper = sum(dot(ls[panel, i, :half, :half], value[:half]) for i in reversed(range(PIECES)))
        out[:half] = upper.astype(BF)
        lower = sum(dot(ls[panel, i, half:], value) for i in reversed(range(PIECES)))
        out[half:] = lower.astype(BF)

    def take_head():
        pl.when(has_head)(load_head.wait)

        @pl.when(jnp.logical_not(has_head))
        def _():
            head_copy(0, {"prow": prow_x}).wait_recv()
            pl.when(r == 0)(pass_head)

    def make_u0():
        lower_times(0, head[...], u0)

    def make_lower(t, low, lane):
        here = unit_of(t, lane)
        cur = (own[here].astype(F32) - dot(low, u0[...])).astype(BF)
        value = times_upper(cur, us, 1)
        buf[1, here] = jnp.where((prow == 1) & (t < PER), cur, value)

    def lend(t):
        pl.when(lends & (t >= 0) & (t < mine))(lambda: lend_copy(t).start())

    def borrow():
        @pl.when(borrows)
        def _():
            def one(k):
                s = n_ax + EARLY + k
                pl.when(far)(lambda: gate(s))
                lend_copy(k).wait_recv()
                for i in range(SPLIT):
                    pl.when(far)(lambda: fwd_copy(1, spare_row(k, i), lane_at(s, i)).start())

            loop(0, mine, one)

    def send_lower(t, lane, s):
        @pl.when(far)
        def _():
            gate(s)
            for i in range(SPLIT):
                fwd_copy(1, row_of(t, lane, i), lane_at(s, i)).start()

    @pl.when(is_s0)
    def _():
        def low_step(i):
            t = a0 + i
            here = tile_of(t)
            buf[0, here] = times_upper(buf[0, here], us, 0)
            pl.when(i == n_a - 2)(lambda: loop(RING, RING + BLOCK, push))
            pl.when(i == jnp.where(prow == 0, HEAD_AT, n_a - 1))(take_head)

        loop(0, n_a, low_step)
        make_u0()

        def make(t, lane, slot):
            unit_copy(t, lane, slot, own).wait_recv()
            make_lower(t, buf[0, unit_of(t, lane)], lane)

        first = PER + 1

        def show(t):
            unit_copy(t, 0, t, buf.at[1]).start()

        def send(k):
            pl.when(k == EARLY)(borrow)
            send_lower(b0 + k, 0, step_of(k))

        def step(i):
            t = a0 + i
            make(t, 0, t)
            lend(t - 1)
            pl.when(i >= PER)(lambda: show(t - PER))

            @pl.when(i < PER)
            def _():
                for n in range(2):
                    k = RING + BLOCK + 2 * i + n
                    pl.when(k <= n_a)(lambda: push(k))

            pl.when(i >= first)(lambda: send(i - first))

        loop(0, n_a, step)
        make(end, 1, tiles)
        loop(n_a - first, n_b, send)
        loop(tiles - PER, end, show)
        send_lower(end, 1, total - 1)

    @pl.when(is_s1)
    def _():
        lag = 8

        def relay(s, i):
            p, sem = row_of(a0 + s, 1, i), lane_at(s, i)
            arrived(0, p, sem)
            pl.when(far)(lambda: fwd_copy(0, p, sem).start())

        def make_part(t, i):
            here, low, cur = unit_of(t, 1), slice(0, unit), slice(unit, tile)
            if i == 0:
                low_now[low] = times_upper(buf[0, here], us, 0)
            elif i == 1:
                low_now[cur] = (own[here].astype(F32) - dot(low_now[low], u0[...])).astype(BF)
            elif i == 2:
                value = times_upper(low_now[cur], us, 1)
                buf[1, here] = jnp.where((prow == 1) & (t < PER), low_now[cur], value)
            else:
                lend(t - 1)

        def make(t, lane=1):
            make_lower(t, times_upper(buf[0, unit_of(t, lane)], us, 0), lane)
            lend(t - 1)

        def step(s):
            pl.when(s == jnp.where(r == 0, PER, lag))(take_head)
            pl.when(s == lag)(make_u0)
            pl.when(far)(lambda: gate(s))
            for i in range(SPLIT):
                relay(s, i)
                pl.when(s >= lag)(functools.partial(make_part, a0 + s - lag, i))
            open_gate(s, n_a + 1, X, {"pcol": pcol_x})

        loop(0, n_a - 1, step)

        @pl.when(prow == 0)
        def _():
            buf[1, :width] = u0[...]

        def late(i):
            pl.when(i == EARLY)(borrow)
            send_lower(b0 + i, 1, step_of(i))

            @pl.when(i <= lag + 1)
            def _():
                lane = jnp.where(i <= lag, 1, 0)

                @pl.when(i >= lag)
                def _():
                    for n in range(SPLIT):
                        arrived(0, row_of(end, lane, n), lane_at(n_a - lane, n))

                make(jnp.minimum(end - lag + i, end), lane)

        loop(0, n_b, late)
        send_lower(end, 0, total - 1)

        def finish(t):
            unit_copy(t, 0, t, buf.at[1]).wait_recv()

        loop(a0, end, finish)

    @pl.when(is_g)
    def _():
        lag_a, lag_b = 6, 4
        give_from = n_ax + EARLY + 3
        use_lent = tiles - PER + EARLY + jnp.where(r == 0, 9, 14)
        first_of_1 = lag_a + PER

        def u1_copy(i, where):
            return remote(u1, u1, hsend.at[3 + i], hrecv.at[1], where)

        def pass_u1():
            u1_copy(0, {"prow": prow - 1}).start()
            pl.when(jnp.logical_not(bottom))(lambda: u1_copy(1, {"prow": prow + 2}).start())

        def arrived_u1():
            u1_copy(0, {"prow": prow_x}).wait_recv()

        tail = tiles - TAIL

        def lower_a(t):
            pl.when((t < end) | (x == 1))(lambda: unit_copy(t, 1 - x, t, buf.at[0]).wait_recv())
            pl.when((t == end) & (x == 1))(lambda: unit_copy(t, x, tiles, buf.at[0]).wait_recv())
            low_now[...] = times_upper(buf[0, tile_of(t)], us, 0)

        def apply_a(t):
            here = tile_of(t)
            own[here] = (own[here].astype(F32) - dot(low_now[...], u0[...])).astype(BF)

        def apply_b(t, was_lent):
            if was_lent:
                give_copy(t).wait_recv()

            pl.when(t < end)(lambda: unit_copy(t, 1 - x, t, buf.at[1]).wait_recv())
            here = tile_of(t)

            @pl.when(t < tail)
            def _():
                own[here] = (own[here].astype(F32) - dot(buf[1, here], u1[...])).astype(BF)

        def place(s):
            q = s - n_ax
            return (q >= EARLY) & (q < EARLY + n_r), q - jnp.where(q >= EARLY + n_r, n_r, 0)

        def apply_plain(u):
            u_spare, n = place(u)
            plain = (u >= n_ax) & jnp.logical_not(u_spare) & (n != n_b - 1)
            pl.when(plain)(lambda: apply_b(jnp.where(n == n_b, end, b0 + n), False))

        def apply_lent(k):
            pl.when(lends & (k >= 0) & (k < mine))(lambda: apply_b(k, True))

        def step(s):
            in_a = s < n_ax
            spare, k = place(s)
            in_r = jnp.logical_not(in_a) & spare
            in_b = (s >= n_ax) & (s < total) & jnp.logical_not(spare)
            ph = jnp.where(in_a, 0, 1)
            other = jnp.where(in_a, s == n_a, k == n_b)
            t = jnp.where(other, end, jnp.where(in_a, a0 + s, b0 + k))
            slot = jnp.where(other, tiles, t)
            lane = jnp.where(other, 1 - x, x)

            pl.when(s == jnp.where(r == 0, PER, lag_a))(take_head)
            pl.when(s == lag_a)(make_u0)

            @pl.when(in_b & ((k == 0) | (t == MID)))
            def _():
                allowed(X)

            pl.when(far & (s < total))(lambda: gate(s))
            pl.when(borrows & (s == n_ax + EARLY))(lambda: allowed(Y))
            ta = s - lag_a

            def micro(i):
                @pl.when((s < total) & jnp.logical_not(in_r))
                def _():
                    p, sem = row_of(t, lane, i), lane_at(s, i)
                    arrived(ph, p, sem)
                    pl.when(far)(lambda: fwd_copy(ph, p, sem).start())
                    pl.when(in_a | (t < end))(lambda: cross_copy(ph, p, unit_at(slot)).start())

                @pl.when(in_r)
                def _():
                    n = s - n_ax - EARLY
                    p, sem = spare_row(n, i), lane_at(s, i)
                    arrived(1, p, sem)
                    pl.when(far)(lambda: fwd_copy(1, p, sem).start())
                    cross_copy(1, p, unit_at(n)).start()
                    pl.when(i == SPLIT - 1)(lambda: give_copy(n).start())

                pl.when((i == 0) & (ta >= 0) & (ta < n_a))(lambda: lower_a(a0 + ta))
                pl.when((i == 1) & (ta >= 0) & (ta < n_a))(lambda: apply_a(a0 + ta))
                pl.when(i == SPLIT - 1)(lambda: apply_plain(s - lag_b))
                pl.when(i == 1)(lambda: apply_lent(s - use_lent))

            loop(0, SPLIT, micro)

            open_gate(s, total, Z, {"pcol": pcol - 2})
            pl.when((ta == MID - 1 - a0) | (ta == n_a - 1))(lambda: allow(X, {"pcol": pcol_x}))
            pl.when(lends & (ta == MID - 1 - a0))(lambda: allow(Y, {"prow": prow - 2}))

            @pl.when((prow == 1) & (s == first_of_1))
            def _():
                lower_times(1, own[pl.ds(0, width)], u1)

            pl.when((prow == 1) & (s == first_of_1 + 1))(pass_u1)
            @pl.when((prow == 0) & (s == first_of_1))
            def _():
                own[:width] = u0[...]

            @pl.when((prow == 1) & (s == first_of_1 + 1))
            def _():
                own[:width] = u1[...]

            @pl.when((r == 1) & (prow > 1) & (s == tiles - PER - 2))
            def _():
                arrived_u1()
                pass_u1()

            pl.when((r == 0) & (s == tiles - PER - 1))(arrived_u1)

            @pl.when(borrows & (s >= give_from) & (s < give_from + mine))
            def _():
                spare_unit_arrived(s - give_from)
                give_unit_copy(s - give_from).start()

        loop(0, total, step)
        loop(total - lag_b, total, apply_plain)

        @pl.when(r == 1)
        def _():
            u1_copy(0, {"prow": prow_x}).wait_send()
            pl.when(jnp.logical_not(bottom))(lambda: u1_copy(1, {"prow": prow_x}).wait_send())

    @pl.when(r == 0)
    def _():
        head_copy(0, {"prow": prow_x}).wait_send()
        pl.when(jnp.logical_not(bottom))(lambda: head_copy(1, {"prow": prow_x}).wait_send())

    pl.when(is_s1 & (prow == 0))(lambda: head_copy(2, {"pcol": pcol_x}).wait_send())
    for k, n in enumerate(moved):
        if n:
            pl.when(is_g & (prow == k))(functools.partial(sent, SIDE, 2 * n))
            pl.when(source & (prow == k + 2))(functools.partial(sent, SIDE, n))
    full = 2 * tiles
    base = [full - 2 * PER + moved[0], full - PER + moved[1], full - moved[0], full - moved[1], full]
    more, less = [n + 2 for n in base], [n - 2 for n in base]
    pl.when(far & (x == 0))(lambda: sent_by_prow(FWD, more))
    pl.when(far & (x == 1))(lambda: sent_by_prow(FWD, base))
    pl.when(is_g & (x == 0))(lambda: sent_by_prow(CROSS, base))
    pl.when(is_g & (x == 1))(lambda: sent_by_prow(CROSS, less))
    pl.when(is_s0)(lambda: sent_by_prow(CROSS, (full - 2 * PER, full)))
    pl.when(is_s1)(lambda: sent_by_prow(CROSS, (tiles - PER + 1, tiles + 1)))


def finish(own, buf, u1, out_ref, res, sem):
    pcol = lax.axis_index("pcol")
    rows, late = own.shape[0], res.shape[0]
    whole, done, rest = pl.ds(0, rows), pl.ds(0, rows - late), pl.ds(rows - late, late)
    for i in range(2):
        copy = pltpu.make_async_copy(buf.at[i, whole], out_ref, sem.at[0])
        pl.when(pcol == i)(copy.start)
        pl.when(pcol == i)(copy.wait)

    @pl.when(pcol >= 2)
    def _():
        bulk = pltpu.make_async_copy(own.at[done], out_ref.at[done], sem.at[0])
        made = pltpu.make_async_copy(res, out_ref.at[rest], sem.at[1])
        bulk.start()
        res[...] = (own[rest].astype(F32) - dot(buf[1, rest], u1[...])).astype(BF)
        made.start()
        bulk.wait()
        made.wait()


def body(n_prow, n_pcol, matrix, u_inverse, l_inverse):
    rows, width = matrix.shape
    tile, unit, pkt, tiles, moved = sizes(rows, width, n_prow)
    square = (width, width)
    dma = pltpu.SemaphoreType.DMA
    operands = [
        pltpu.with_memory_space_constraint(a, pltpu.HBM) for a in (matrix, u_inverse, l_inverse)
    ]
    lanes = (2, rows + PER * tile, width)
    pieces = pl.pallas_call(
        functools.partial(kernel, n_prow, n_pcol, width),
        out_shape=[jax.ShapeDtypeStruct(shape, BF) for shape in (matrix.shape, lanes, square)],
        in_specs=[pl.BlockSpec(memory_space=pltpu.HBM)] * 3,
        out_specs=[pl.BlockSpec(memory_space=pltpu.VMEM)] * 3,
        scratch_shapes=[
            pltpu.VMEM((tile, width), BF),
            pltpu.VMEM(square, BF),
            pltpu.VMEM((2,) + square, F32),
            pltpu.VMEM((2,) + square, F32),
            pltpu.VMEM((2, PIECES) + square, BF),
            pltpu.VMEM((2, PIECES) + square, BF),
            pltpu.VMEM(square, BF),
            dma((4,)),
            dma((SPLIT * RING,)),
            dma((tiles + 1,)),
            dma((PER,)),
            dma((3,)),
            dma((2,)),
            dma((5,)),
            pltpu.SemaphoreType.REGULAR((3,)),
        ],
        compiler_params=pltpu.CompilerParams(
            collective_id=0, has_side_effects=True, vmem_limit_bytes=40 * 1024 * 1024
        ),
    )(*operands)
    return pl.pallas_call(
        finish,
        out_shape=jax.ShapeDtypeStruct(matrix.shape, BF),
        in_specs=[pl.BlockSpec(memory_space=pltpu.VMEM)] * 3,
        out_specs=pl.BlockSpec(memory_space=pl.ANY),
        scratch_shapes=[pltpu.VMEM((TAIL * tile, width), BF), dma((2,))],
        compiler_params=pltpu.CompilerParams(vmem_limit_bytes=8 * 1024 * 1024),
    )(*pieces)


def solution(mesh):
    run = functools.partial(body, mesh.shape["prow"], mesh.shape["pcol"])
    in_specs = (P("prow", "pcol"), P(), P())
    out_specs = P("prow", "pcol")
    return jax.shard_map(run, mesh=mesh, in_specs=in_specs, out_specs=out_specs, check_vma=False)
```
